32 devices in a mesh: dp: 8 (over z, core), fsdp: 4 (over y, x).
Axes of the slice: x: 2, y: 2, z: 4, core: 2. Of those that a mesh axis runs over, the one named last changes fastest.
Arguments:
- pixels: bfloat16 [32768, 768], P(('dp', 'fsdp')), may hold values from -6 to 6
- valid_mask: int32 [32768, 768], P(('dp', 'fsdp')), may hold values from 0 to 1
- size_groups: int32 [32], P(('dp', 'fsdp')), may hold values from 0 to 2
- code_index: int32 [4, 8192], P(None, ('dp', 'fsdp')), may hold values from 0 to 16383, as said below
- w_pixel: float32 [2, 768, 512], P(None, 'fsdp', 'dp'), may hold values from -0.625 to 0.625
- w_res: float32 [4, 4608, 512], P(None, 'fsdp', 'dp'), may hold values from -0.1875 to 0.1875
- w_scale: float32 [2, 2048, 512], P(None, 'fsdp', 'dp'), may hold values from -0.5 to 0.5
- w_latent: float32 [2, 512, 256], P(None, 'fsdp', 'dp'), may hold values from -0.75 to 0.75
- norm_gains: float32 [8, 512], replicated, may hold values from -0.9 to 1.5
- moment_pixel: float32 [2, 768, 512], P(None, 'fsdp', 'dp'), may hold values from -4.4703484e-08 to 4.4703484e-08
- moment_res: float32 [4, 4608, 512], P(None, 'fsdp', 'dp'), may hold values from -4.4703484e-08 to 4.4703484e-08
- moment_scale: float32 [2, 2048, 512], P(None, 'fsdp', 'dp'), may hold values from -4.4703484e-08 to 4.4703484e-08
- moment_latent: float32 [2, 512, 256], P(None, 'fsdp', 'dp'), may hold values from -4.4703484e-08 to 4.4703484e-08
- moment_gains: float32 [8, 512], replicated, may hold values from -1.4901161e-07 to 1.4901161e-07
- second_pixel: float32 [2, 768, 512], P(None, 'fsdp', 'dp'), may hold values from 7.84e-18 to 3.136e-17
- second_res: float32 [4, 4608, 512], P(None, 'fsdp', 'dp'), may hold values from 7.84e-18 to 3.136e-17
- second_scale: float32 [2, 2048, 512], P(None, 'fsdp', 'dp'), may hold values from 7.84e-18 to 3.136e-17
- second_latent: float32 [2, 512, 256], P(None, 'fsdp', 'dp'), may hold values from 7.84e-18 to 3.136e-17
- second_gains: float32 [8, 512], replicated, may hold values from 1e-16 to 4e-16
- ema_counts: float32 [16384], P(('dp', 'fsdp')), may hold values from 0.5 to 4
- ema_sums: float32 [16384, 256], P(('dp', 'fsdp')), may hold values from -6 to 6
Outputs:
- loss_parts: float32 [3], replicated
- grad_norm: float32 [1], replicated
- next_pixel: float32 [2, 768, 512], P(None, 'fsdp', 'dp')
- next_moment_pixel: float32 [2, 768, 512], P(None, 'fsdp', 'dp')
- next_second_pixel: float32 [2, 768, 512], P(None, 'fsdp', 'dp')
- copy_pixel: bfloat16 [2, 768, 512], P(None, 'fsdp', 'dp')
- next_res: float32 [4, 4608, 512], P(None, 'fsdp', 'dp')
- next_moment_res: float32 [4, 4608, 512], P(None, 'fsdp', 'dp')
- next_second_res: float32 [4, 4608, 512], P(None, 'fsdp', 'dp')
- copy_res: bfloat16 [4, 4608, 512], P(None, 'fsdp', 'dp')
- next_scale: float32 [2, 2048, 512], P(None, 'fsdp', 'dp')
- next_moment_scale: float32 [2, 2048, 512], P(None, 'fsdp', 'dp')
- next_second_scale: float32 [2, 2048, 512], P(None, 'fsdp', 'dp')
- copy_scale: bfloat16 [2, 2048, 512], P(None, 'fsdp', 'dp')
- next_latent: float32 [2, 512, 256], P(None, 'fsdp', 'dp')
- next_moment_latent: float32 [2, 512, 256], P(None, 'fsdp', 'dp')
- next_second_latent: float32 [2, 512, 256], P(None, 'fsdp', 'dp')
- copy_latent: bfloat16 [2, 512, 256], P(None, 'fsdp', 'dp')
- next_gains: float32 [8, 512], replicated
- next_moment_gains: float32 [8, 512], replicated
- next_second_gains: float32 [8, 512], replicated
- next_counts: float32 [16384], P(('dp', 'fsdp'))
- next_sums: float32 [16384, 256], P(('dp', 'fsdp'))
- codebook: float32 [16384, 256], P(('dp', 'fsdp'))
- codebook_copy: bfloat16 [16384, 256], P(('dp', 'fsdp'))
The draws below stay inside these ranges and needn't reach their ends.
Inputs may be any that keep to these rules, and one draw needn't show every extreme that they name: `code_index`: among the 4 x 256 codes of one device's positions, at most 64 lie in any one device's block of 16384 / 32 consecutive codes, and on every device some block holds exactly 64 of them.
All inputs are finite; a program needn't handle non-finite values.
Results may differ from the reference program's by a relative error of at most 0.0061.
Values may be sent and summed in bfloat16 or wider, within the bound.
No kernel may reach another device: no remote copies, remote signals or barrier semaphores. Data moves between devices by JAX's collectives and lax.ppermute only.
A program may use at most 256 MiB of HBM per device.

```python
import math
import jax
import jax.numpy as jnp
from jax import lax

C = 512
ZD = 256
K = 16384
GROUPS = 32
PATCH_DIM = 768
SIDE = 32
DEPTH = 4
STEP = 5
ROWS_DEV = 1024
LAT_DEV = 256
TOKENS = 32768
LATENT = 8192
CANVASES = 32
CAP = 64
N_DP = 8
N_FSDP = 4


def draw_valid_mask(key, part):
    row = jnp.arange(TOKENS, dtype=jnp.int32)
    device = row // ROWS_DEV
    outer_span = max(N_DP - 1, 1)
    inner_span = max(N_FSDP - 1, 1)
    outer = device // N_FSDP
    inner = device % N_FSDP
    limit = 90 * (outer_span + 2 * outer) * (inner_span + 2 * inner) // (outer_span * inner_span)
    level = jax.random.randint(key, (TOKENS, PATCH_DIM), 0, 1000, dtype=jnp.int32)
    return (level < limit[:, None]).astype(jnp.int32)


def draw_norm_gains(key, part):
    first, second = jax.random.split(key)
    scales = jax.random.uniform(first, (4, C), jnp.float32, 0.5, 1.5)
    shifts = 0.3 * jnp.clip(jax.random.normal(second, (4, C), jnp.float32), -3.0, 3.0)
    return jnp.concatenate([scales, shifts], axis=0)


def draw_code_index(key, part):
    devices = N_DP * N_FSDP
    slots = devices * CAP
    pairs = DEPTH * LAT_DEV
    rows_own = K // devices

    def one_device(device_key):
        key_heavy, key_score, key_order, key_rows = jax.random.split(device_key, 4)
        heavy = jax.random.randint(key_heavy, (), 0, devices, dtype=jnp.int32)
        slot = jnp.arange(slots, dtype=jnp.int32)
        boost = jnp.where(slot // CAP == heavy, 1 << 23, 0).astype(jnp.int32)
        score = jax.random.randint(key_score, (slots,), 0, 1024, dtype=jnp.int32) * 8192 + slot + boost
        _, picked = lax.top_k(score, pairs)
        picked = picked.astype(jnp.int32)[jax.random.permutation(key_order, pairs)]
        rows = jax.random.randint(key_rows, (pairs,), 0, rows_own, dtype=jnp.int32)
        return (picked // CAP * rows_own + rows).astype(jnp.int32).reshape(DEPTH, LAT_DEV)
    codes = jax.vmap(one_device)(jax.random.split(jax.random.fold_in(key, 7), devices))
    return codes.transpose(1, 0, 2).reshape(DEPTH, LATENT)


def touch_ends(result, stream_key, low, high):
    longest = result.shape.index(max(result.shape))
    spots = []
    for shift in (0, 1):
        where = [jax.random.randint(jax.random.fold_in(stream_key, axis), (), 0, length) for axis, length in enumerate(result.shape)]
        where[longest] = (where[longest] + shift) % result.shape[longest]
        spots.append(tuple(where))
    return result.at[spots[0]].set(low).at[spots[1]].set(high)


def level_of(key, extent, shards, low, high):
    def one(axis_at, blocks):
        heights = jax.random.uniform(jax.random.fold_in(jax.random.fold_in(key, 6), axis_at), (blocks,), jnp.float32, low / len(shards), high / len(shards))
        return jnp.repeat(jnp.exp(heights), extent[axis_at] // blocks).reshape((-1,) + (1,) * (len(extent) - axis_at - 1))

    level = one(*shards[0])
    for cut in shards[1:]:
        level = level * one(*cut)
    return level


def bell_draw(rng, extent, scale, most, cuts=(), kind=jnp.bfloat16):
    entries = scale * jax.random.normal(rng, extent, jnp.float32)
    if cuts:
        entries = entries * level_of(rng, extent, cuts, -0.22, 0.18)
    return jnp.clip(entries, -most, most).astype(kind)


def setup_inputs(seed: int = 0) -> dict:
    keys = jax.random.split(jax.random.key(seed), 22)
    return {
        "pixels": bell_draw(keys[0], (TOKENS, PATCH_DIM), 1.0, 6.0, ((0, 32),)),
        "valid_mask": draw_valid_mask(jax.random.fold_in(keys[21], 71), 0),
        "size_groups": touch_ends(jax.random.randint(keys[2], (CANVASES,), 0, 3), jax.random.fold_in(keys[2], 1), 0, 2).astype(jnp.int32),
        "code_index": draw_code_index(jax.random.fold_in(keys[21], 71), 0),
        "w_pixel": bell_draw(keys[4], (2, PATCH_DIM, C), ((PATCH_DIM * C) ** -0.25), 0.625, ((1, 4), (2, 8)), jnp.float32),
        "w_res": bell_draw(keys[5], (4, 9 * C, C), (9 * C // 4) ** -0.5, 0.1875, ((1, 4), (2, 8)), jnp.float32),
        "w_scale": bell_draw(keys[6], (2, 4 * C, C), ((4 * C * C) ** -0.25), 0.5, ((1, 4), (2, 8)), jnp.float32),
        "w_latent": bell_draw(keys[7], (2, C, ZD), ((C * ZD) ** -0.25), 0.75, ((1, 4), (2, 8)), jnp.float32),
        "norm_gains": draw_norm_gains(jax.random.fold_in(keys[21], 71), 0),
        "moment_pixel": bell_draw(keys[9], (2, PATCH_DIM, C), 0.0000000028, 4.470348358154297e-08, ((1, 4), (2, 8)), jnp.float32),
        "moment_res": bell_draw(keys[10], (4, 9 * C, C), 0.0000000028, 4.470348358154297e-08, ((1, 4), (2, 8)), jnp.float32),
        "moment_scale": bell_draw(keys[11], (2, 4 * C, C), 0.0000000028, 4.470348358154297e-08, ((1, 4), (2, 8)), jnp.float32),
        "moment_latent": bell_draw(keys[12], (2, C, ZD), 0.0000000028, 4.470348358154297e-08, ((1, 4), (2, 8)), jnp.float32),
        "moment_gains": bell_draw(keys[13], (8, C), 0.00000001, 1.4901161193847656e-07, (), jnp.float32),
        "second_pixel": jnp.clip(jnp.exp(math.log(3.135999859121648e-17) - 1.3862944 * jax.random.uniform(keys[14], (2, PATCH_DIM, C), jnp.float32) ** level_of(keys[14], (2, PATCH_DIM, C), ((1, 4), (2, 8)), -0.2, 0.2)), 7.83999964780412e-18, 3.135999859121648e-17),
        "second_res": jnp.clip(jnp.exp(math.log(3.135999859121648e-17) - 1.3862944 * jax.random.uniform(keys[15], (4, 9 * C, C), jnp.float32) ** level_of(keys[15], (4, 9 * C, C), ((1, 4), (2, 8)), -0.2, 0.2)), 7.83999964780412e-18, 3.135999859121648e-17),
        "second_scale": jnp.clip(jnp.exp(math.log(3.135999859121648e-17) - 1.3862944 * jax.random.uniform(keys[16], (2, 4 * C, C), jnp.float32) ** level_of(keys[16], (2, 4 * C, C), ((1, 4), (2, 8)), -0.2, 0.2)), 7.83999964780412e-18, 3.135999859121648e-17),
        "second_latent": jnp.clip(jnp.exp(math.log(3.135999859121648e-17) - 1.3862944 * jax.random.uniform(keys[17], (2, C, ZD), jnp.float32) ** level_of(keys[17], (2, C, ZD), ((1, 4), (2, 8)), -0.2, 0.2)), 7.83999964780412e-18, 3.135999859121648e-17),
        "second_gains": jnp.clip(jnp.exp(jax.random.uniform(keys[18], (8, C), jnp.float32, math.log(1.0000000168623835e-16), math.log(4.000000067449534e-16))), 1.0000000168623835e-16, 4.000000067449534e-16),
        "ema_counts": jnp.clip(jnp.exp(math.log(4.0) - 2.0794415 * jax.random.uniform(keys[19], (K,), jnp.float32) ** level_of(keys[19], (K,), ((0, 32),), -0.2, 0.2)), 0.5, 4.0),
        "ema_sums": bell_draw(keys[20], (K, ZD), 1.0, 6.0, ((0, 32),), jnp.float32),
    }


HIGH = lax.Precision.HIGHEST
TAPS = [(dy, dx) for dy in (-1, 0, 1) for dx in (-1, 0, 1)]
COMMIT_WEIGHT = 0.25
CLIP_AT = 1e-05
EMA_DECAY = 0.8
WEIGHT_RATE = 0.03
GAIN_RATE = 0.4

@jax.custom_vjp
def low(v):
    return lax.optimization_barrier(v.astype(jnp.bfloat16)).astype(jnp.float32)

@jax.custom_vjp
def low_back(v):
    return v

def low_keep(v):
    return (low(v), None)

def low_pass(kept, grad):
    return (grad,)

def back_keep(v):
    return (v, None)

def back_low(kept, grad):
    return (low(grad),)
low.defvjp(low_keep, low_pass)
low_back.defvjp(back_keep, back_low)

def product(left, right):
    return jnp.dot(left, right, precision=HIGH, preferred_element_type=jnp.float32)

def geometry(groups, size, width):
    span = jnp.left_shift(jnp.ones_like(groups), groups)
    sides = size // 4 * span
    tile = jnp.arange(16, dtype=jnp.int32)[None, :]
    image = tile // 4 // span[:, None] * (4 // span[:, None]) + tile % 4 // span[:, None]
    member = (image[:, :, None] == jnp.arange(16, dtype=jnp.int32)[None, None, :]).astype(jnp.float32)
    count = (sides * sides).astype(jnp.float32) * (width // GROUPS)
    return (sides, member, count)

def image_means(field, member, count):
    batch, size, _, width = field.shape
    tile = size // 4
    sums = lax.optimization_barrier(jnp.sum(field.reshape(batch, 4, tile, 4, tile, width), axis=(2, 4))).reshape(batch, 16, width)
    per_image = jnp.einsum('btm,btc->bmc', member, sums, precision=HIGH)
    grouped = lax.optimization_barrier(jnp.sum(per_image.reshape(batch, 16, GROUPS, width // GROUPS), axis=3)) / count[:, None, None]
    spread = jnp.einsum('btm,bmg->btg', member, grouped, precision=HIGH)
    full = jnp.repeat(spread, width // GROUPS, axis=2).reshape(batch, 4, 1, 4, 1, width)
    return jnp.broadcast_to(full, (batch, 4, tile, 4, tile, width)).reshape(batch, size, size, width)

def gn_silu(field, gamma, beta, geom):
    mean = image_means(field, geom[1], geom[2])
    centered = field - mean
    var = image_means(centered * centered, geom[1], geom[2])
    return jax.nn.silu(centered * lax.rsqrt(var + 1e-05) * gamma + beta)

def side_masks(sides, size, delta):
    pos = jnp.arange(size, dtype=jnp.int32)
    near = pos + delta
    inside = (near >= 0) & (near < size)
    same = near[None, :] // sides[:, None] == pos[None, :] // sides[:, None]
    return (inside[None, :] & same).astype(jnp.float32)

def shifted(act, sides, dy, dx):
    size = act.shape[1]
    padded = jnp.pad(act, ((0, 0), (1, 1), (1, 1), (0, 0)))
    part = padded[:, 1 + dy:1 + dy + size, 1 + dx:1 + dx + size, :]
    keep = side_masks(sides, size, dy)[:, :, None] * side_masks(sides, size, dx)[:, None, :]
    return part * keep[..., None].astype(act.dtype)

def conv(act, weight, geom):
    width = act.shape[3]
    taps = weight.reshape(9, width, width)
    total = jnp.zeros((act.shape[0] * act.shape[1] * act.shape[2], width), jnp.float32)
    for index, (dy, dx) in enumerate(TAPS):
        total = total + product(shifted(act, geom[0], dy, dx).reshape(-1, width), taps[index])
    return total.reshape(act.shape)

def block(field, w_one, w_two, gains, first, geom):
    a_one = low(gn_silu(field, gains[first], gains[4 + first], geom))
    t_one = low_back(conv(a_one, w_one, geom))
    a_two = low(gn_silu(t_one, gains[first + 1], gains[5 + first], geom))
    t_two = low_back(conv(a_two, w_two, geom))
    return field + t_two

def to_depth(field):
    batch, size, _, width = field.shape
    half = size // 2
    parts = field.reshape(batch, half, 2, half, 2, width).transpose(0, 1, 3, 2, 4, 5)
    return parts.reshape(batch * half * half, 4 * width)

def from_depth(rows, batch, size):
    half = size // 2
    width = rows.shape[1] // 4
    parts = rows.reshape(batch, half, half, 2, 2, width).transpose(0, 1, 3, 2, 4, 5)
    return parts.reshape(batch, size, size, width)

def encode(params, pix, geom):
    w_pixel, w_res, w_scale, w_latent, gains = params
    batch = geom[0].shape[0]
    field = low_back(product(pix, low(w_pixel[0]))).reshape(batch, SIDE, SIDE, C)
    field = block(field, low(w_res[0]), low(w_res[1]), gains, 0, geom)
    hidden = low_back(product(to_depth(low(field)), low(w_scale[0])))
    return low_back(product(low(jax.nn.silu(hidden)), low(w_latent[0])))

def decode_loss(params, latent, shift, pix, mask, geom):
    w_pixel, w_res, w_scale, w_latent, gains = params
    batch = geom[0].shape[0]
    quant = latent + shift
    inner = low_back(product(low(quant), low(w_latent[1]).T))
    upper = low_back(product(low(jax.nn.silu(inner)), low(w_scale[1]).T))
    field = from_depth(upper, batch, SIDE)
    field = block(field, low(w_res[2]), low(w_res[3]), gains, 2, geom)
    outer = low(jax.nn.silu(field)).reshape(-1, C)
    recon = low_back(product(outer, low(w_pixel[1]).T))
    err = recon - pix
    return jnp.sum(mask * (jnp.sqrt(err * err + 1.0) - 1.0))

def adam_step(weight, moment, second, grad, rate):
    moment_new = 0.5 * moment + 0.5 * grad
    second_new = 0.5 * second + 0.5 * grad * grad
    fix = 1.0 - 0.5 ** STEP
    weight_new = weight - rate * (moment_new / fix / (jnp.sqrt(second_new / fix) + 1e-12) + 0.01 * weight)
    return (weight_new, moment_new, second_new)

def reference(pixels, valid_mask, size_groups, code_index, w_pixel, w_res, w_scale, w_latent, norm_gains, moment_pixel, moment_res, moment_scale, moment_latent, moment_gains, second_pixel, second_res, second_scale, second_latent, second_gains, ema_counts, ema_sums):
    devices = N_DP * N_FSDP
    rows_dev = pixels.shape[0] // devices
    lat_dev = code_index.shape[1] // devices
    canv = size_groups.shape[0] // devices
    latent_all = code_index.shape[1]
    mask = valid_mask.astype(jnp.float32)
    count = jnp.sum(mask)
    book = low(ema_sums / ema_counts[:, None])
    q_cum = jnp.cumsum(book[code_index], axis=0)
    params = (w_pixel, w_res, w_scale, w_latent, norm_gains)
    pix_all = pixels.astype(jnp.float32).reshape(devices, rows_dev, -1)
    mask_all = mask.reshape(devices, rows_dev, -1)
    group_all = size_groups.reshape(devices, canv)
    q_all = q_cum.reshape(DEPTH, devices, lat_dev, -1).transpose(1, 0, 2, 3)

    def one_device(carry, item):
        pix, msk, groups, qc = item
        geom = geometry(groups, SIDE, C)
        shift = qc[DEPTH - 1] - encode(params, pix, geom)

        def loss_of(values):
            latent = encode(values, pix, geom)
            diff = latent[None] - qc
            commit = jnp.sum(diff * diff)
            smooth = decode_loss(values, latent, shift, pix, msk, geom)
            return (smooth / count + COMMIT_WEIGHT * commit / (latent_all * ZD), (smooth, commit, latent))
        value, pull, extra = jax.vjp(loss_of, params, has_aux=True)
        grads = pull(jnp.ones_like(value))[0]
        grad_total, smooth_total, commit_total = carry
        grad_total = jax.tree.map(jnp.add, grad_total, grads)
        return ((grad_total, smooth_total + extra[0], commit_total + extra[1]), extra[2])
    start = (jax.tree.map(jnp.zeros_like, params), jnp.zeros((), jnp.float32), jnp.zeros((), jnp.float32))
    (grads, smooth_sum, commit_sum), latent_parts = lax.scan(one_device, start, (pix_all, mask_all, group_all, q_all))
    latent = latent_parts.reshape(latent_all, -1)
    squares = jnp.zeros((), jnp.float32)
    for grad in grads:
        squares = squares + jnp.sum(grad * grad)
    norm = jnp.sqrt(squares)
    factor = CLIP_AT / jnp.maximum(norm, CLIP_AT)
    moments = (moment_pixel, moment_res, moment_scale, moment_latent, moment_gains)
    seconds = (second_pixel, second_res, second_scale, second_latent, second_gains)
    rates = (WEIGHT_RATE, WEIGHT_RATE, WEIGHT_RATE, WEIGHT_RATE, GAIN_RATE)
    updated = [adam_step(w, m, v, g * factor, r) for w, m, v, g, r in zip(params, moments, seconds, grads, rates)]
    prev = jnp.concatenate([jnp.zeros_like(q_cum[:1]), q_cum[:-1]], axis=0)
    resid = low(latent[None] - prev).reshape(-1, ZD)
    flat = code_index.reshape(-1)
    sums = jax.ops.segment_sum(resid, flat, num_segments=K)
    counts = jax.ops.segment_sum(jnp.ones(flat.shape, jnp.float32), flat, num_segments=K)
    counts_new = EMA_DECAY * ema_counts + (1.0 - EMA_DECAY) * counts
    sums_new = EMA_DECAY * ema_sums + (1.0 - EMA_DECAY) * sums
    book_new = sums_new / counts_new[:, None]
    outputs = [jnp.stack([smooth_sum, count, commit_sum]), norm.reshape(1)]
    for index in range(4):
        weight_new, moment_new, second_new = updated[index]
        outputs += [weight_new, moment_new, second_new, weight_new.astype(jnp.bfloat16)]
    outputs += list(updated[4])
    outputs += [counts_new, sums_new, book_new, book_new.astype(jnp.bfloat16)]
    return tuple(outputs)
```

```python
import functools
import jax
import jax.numpy as jnp
from jax import lax
from jax.experimental import pallas as pl
from jax.experimental.pallas import tpu as pltpu
from jax.sharding import PartitionSpec as P

C = 512
ZD = 256
GROUPS = 32
SIDE = 32
STEP = 5
COMMIT_WEIGHT = 0.25
CLIP_AT = 1e-05
EMA_DECAY = 0.8
WEIGHT_RATE = 0.03
GAIN_RATE = 0.4
ROWS = SIDE * SIDE
PAD = SIDE
HIGH = lax.Precision.HIGHEST
F32 = jnp.float32
BF16 = jnp.bfloat16
VMEM_LIMIT = 60 * 1024 * 1024


def sigmoid(v):
    return 1.0 / (1.0 + jnp.exp(-v))


def nt(left, right):
    return lax.dot_general(left, right, (((1,), (1,)), ((), ())), preferred_element_type=F32)


def nn(left, right):
    return lax.dot_general(left, right, (((1,), (0,)), ((), ())), preferred_element_type=F32)


def image_mean(sums, group):
    width = C // GROUPS
    row = lax.broadcasted_iota(jnp.int32, (C, C), 0) // width
    col = lax.broadcasted_iota(jnp.int32, (C, C), 1) // width
    same_group = (row == col).astype(F32)
    left = lax.broadcasted_iota(jnp.int32, (16, 16), 0)
    right = lax.broadcasted_iota(jnp.int32, (16, 16), 1)
    same_image = (((left >> 2) >> group) == ((right >> 2) >> group)) & (
        ((left & 3) >> group) == ((right & 3) >> group)
    )
    side = 8 << group
    count = (side * side * width).astype(F32)
    spread = lax.dot_general(
        sums, same_group, (((1,), (0,)), ((), ())), precision=HIGH, preferred_element_type=F32
    )
    total = lax.dot_general(
        same_image.astype(F32), spread, (((1,), (0,)), ((), ())), precision=HIGH, preferred_element_type=F32
    )
    return total / count


def tile_rows(block):
    return jnp.sum(block.reshape(4, 8, C), axis=1)


def spread_rows(ref, tiles):
    for ty in range(4):
        for tx in range(4):
            t = 4 * ty + tx
            ref[ty, 8 * tx : 8 * tx + 8, :] = jnp.broadcast_to(tiles[t : t + 1, :], (8, C))


def norm_stats(x_ref, group, mean_ref, rstd_ref):
    parts = []
    for ty in range(4):
        acc = x_ref[pl.ds(ty * 256, 32), :]
        for y in range(1, 8):
            acc = acc + x_ref[pl.ds(ty * 256 + y * 32, 32), :]
        parts.append(tile_rows(acc))
    spread_rows(mean_ref, image_mean(jnp.concatenate(parts, axis=0), group))
    parts = []
    for ty in range(4):
        mu = mean_ref[ty]
        acc = jnp.zeros((32, C), F32)
        for y in range(8):
            cen = x_ref[pl.ds(ty * 256 + y * 32, 32), :] - mu
            acc = acc + cen * cen
        parts.append(tile_rows(acc))
    var = image_mean(jnp.concatenate(parts, axis=0), group)
    spread_rows(rstd_ref, lax.rsqrt(var + 1e-05))


def store_shifts(ref, y, val, side):
    x = lax.broadcasted_iota(jnp.int32, (32, C), 0) & (side - 1)
    zero = jnp.zeros((32, C), F32)
    left = jnp.where(x != 0, pltpu.roll(val, 1, 0), zero)
    right = jnp.where(x != side - 1, pltpu.roll(val, 31, 0), zero)
    rows = pl.ds(pl.multiple_of(PAD + y * 32, 32), 32)
    ref[rows, 0:C] = left.astype(BF16)
    ref[rows, C : 2 * C] = val.astype(BF16)
    ref[rows, 2 * C : 3 * C] = right.astype(BF16)


def clear_pads(ref):
    ref[0:PAD, :] = jnp.zeros((PAD, 3 * C), BF16)
    ref[PAD + ROWS : 2 * PAD + ROWS, :] = jnp.zeros((PAD, 3 * C), BF16)


def row_mask(shape, dim, dy, side):
    y = (lax.broadcasted_iota(jnp.int32, shape, dim) // 32) & (side - 1)
    return y != 0 if dy < 0 else y != side - 1


def conv_fwd_kernel(has_res, sg_ref, x_ref, gain_ref, wt_hbm, *rest):
    if has_res:
        res_ref, t_ref, a3_ref, wt_ref, mean_ref, rstd_ref, sem = rest
    else:
        t_ref, a3_ref, wt_ref, mean_ref, rstd_ref, sem = rest
    copy = pltpu.make_async_copy(wt_hbm, wt_ref, sem)
    copy.start()
    group = sg_ref[0]
    side = 8 << group
    norm_stats(x_ref, group, mean_ref, rstd_ref)
    clear_pads(a3_ref)
    gamma = gain_ref[0:1, :]
    beta = gain_ref[1:2, :]

    def body(y, carry):
        ty = y // 8
        v = (x_ref[pl.ds(pl.multiple_of(y * 32, 32), 32), :] - mean_ref[ty]) * rstd_ref[ty] * gamma + beta
        store_shifts(a3_ref, y, v * sigmoid(v), side)
        return carry

    lax.fori_loop(0, 32, body, 0, unroll=2)
    copy.wait()
    out = nt(a3_ref[PAD : PAD + ROWS, :], wt_ref[:, 3 * C : 6 * C])
    if has_res:
        out = out + res_ref[...]
    t_ref[...] = out
    for dy in (-1, 1):
        part = nt(a3_ref[PAD + 32 * dy : PAD + 32 * dy + ROWS, :], wt_ref[:, (dy + 1) * 3 * C : (dy + 2) * 3 * C])
        t_ref[...] += jnp.where(row_mask((ROWS, 1), 0, dy, side), part, 0.0)


SMEM = pl.BlockSpec(memory_space=pltpu.SMEM)
VM = pl.BlockSpec(memory_space=pltpu.VMEM)
ANY = pl.BlockSpec(memory_space=pl.ANY)
PARAMS = pltpu.CompilerParams(vmem_limit_bytes=VMEM_LIMIT)


def conv_fwd(group, x, gains, wt, res=None):
    args = [group, x, gains, wt] + ([] if res is None else [res])
    return pl.pallas_call(
        functools.partial(conv_fwd_kernel, res is not None),
        out_shape=(
            jax.ShapeDtypeStruct((ROWS, C), F32),
            jax.ShapeDtypeStruct((ROWS + 2 * PAD, 3 * C), BF16),
        ),
        in_specs=[SMEM, VM, VM, ANY] + ([] if res is None else [VM]),
        out_specs=(VM, VM),
        scratch_shapes=[
            pltpu.VMEM((C, 9 * C), BF16),
            pltpu.VMEM((4, 32, C), F32),
            pltpu.VMEM((4, 32, C), F32),
            pltpu.SemaphoreType.DMA,
        ],
        compiler_params=PARAMS,
        name="conv_fwd",
    )(*args)


def conv_bwd_kernel(has_res, out_low, sg_ref, dt_ref, a3_ref, x_ref, gain_ref, wt_hbm, *rest):
    if has_res:
        res_ref, *rest = rest
    dw_ref, dx_ref, dgain_ref, wt_ref, d3_ref, dtt_ref, mean_ref, rstd_ref, ds_ref, sem = rest
    copy = pltpu.make_async_copy(wt_hbm, wt_ref, sem)
    copy.start()
    group = sg_ref[0]
    side = 8 << group
    clear_pads(d3_ref)

    def body(y, carry):
        val = dt_ref[pl.ds(pl.multiple_of(y * 32, 32), 32), :].astype(F32)
        store_shifts(d3_ref, y, val, side)
        return carry

    lax.fori_loop(0, 32, body, 0, unroll=2)
    dtt_ref[1] = dt_ref[...].astype(F32).T.astype(BF16)
    flat = dtt_ref[1]
    for dy in (-1, 1):
        keep = row_mask((1, ROWS), 1, dy, side).astype(BF16)
        dtt_ref[dy + 1] = flat * keep
    for dy in (-1, 0, 1):
        dw = nn(dtt_ref[dy + 1], a3_ref[PAD + 32 * dy : PAD + 32 * dy + ROWS, :])
        dw_ref[:, (dy + 1) * 3 * C : (dy + 2) * 3 * C] = dw.astype(dw_ref.dtype)
    copy.wait()
    for dy in (0, -1, 1):
        part = None
        for dx in (-1, 0, 1):
            t = 3 * (dy + 1) + dx + 1
            one = nn(
                d3_ref[PAD - 32 * dy : PAD - 32 * dy + ROWS, (1 - dx) * C : (2 - dx) * C],
                wt_ref[:, t * C : (t + 1) * C],
            )
            part = one if part is None else part + one
        if dy == 0:
            ds_ref[...] = part
        else:
            ds_ref[...] += jnp.where(row_mask((ROWS, 1), 0, -dy, side), part, 0.0)
    norm_stats(x_ref, group, mean_ref, rstd_ref)
    gamma = gain_ref[0:1, :]
    beta = gain_ref[1:2, :]
    first, second = [], []
    for ty in range(4):
        mu, rs = mean_ref[ty], rstd_ref[ty]

        def step(y, carry, ty=ty, mu=mu, rs=rs):
            one, two = carry
            rows = pl.ds(pl.multiple_of(ty * 256 + y * 32, 32), 32)
            xh = (x_ref[rows, :] - mu) * rs
            v = xh * gamma + beta
            sg = sigmoid(v)
            ds = ds_ref[rows, :] * (sg * (1.0 + v * (1.0 - sg)))
            ds_ref[rows, :] = ds
            return (one + ds, two + ds * xh)

        zero = jnp.zeros((32, C), F32)
        one, two = lax.fori_loop(0, 8, step, (zero, zero))
        first.append(tile_rows(one))
        second.append(tile_rows(two))
    first = jnp.concatenate(first, axis=0)
    second = jnp.concatenate(second, axis=0)
    dgain_ref[0:1, :] = jnp.sum(second, axis=0, keepdims=True)
    dgain_ref[1:2, :] = jnp.sum(first, axis=0, keepdims=True)
    m_one = image_mean(first * gamma, group)
    m_two = image_mean(second * gamma, group)
    for ty in range(4):
        mu, rs = mean_ref[ty], rstd_ref[ty]
        one = jnp.concatenate([jnp.broadcast_to(m_one[4 * ty + tx : 4 * ty + tx + 1, :], (8, C)) for tx in range(4)], axis=0)
        two = jnp.concatenate([jnp.broadcast_to(m_two[4 * ty + tx : 4 * ty + tx + 1, :], (8, C)) for tx in range(4)], axis=0)

        def step(y, carry, ty=ty, mu=mu, rs=rs, one=one, two=two):
            rows = pl.ds(pl.multiple_of(ty * 256 + y * 32, 32), 32)
            xh = (x_ref[rows, :] - mu) * rs
            dx = rs * (ds_ref[rows, :] * gamma - one - xh * two)
            if has_res:
                dx = dx + res_ref[rows, :]
            dx_ref[rows, :] = dx.astype(dx_ref.dtype)
            return carry

        lax.fori_loop(0, 8, step, 0)


def conv_bwd(group, dt, a3, x, gains, wt, res=None, low=True, grad_type=BF16):
    args = [group, dt, a3, x, gains, wt] + ([] if res is None else [res])
    return pl.pallas_call(
        functools.partial(conv_bwd_kernel, res is not None, low),
        out_shape=(
            jax.ShapeDtypeStruct((C, 9 * C), grad_type),
            jax.ShapeDtypeStruct((ROWS, C), BF16 if low else F32),
            jax.ShapeDtypeStruct((2, C), F32),
        ),
        in_specs=[SMEM, VM, VM, VM, VM, ANY] + ([] if res is None else [VM]),
        out_specs=(VM, VM, VM),
        scratch_shapes=[
            pltpu.VMEM((C, 9 * C), BF16),
            pltpu.VMEM((ROWS + 2 * PAD, 3 * C), BF16),
            pltpu.VMEM((3, C, ROWS), BF16),
            pltpu.VMEM((4, 32, C), F32),
            pltpu.VMEM((4, 32, C), F32),
            pltpu.VMEM((ROWS, C), F32),
            pltpu.SemaphoreType.DMA,
        ],
        compiler_params=PARAMS,
        name="conv_bwd",
    )(*args)


def silu_slope(value):
    gate = sigmoid(value)
    return gate * (1.0 + value * (1.0 - gate))


def transposed(value):
    return value.astype(F32).T.astype(BF16)


HALF = SIDE // 2
LAT = HALF * HALF


def to_depth(src_ref, lanes_ref, dst_ref):
    for k in range(C // 128):
        lanes_ref[k] = src_ref[:, k * 128 : (k + 1) * 128]
    for k in range(C // 128):
        for b in range(2):
            block = lanes_ref[k, pl.ds(b, ROWS // 2, stride=2), :].reshape(HALF, 2, HALF, 128)
            for a in range(2):
                at = (2 * a + b) * C + k * 128
                dst_ref[:, at : at + 128] = block[:, a].reshape(LAT, 128).astype(dst_ref.dtype)


def from_depth(src_ref, lanes_ref, dst_ref):
    for k in range(C // 128):
        for b in range(2):
            pair = [
                src_ref[:, (2 * a + b) * C + k * 128 : (2 * a + b) * C + (k + 1) * 128].reshape(HALF, 1, HALF, 128)
                for a in range(2)
            ]
            lanes_ref[k, pl.ds(b, ROWS // 2, stride=2), :] = jnp.concatenate(pair, axis=1).reshape(ROWS // 2, 128)
    for k in range(C // 128):
        dst_ref[:, k * 128 : (k + 1) * 128] = lanes_ref[k]


def mid_fwd_kernel(
    h_ref, ws0_ref, wl0_ref, code_ref, wl1_ref, ws1_ref,
    e_ref, d_ref, s_ref, q_ref, y_ref, s2_ref, g_ref, commit_ref, dcom_ref, resid_ref, u_ref, lanes_ref,
):
    to_depth(h_ref, lanes_ref, e_ref)
    d = nt(e_ref[...], ws0_ref[...])
    d_ref[...] = d
    s = (d * sigmoid(d)).astype(BF16)
    s_ref[...] = s
    z = nt(s, wl0_ref[...])
    q = jnp.zeros((LAT, ZD), F32)
    commit = jnp.zeros((LAT, ZD), F32)
    dcom = jnp.zeros((LAT, ZD), F32)
    for k in range(4):
        resid_ref[k * LAT : (k + 1) * LAT, :] = (z - q).astype(BF16)
        q = q + code_ref[k * LAT : (k + 1) * LAT, :].astype(F32)
        diff = z - q
        commit = commit + diff * diff
        dcom = dcom + diff
    commit_ref[...] = jnp.sum(commit, axis=0, keepdims=True)
    dcom_ref[...] = dcom
    quant = (z + (q - z)).astype(BF16)
    q_ref[...] = quant
    y = nn(quant, wl1_ref[...])
    y_ref[...] = y
    s2 = (y * sigmoid(y)).astype(BF16)
    s2_ref[...] = s2
    u_ref[...] = nn(s2, ws1_ref[...])
    from_depth(u_ref, lanes_ref, g_ref)


def mid_fwd(h, ws0, wl0, codes, wl1, ws1):
    shape = jax.ShapeDtypeStruct
    return pl.pallas_call(
        mid_fwd_kernel,
        out_shape=(
            shape((LAT, 4 * C), BF16),
            shape((LAT, C), F32),
            shape((LAT, C), BF16),
            shape((LAT, ZD), BF16),
            shape((LAT, C), F32),
            shape((LAT, C), BF16),
            shape((ROWS, C), F32),
            shape((1, ZD), F32),
            shape((LAT, ZD), F32),
            shape((4 * LAT, ZD), BF16),
        ),
        in_specs=[VM] * 6,
        out_specs=(VM,) * 10,
        scratch_shapes=[pltpu.VMEM((LAT, 4 * C), F32), pltpu.VMEM((C // 128, ROWS, 128), F32)],
        compiler_params=PARAMS,
        name="mid_fwd",
    )(h, ws0, wl0, codes, wl1, ws1)


def mid_bwd_kernel(
    scale, dg_ref, e_ref, d_ref, s_ref, q_ref, y_ref, s2_ref, dcom_ref, ws0_ref, wl0_ref, wl1_ref, ws1_ref,
    dws0_ref, dws1_ref, dwl0_ref, dwl1_ref, dh_ref, du_ref, de_ref, lanes_ref,
):
    to_depth(dg_ref, lanes_ref, du_ref)
    out = dws0_ref.dtype
    ds2 = nt(du_ref[...], ws1_ref[...])
    dy = (ds2 * silu_slope(y_ref[...])).astype(BF16)
    dws1_ref[...] = nn(transposed(s2_ref[...]), du_ref[...]).astype(out)
    dwl1_ref[...] = nn(transposed(q_ref[...]), dy).astype(out)
    dz = (nt(dy, wl1_ref[...]) + scale * dcom_ref[...]).astype(BF16)
    dwl0_ref[...] = nn(transposed(dz), s_ref[...]).astype(out)
    ds = nn(dz, wl0_ref[...])
    dd = (ds * silu_slope(d_ref[...])).astype(BF16)
    dws0_ref[...] = nn(transposed(dd), e_ref[...]).astype(out)
    de_ref[...] = nn(dd, ws0_ref[...])
    from_depth(de_ref, lanes_ref, dh_ref)


def mid_bwd(scale, dg, e, d, s, q, y, s2, dcom, ws0, wl0, wl1, ws1, grad_type=BF16):
    shape = jax.ShapeDtypeStruct
    return pl.pallas_call(
        functools.partial(mid_bwd_kernel, scale),
        out_shape=(
            shape((C, 4 * C), grad_type),
            shape((C, 4 * C), grad_type),
            shape((ZD, C), grad_type),
            shape((ZD, C), grad_type),
            shape((ROWS, C), F32),
        ),
        in_specs=[VM] * 12,
        out_specs=(VM,) * 5,
        scratch_shapes=[
            pltpu.VMEM((LAT, 4 * C), BF16),
            pltpu.VMEM((LAT, 4 * C), F32),
            pltpu.VMEM((C // 128, ROWS, 128), F32),
        ],
        compiler_params=PARAMS,
        name="mid_bwd",
    )(dg, e, d, s, q, y, s2, dcom, ws0, wl0, wl1, ws1)


def head_kernel(total_ref, g_ref, wp_ref, pix_ref, mask_ref, dw_ref, dg_ref, loss_ref, o_ref, dr_ref):
    inv = total_ref[0]
    loss = jnp.zeros((1, pix_ref.shape[1]), F32)
    for i in range(4):
        rows = pl.ds(i * 256, 256)
        g = g_ref[rows, :]
        gate = sigmoid(g)
        o = (g * gate).astype(BF16)
        o_ref[rows, :] = o
        err = nn(o, wp_ref[...]) - pix_ref[rows, :].astype(F32)
        keep = mask_ref[rows, :].astype(F32)
        smooth = jnp.sqrt(err * err + 1.0)
        loss = loss + jnp.sum(keep * (smooth - 1.0), axis=0, keepdims=True)
        dr = (keep * err / smooth / inv).astype(BF16)
        dr_ref[rows, :] = dr
        do = nt(dr, wp_ref[...])
        dg_ref[rows, :] = do * (gate * (1.0 + g * (1.0 - gate)))
    loss_ref[...] = loss
    dw_ref[...] = nn(transposed(o_ref[...]), dr_ref[...]).astype(dw_ref.dtype)


def head(total, g, wp, pix, mask, grad_type=BF16):
    shape = jax.ShapeDtypeStruct
    width = pix.shape[1]
    return pl.pallas_call(
        head_kernel,
        out_shape=(shape((C, width), grad_type), shape((ROWS, C), F32), shape((1, width), F32)),
        in_specs=[SMEM, VM, VM, VM, VM],
        out_specs=(VM,) * 3,
        scratch_shapes=[pltpu.VMEM((ROWS, C), BF16), pltpu.VMEM((ROWS, width), BF16)],
        compiler_params=PARAMS,
        name="head",
    )(total, g, wp, pix, mask)


BOTH = ("dp", "fsdp")
RES_W, PIX_W, SC_W, LAT_W = 9 * C, 768, 4 * C, C


def swap(shard):
    return jnp.swapaxes(shard, -1, -2).astype(BF16)


def exchange(x, axis, mask):
    n = lax.axis_size(axis)
    return lax.ppermute(x, axis, [(i, i ^ mask) for i in range(n)])


def everyone(x):
    n = lax.axis_size("dp") * lax.axis_size("fsdp")
    return lax.all_to_all(jnp.broadcast_to(x[None], (n,) + x.shape), BOTH, 0, 0, tiled=True)


STREAM_MASKS = ((2, 1), (1, 2))


def part_shapes(kind, lanes, blocks, dtype):
    if kind == "mat":
        return [jax.ShapeDtypeStruct((32 * 2 * blocks, 4 * lanes), dtype)]
    if kind == "lat":
        return [jax.ShapeDtypeStruct((32 * blocks, 4 * lanes), dtype)] * 2
    return [jax.ShapeDtypeStruct((4, 32 * 2 * blocks, lanes), dtype)]


def part_place(kind, refs, lanes, stream, dp, f):
    if kind == "lat":
        rows = pl.ds(pl.multiple_of(dp * 32, 32), 32)
        return refs[stream].at[rows, pl.ds(pl.multiple_of(f * lanes, 128), lanes)]
    rows = pl.ds(pl.multiple_of(dp * 64 + stream * 32, 32), 32)
    if kind == "mat":
        return refs[0].at[rows, pl.ds(pl.multiple_of(f * lanes, 128), lanes)]
    return refs[0].at[f, rows, :]


def part_count(kind):
    return 2 if kind == "lat" else 1


def assemble_kernel(parts, z_size, me_ref, *rest):
    pieces = rest[:8]
    outs = rest[8:-1]
    sems = rest[-1]
    dp, f = me_ref[0], me_ref[1]
    copies = []
    for stream in range(2):
        near, far = STREAM_MASKS[stream]
        for far_bit in range(2):
            for core_bit in range(2):
                piece = pieces[stream * 4 + core_bit * 2 + far_bit]
                for near_bit in range(2):
                    for z in range(z_size):
                        at_dp = dp ^ (2 * z + core_bit)
                        at_f = f ^ (near * near_bit + far * far_bit)
                        lane, first = 0, 0
                        for kind, lanes in parts:
                            refs = outs[first : first + part_count(kind)]
                            copies.append(
                                pltpu.make_async_copy(
                                    piece.at[near_bit * z_size + z, :, pl.ds(lane, lanes)],
                                    part_place(kind, refs, lanes, stream, at_dp, at_f),
                                    sems.at[len(copies)],
                                )
                            )
                            lane += lanes
                            first += part_count(kind)
    for copy in copies:
        copy.start()
    for copy in copies:
        copy.wait()


def my_place():
    return jnp.stack([lax.axis_index("dp"), lax.axis_index("fsdp")]).astype(jnp.int32)


def gather_chunk(shard, parts):
    z_size = lax.axis_size("dp") // 2
    lanes = shard.shape[1]
    got = [shard] + [exchange(shard, "dp", 2 * k) for k in range(1, z_size)]
    pieces = []
    for stream in range(2):
        near, far = STREAM_MASKS[stream]
        a = jnp.stack([g[stream * 32 : stream * 32 + 32] for g in got])
        b = jnp.concatenate([a, exchange(a, "fsdp", near)], axis=0)
        c = exchange(b, "fsdp", far)
        pieces += [b, c, exchange(b, "dp", 1), exchange(c, "dp", 1)]
    blocks = 2 * z_size
    shapes = [s for kind, width in parts for s in part_shapes(kind, width, blocks, BF16)]
    return pl.pallas_call(
        functools.partial(assemble_kernel, parts, z_size),
        out_shape=tuple(shapes),
        in_specs=[SMEM] + [ANY] * 8,
        out_specs=(ANY,) * len(shapes),
        scratch_shapes=[pltpu.SemaphoreType.DMA((32 * z_size // 2 * 2 * len(parts),))],
        compiler_params=PARAMS,
        name="assemble",
    )(my_place(), *pieces)


def split_kernel(parts, z_size, me_ref, *rest):
    count = sum(part_count(kind) for kind, _ in parts)
    ins = rest[:count]
    outs = rest[count : count + 2]
    sems = rest[-1]
    dp, f = me_ref[0], me_ref[1]
    copies = []
    for core_bit in range(2):
        for stream in range(2):
            near, far = STREAM_MASKS[stream]
            for far_bit in range(2):
                for near_bit in range(2):
                    for z in range(z_size):
                        at_dp = dp ^ (2 * z + core_bit)
                        at_f = f ^ (near * near_bit + far * far_bit)
                        lane, first = 0, 0
                        for kind, lanes in parts:
                            refs = ins[first : first + part_count(kind)]
                            copies.append(
                                pltpu.make_async_copy(
                                    part_place(kind, refs, lanes, stream, at_dp, at_f),
                                    outs[core_bit].at[
                                        stream, (2 * far_bit + near_bit) * z_size + z, :, pl.ds(lane, lanes)
                                    ],
                                    sems.at[len(copies)],
                                )
                            )
                            lane += lanes
                            first += part_count(kind)
    for copy in copies:
        copy.start()
    for copy in copies:
        copy.wait()


def scatter_chunk(grads, parts):
    z_size = lax.axis_size("dp") // 2
    lanes = sum(width for _, width in parts)
    block = jax.ShapeDtypeStruct((2, 4 * z_size, 32, lanes), BF16)
    keep, send = pl.pallas_call(
        functools.partial(split_kernel, parts, z_size),
        out_shape=(block, block),
        in_specs=[SMEM] + [ANY] * len(grads),
        out_specs=(ANY, ANY),
        scratch_shapes=[pltpu.SemaphoreType.DMA((32 * z_size // 2 * 2 * len(parts),))],
        compiler_params=PARAMS,
        name="split",
    )(my_place(), *grads)
    got = exchange(send, "dp", 1)
    totals = []
    for stream in range(2):
        near, far = STREAM_MASKS[stream]
        a = keep[stream].astype(F32) + got[stream].astype(F32)
        r = exchange(a[2 * z_size :].astype(BF16), "fsdp", far)
        a = a[: 2 * z_size] + r.astype(F32)
        r = exchange(a[z_size:].astype(BF16), "fsdp", near)
        totals.append(a[:z_size] + r.astype(F32))
    both = jnp.concatenate(totals, axis=1)
    total = both[0]
    for k in range(1, z_size):
        total = total + exchange(both[k].astype(BF16), "dp", 2 * k).astype(F32)
    return total


def fetch_whole(shard):
    cols = lax.all_gather(shard.astype(BF16), "dp", axis=1, tiled=True)
    return jnp.swapaxes(lax.all_gather(cols, "fsdp", axis=0, tiled=True), 0, 1)


def reduce_whole(grad):
    rows = lax.psum_scatter(jnp.swapaxes(grad, 0, 1), "fsdp", scatter_dimension=0, tiled=True)
    return jnp.swapaxes(lax.psum_scatter(rows, "dp", scatter_dimension=1, tiled=True), 0, 1)


MIX = (("mat", 512), ("mat", 512), ("lat", 128))
RES = (("mat", 1152),)
RES_PIX = (("mat", 1152), ("pix", 384))


def fetch_all(w_pixel, w_res, w_scale, w_latent, paired):
    if not paired:
        pix = [fetch_whole(w_pixel[i]) for i in range(2)]
        res = [fetch_whole(w_res[i]) for i in range(4)]
        scale = [fetch_whole(w_scale[i]) for i in range(2)]
        latent = [fetch_whole(w_latent[i]) for i in range(2)]
        return pix, res, scale, latent
    res_t, pix_t, scale_t, lat_t = swap(w_res), swap(w_pixel), swap(w_scale), swap(w_latent)
    res0, pix = gather_chunk(jnp.concatenate([res_t[0], pix_t[0], pix_t[1]], axis=1), RES_PIX)
    (res1,) = gather_chunk(res_t[1], RES)
    mix = jnp.concatenate([scale_t[0], scale_t[1], lat_t.reshape(-1, lat_t.shape[2])], axis=1)
    scale0, scale1, lat0, lat1 = gather_chunk(mix, MIX)
    (res2,) = gather_chunk(res_t[2], RES)
    (res3,) = gather_chunk(res_t[3], RES)
    half = pix.shape[2] // 2
    pixs = [pix[:, :, i * half : (i + 1) * half].transpose(1, 0, 2).reshape(C, 4 * half) for i in range(2)]
    return pixs, [res0, res1, res2, res3], [scale0, scale1], [lat0, lat1]


def adam_step(weight, moment, second, grad, rate):
    moment_new = 0.5 * moment + 0.5 * grad
    second_new = 0.5 * second + 0.5 * grad * grad
    fix = 1.0 - 0.5**STEP
    weight_new = weight - rate * (
        moment_new / fix / (jnp.sqrt(second_new / fix) + 1e-12) + 0.01 * weight
    )
    return (weight_new, moment_new, second_new)


def exact(left, right, dims):
    return lax.dot_general(left, right, (dims, ((), ())), preferred_element_type=F32)


def code_slots(codes, devices, capacity, rows):
    n = codes.shape[0]
    owner = codes // rows
    hot = (owner[:, None] == jnp.arange(devices, dtype=jnp.int32)[None, :]).astype(BF16)
    at = jnp.arange(n, dtype=jnp.int32)
    before = (at[None, :] < at[:, None]).astype(BF16)
    rank = exact(before, hot, ((1,), (0,)))
    place = jnp.sum(rank * hot.astype(F32), axis=1).astype(jnp.int32)
    slot = owner * capacity + place
    return (jnp.arange(devices * capacity, dtype=jnp.int32)[:, None] == slot[None, :]).astype(BF16)


def on_device(
    pixels,
    valid_mask,
    size_groups,
    code_index,
    w_pixel,
    w_res,
    w_scale,
    w_latent,
    norm_gains,
    moment_pixel,
    moment_res,
    moment_scale,
    moment_latent,
    moment_gains,
    second_pixel,
    second_res,
    second_scale,
    second_latent,
    second_gains,
    ema_counts,
    ema_sums,
):
    n_outer = lax.axis_size("dp")
    n_inner = lax.axis_size("fsdp")
    devices = n_outer * n_inner
    latent_all = code_index.shape[1] * devices
    rows = ema_sums.shape[0]
    paired = n_inner == 4 and w_res.shape[1] == 1152 and w_res.shape[2] == 64
    grad_type = BF16 if paired else F32

    pix_w, res_w, scale_w, lat_w = fetch_all(w_pixel, w_res, w_scale, w_latent, paired)

    valid = everyone(jnp.sum(valid_mask.astype(F32).reshape(-1, 128), axis=0, keepdims=True))
    total_valid = jnp.sum(valid)

    codes = code_index.reshape(-1)
    capacity = max(2, 2 * codes.shape[0] // devices)
    pick = code_slots(codes, devices, capacity, rows)
    local = codes % rows
    cols = jnp.stack([local // 16, local % 16, jnp.ones_like(local)], axis=1).astype(BF16)
    want = exact(pick, cols, ((1,), (0,)))
    wanted = jnp.where(want[:, 2] > 0.5, want[:, 0] * 16.0 + want[:, 1], -1.0).astype(jnp.int32)
    asked = lax.all_to_all(wanted.reshape(devices, 1, capacity), BOTH, 0, 0, tiled=True).reshape(-1)
    hot_rows = (asked[:, None] == jnp.arange(rows, dtype=jnp.int32)[None, :]).astype(BF16)
    book = (ema_sums / ema_counts[:, None]).astype(BF16)
    answer = exact(hot_rows, book, ((1,), (0,))).astype(BF16)
    replies = lax.all_to_all(answer.reshape(devices, capacity, ZD), BOTH, 0, 0, tiled=True).reshape(-1, ZD)
    picked = exact(pick, replies, ((0,), (0,))).astype(BF16)

    gains = [jnp.stack([norm_gains[j], norm_gains[4 + j]]) for j in range(4)]
    h0 = nt(pixels, pix_w[0])
    t1, a1 = conv_fwd(size_groups, h0, gains[0], res_w[0])
    h1, a2 = conv_fwd(size_groups, t1, gains[1], res_w[1], h0)
    e, d, s, quant, y, s2, g0, commit, dcom, resid = mid_fwd(h1, scale_w[0], lat_w[0], picked, lat_w[1], scale_w[1])
    t3, a3 = conv_fwd(size_groups, g0, gains[2], res_w[2])
    g1, a4 = conv_fwd(size_groups, t3, gains[3], res_w[3], g0)

    sent = exact(pick, resid, ((1,), (0,))).astype(BF16)
    held = lax.all_to_all(sent.reshape(devices, capacity, ZD), BOTH, 0, 0, tiled=True).reshape(-1, ZD)
    my_sums = exact(hot_rows, held, ((0,), (0,)))
    my_counts = jnp.sum(hot_rows.astype(F32), axis=0)
    counts_new = EMA_DECAY * ema_counts + (1.0 - EMA_DECAY) * my_counts
    sums_new = EMA_DECAY * ema_sums + (1.0 - EMA_DECAY) * my_sums
    book_new = sums_new / counts_new[:, None]

    d_head, dg1, loss = head(total_valid.reshape(1), g1, pix_w[1], pixels, valid_mask, grad_type)
    d_res3, dt3, dn3 = conv_bwd(size_groups, dg1, a4, t3, gains[3], res_w[3], None, True, grad_type)
    d_res2, dg0, dn2 = conv_bwd(size_groups, dt3, a3, g0, gains[2], res_w[2], dg1, False, grad_type)
    scale = 2.0 * COMMIT_WEIGHT / (latent_all * ZD)
    d_scale0, d_scale1, d_lat0, d_lat1, dh1 = mid_bwd(
        scale, dg0, e, d, s, quant, y, s2, dcom, scale_w[0], lat_w[0], lat_w[1], scale_w[1], grad_type
    )
    d_res1, dt1, dn1 = conv_bwd(size_groups, dh1, a2, t1, gains[1], res_w[1], None, True, grad_type)
    d_res0, dh0, dn0 = conv_bwd(size_groups, dt1, a1, h0, gains[0], res_w[0], dh1, True, grad_type)
    d_patch = exact(dh0, pixels, ((0,), (0,))).astype(grad_type)

    if paired:
        g_res3 = scatter_chunk([d_res3], RES)
        g_res2 = scatter_chunk([d_res2], RES)
        g_mix = scatter_chunk([d_scale0, d_scale1, d_lat0, d_lat1], MIX)
        g_res1 = scatter_chunk([d_res1], RES)
        d_pix = [g.reshape(C, 4, -1).transpose(1, 0, 2) for g in (d_patch, d_head)]
        g_last = scatter_chunk([d_res0, jnp.concatenate(d_pix, axis=2)], RES_PIX)
        wide = w_res.shape[1]
        g_pix = g_last[:, wide:]
        half = g_pix.shape[1] // 2
        grad_pixel = jnp.stack([g_pix[:, :half], g_pix[:, half:]])
        grad_res = jnp.stack([g_last[:, :wide], g_res1, g_res2, g_res3])
        grad_scale = jnp.stack([g_mix[:, :512], g_mix[:, 512:1024]])
        grad_latent = g_mix[:, 1024:].reshape(2, 32, -1)
    else:
        grad_pixel = jnp.stack([reduce_whole(g) for g in (d_patch, d_head)])
        grad_res = jnp.stack([reduce_whole(g) for g in (d_res0, d_res1, d_res2, d_res3)])
        grad_scale = jnp.stack([reduce_whole(g) for g in (d_scale0, d_scale1)])
        grad_latent = jnp.stack([reduce_whole(g) for g in (d_lat0, d_lat1)])

    gain_local = jnp.stack([dn0[0], dn1[0], dn2[0], dn3[0], dn0[1], dn1[1], dn2[1], dn3[1]])
    sums_local = jnp.concatenate(
        [
            gain_local.reshape(-1, 128),
            jnp.sum(loss.reshape(-1, 128), axis=0, keepdims=True),
            jnp.sum(commit.reshape(-1, 128), axis=0, keepdims=True),
        ]
    )
    sums_all = jnp.sum(everyone(sums_local), axis=0)
    grad_gains = sums_all[:-2].reshape(8, C)
    smooth_sum = jnp.sum(sums_all[-2])
    commit_sum = jnp.sum(sums_all[-1])

    squares = jnp.sum(grad_pixel * grad_pixel) + jnp.sum(grad_res * grad_res)
    squares = squares + jnp.sum(grad_scale * grad_scale) + jnp.sum(grad_latent * grad_latent)
    total_squares = jnp.sum(everyone(jnp.broadcast_to(squares, (1, 128)))[:, 0, 0]) + jnp.sum(grad_gains * grad_gains)
    norm = jnp.sqrt(total_squares)
    factor = CLIP_AT / jnp.maximum(norm, CLIP_AT)
    groups_all = [
        (w_pixel, moment_pixel, second_pixel, grad_pixel),
        (w_res, moment_res, second_res, grad_res),
        (w_scale, moment_scale, second_scale, grad_scale),
        (w_latent, moment_latent, second_latent, grad_latent),
    ]
    outputs = [jnp.stack([smooth_sum, total_valid, commit_sum]), norm.reshape(1)]
    for weight, moment, second, grad in groups_all:
        grad = jnp.swapaxes(grad * factor, 1, 2)
        weight_new, moment_new, second_new = adam_step(weight, moment, second, grad, WEIGHT_RATE)
        outputs += [weight_new, moment_new, second_new, weight_new.astype(BF16)]
    outputs += list(adam_step(norm_gains, moment_gains, second_gains, grad_gains * factor, GAIN_RATE))
    outputs += [counts_new, sums_new, book_new, book_new.astype(BF16)]
    return tuple(outputs)


def solution(mesh):
    placed = (
        P(("dp", "fsdp"), None),
        P(("dp", "fsdp"), None),
        P(("dp", "fsdp")),
        P(None, ("dp", "fsdp")),
        P(None, "fsdp", "dp"),
        P(None, "fsdp", "dp"),
        P(None, "fsdp", "dp"),
        P(None, "fsdp", "dp"),
        P(),
        P(None, "fsdp", "dp"),
        P(None, "fsdp", "dp"),
        P(None, "fsdp", "dp"),
        P(None, "fsdp", "dp"),
        P(),
        P(None, "fsdp", "dp"),
        P(None, "fsdp", "dp"),
        P(None, "fsdp", "dp"),
        P(None, "fsdp", "dp"),
        P(),
        P(("dp", "fsdp")),
        P(("dp", "fsdp"), None),
    )
    return jax.shard_map(
        on_device,
        mesh=mesh,
        in_specs=placed,
        out_specs=(
            P(),
            P(),
            P(None, "fsdp", "dp"),
            P(None, "fsdp", "dp"),
            P(None, "fsdp", "dp"),
            P(None, "fsdp", "dp"),
            P(None, "fsdp", "dp"),
            P(None, "fsdp", "dp"),
            P(None, "fsdp", "dp"),
            P(None, "fsdp", "dp"),
            P(None, "fsdp", "dp"),
            P(None, "fsdp", "dp"),
            P(None, "fsdp", "dp"),
            P(None, "fsdp", "dp"),
            P(None, "fsdp", "dp"),
            P(None, "fsdp", "dp"),
            P(None, "fsdp", "dp"),
            P(None, "fsdp", "dp"),
            P(),
            P(),
            P(),
            P(("dp", "fsdp")),
            P(("dp", "fsdp"), None),
            P(("dp", "fsdp"), None),
            P(("dp", "fsdp"), None),
        ),
        check_vma=False,
    )
```

```python
import functools
import jax
import jax.numpy as jnp
from jax import lax
from jax.experimental import pallas as pl
from jax.experimental.pallas import tpu as pltpu
from jax.sharding import Mesh
from jax.sharding import PartitionSpec as P

C = 512
ZD = 256
GROUPS = 32
SIDE = 32
STEP = 5
COMMIT_WEIGHT = 0.25
CLIP_AT = 1e-05
EMA_DECAY = 0.8
WEIGHT_RATE = 0.03
GAIN_RATE = 0.4
ROWS = SIDE * SIDE
PAD = SIDE
HIGH = lax.Precision.HIGHEST
F32 = jnp.float32
BF16 = jnp.bfloat16
VMEM_LIMIT = 60 * 1024 * 1024


def sigmoid(v):
    return 1.0 / (1.0 + jnp.exp(-v))


def nt(left, right):
    return lax.dot_general(left, right, (((1,), (1,)), ((), ())), preferred_element_type=F32)


def nn(left, right):
    return lax.dot_general(left, right, (((1,), (0,)), ((), ())), preferred_element_type=F32)


def image_mean(sums, group):
    width = C // GROUPS
    row = lax.broadcasted_iota(jnp.int32, (C, C), 0) // width
    col = lax.broadcasted_iota(jnp.int32, (C, C), 1) // width
    same_group = (row == col).astype(F32)
    left = lax.broadcasted_iota(jnp.int32, (16, 16), 0)
    right = lax.broadcasted_iota(jnp.int32, (16, 16), 1)
    same_image = (((left >> 2) >> group) == ((right >> 2) >> group)) & (
        ((left & 3) >> group) == ((right & 3) >> group)
    )
    side = 8 << group
    count = (side * side * width).astype(F32)
    spread = lax.dot_general(
        sums, same_group, (((1,), (0,)), ((), ())), precision=HIGH, preferred_element_type=F32
    )
    total = lax.dot_general(
        same_image.astype(F32), spread, (((1,), (0,)), ((), ())), precision=HIGH, preferred_element_type=F32
    )
    return total / count


def tile_rows(block):
    return jnp.sum(block.reshape(4, 8, C), axis=1)


def spread_rows(ref, tiles):
    for ty in range(4):
        for tx in range(4):
            t = 4 * ty + tx
            ref[ty, 8 * tx : 8 * tx + 8, :] = jnp.broadcast_to(tiles[t : t + 1, :], (8, C))


def norm_stats(x_ref, group, mean_ref, rstd_ref):
    parts = []
    for ty in range(4):
        acc = x_ref[pl.ds(ty * 256, 32), :]
        for y in range(1, 8):
            acc = acc + x_ref[pl.ds(ty * 256 + y * 32, 32), :]
        parts.append(tile_rows(acc))
    spread_rows(mean_ref, image_mean(jnp.concatenate(parts, axis=0), group))
    parts = []
    for ty in range(4):
        mu = mean_ref[ty]
        acc = jnp.zeros((32, C), F32)
        for y in range(8):
            cen = x_ref[pl.ds(ty * 256 + y * 32, 32), :] - mu
            acc = acc + cen * cen
        parts.append(tile_rows(acc))
    var = image_mean(jnp.concatenate(parts, axis=0), group)
    spread_rows(rstd_ref, lax.rsqrt(var + 1e-05))


def store_shifts(ref, y, val, side):
    x = lax.broadcasted_iota(jnp.int32, (32, C), 0) & (side - 1)
    zero = jnp.zeros((32, C), F32)
    left = jnp.where(x != 0, pltpu.roll(val, 1, 0), zero)
    right = jnp.where(x != side - 1, pltpu.roll(val, 31, 0), zero)
    rows = pl.ds(pl.multiple_of(PAD + y * 32, 32), 32)
    ref[rows, 0:C] = left.astype(BF16)
    ref[rows, C : 2 * C] = val.astype(BF16)
    ref[rows, 2 * C : 3 * C] = right.astype(BF16)


def clear_pads(ref):
    ref[0:PAD, :] = jnp.zeros((PAD, 3 * C), BF16)
    ref[PAD + ROWS : 2 * PAD + ROWS, :] = jnp.zeros((PAD, 3 * C), BF16)


def row_mask(shape, dim, dy, side):
    y = (lax.broadcasted_iota(jnp.int32, shape, dim) // 32) & (side - 1)
    return y != 0 if dy < 0 else y != side - 1


SHARD = 64
RES = (("mat", 0, 1152),)
MIX = (("mat", 0, 512), ("mat", 512, 512), ("lat", 1024, 128))


def part_shapes(kind, lanes, z_size, dtype):
    rows = 2 * SHARD * z_size
    if kind == "mat":
        return [((rows, 4 * lanes), dtype)]
    if kind == "lat":
        return [((rows // 2, 4 * lanes), dtype)] * 2
    return [((4, rows, lanes), dtype)]


def part_blocks(kind, refs, lanes, dp, f):
    cols = pl.ds(pl.multiple_of(f * lanes, 128), lanes)
    if kind == "lat":
        half = SHARD // 2
        at = pl.ds(pl.multiple_of(dp * half, half), half)
        return [(pl.ds(i * half, half), refs[i].at[at, cols]) for i in range(2)]
    at = pl.ds(pl.multiple_of(dp * SHARD, SHARD), SHARD)
    where = refs[0].at[at, cols] if kind == "mat" else refs[0].at[f, at, :]
    return [(pl.ds(0, SHARD), where)]


def part_count(kind):
    return 2 if kind == "lat" else 1


def copy_count(parts, z_size):
    return 8 * z_size * sum(part_count(kind) for kind, _, _ in parts)


def block_copies(parts, info_ref, pieces, wholes, sems, inward):
    core, f, my_z = info_ref[1], info_ref[2], info_ref[3]
    z_size = pieces[0].shape[0] // 4
    copies = []
    for side in range(2):
        owner = core if side == 0 else 1 - core
        for far in range(2):
            for near in range(2):
                for z in range(z_size):
                    at_f = f ^ ((2 - owner) * near) ^ ((1 + owner) * far)
                    at_dp = 2 * (z if inward else my_z ^ z) + owner
                    first = 0
                    for kind, lane, lanes in parts:
                        refs = wholes[first : first + part_count(kind)]
                        for rows, where in part_blocks(kind, refs, lanes, at_dp, at_f):
                            piece = pieces[side].at[(2 * far + near) * z_size + z, rows, pl.ds(lane, lanes)]
                            ends = (piece, where) if inward else (where, piece)
                            copies.append(pltpu.make_async_copy(*ends, sems.at[len(copies)]))
                        first += part_count(kind)
    return copies


def weight_copies(info_ref, refs, dst_ref, sems):
    if len(refs) == 1:
        return [pltpu.make_async_copy(refs[0], dst_ref, sems.at[0])]
    return block_copies(RES, info_ref, refs, (dst_ref,), sems, True)


def weight_sems(weight):
    return pltpu.SemaphoreType.DMA((1 if len(weight) == 1 else copy_count(RES, weight[0].shape[0] // 4),))


def conv_fwd_kernel(n_weight, has_res, info_ref, x_ref, gain_ref, *rest):
    weight, rest = rest[:n_weight], rest[n_weight:]
    if has_res:
        res_ref, *rest = rest
    t_ref, a3_ref, wt_ref, mean_ref, rstd_ref, sems = rest
    copies = weight_copies(info_ref, weight, wt_ref, sems)
    for copy in copies:
        copy.start()
    group = info_ref[0]
    side = 8 << group
    norm_stats(x_ref, group, mean_ref, rstd_ref)
    clear_pads(a3_ref)
    gamma = gain_ref[0:1, :]
    beta = gain_ref[1:2, :]

    def body(y, carry):
        ty = y // 8
        v = (x_ref[pl.ds(pl.multiple_of(y * 32, 32), 32), :] - mean_ref[ty]) * rstd_ref[ty] * gamma + beta
        store_shifts(a3_ref, y, v * sigmoid(v), side)
        return carry

    lax.fori_loop(0, 32, body, 0, unroll=2)
    for copy in copies:
        copy.wait()
    out = nt(a3_ref[PAD : PAD + ROWS, :], wt_ref[:, 3 * C : 6 * C])
    if has_res:
        out = out + res_ref[...]
    t_ref[...] = out
    for dy in (-1, 1):
        part = nt(a3_ref[PAD + 32 * dy : PAD + 32 * dy + ROWS, :], wt_ref[:, (dy + 1) * 3 * C : (dy + 2) * 3 * C])
        t_ref[...] += jnp.where(row_mask((ROWS, 1), 0, dy, side), part, 0.0)


SMEM = pl.BlockSpec(memory_space=pltpu.SMEM)
VM = pl.BlockSpec(memory_space=pltpu.VMEM)
ANY = pl.BlockSpec(memory_space=pl.ANY)
PARAMS = pltpu.CompilerParams(vmem_limit_bytes=VMEM_LIMIT)
CONV_FLOPS = 2 * ROWS * 9 * C * C


def cost(flops, size):
    return pl.CostEstimate(flops=flops, bytes_accessed=size, transcendentals=0)


def conv_fwd(info, x, gains, weight, res=None):
    args = [info, x, gains, *weight] + ([] if res is None else [res])
    return pl.pallas_call(
        functools.partial(conv_fwd_kernel, len(weight), res is not None),
        out_shape=(
            jax.ShapeDtypeStruct((ROWS, C), F32),
            jax.ShapeDtypeStruct((ROWS + 2 * PAD, 3 * C), BF16),
        ),
        in_specs=[SMEM, VM, VM] + [ANY] * len(weight) + ([] if res is None else [VM]),
        out_specs=(VM, VM),
        scratch_shapes=[
            pltpu.VMEM((C, 9 * C), BF16),
            pltpu.VMEM((4, 32, C), F32),
            pltpu.VMEM((4, 32, C), F32),
            weight_sems(weight),
        ],
        compiler_params=PARAMS,
        cost_estimate=cost(2 * CONV_FLOPS, 12 << 20),
        name="conv_fwd",
    )(*args)


def conv_dw_kernel(split, info_ref, dt_ref, a3_ref, *rest):
    if split:
        keep_ref, send_ref, dw_ref, dtt_ref, sems = rest
    else:
        dw_ref, dtt_ref = rest
    side = 8 << info_ref[0]
    dtt_ref[1] = dt_ref[...].astype(F32).T.astype(BF16)
    flat = dtt_ref[1]
    for dy in (-1, 1):
        keep = row_mask((1, ROWS), 1, dy, side).astype(BF16)
        dtt_ref[dy + 1] = flat * keep
    for dy in (-1, 0, 1):
        dw = nn(dtt_ref[dy + 1], a3_ref[PAD + 32 * dy : PAD + 32 * dy + ROWS, :])
        dw_ref[:, (dy + 1) * 3 * C : (dy + 2) * 3 * C] = dw.astype(dw_ref.dtype)
    if split:
        copies = block_copies(RES, info_ref, (keep_ref, send_ref), (dw_ref,), sems, False)
        for copy in copies:
            copy.start()
        for copy in copies:
            copy.wait()


def conv_dw(info, dt, a3, z_size):
    scratch = [pltpu.VMEM((3, C, ROWS), BF16)]
    if z_size:
        block = jax.ShapeDtypeStruct((4 * z_size, SHARD, 9 * C // 4), BF16)
        shapes, specs = (block, block), (ANY, ANY)
        scratch = [pltpu.VMEM((C, 9 * C), BF16)] + scratch + [pltpu.SemaphoreType.DMA((copy_count(RES, z_size),))]
    else:
        shapes, specs = jax.ShapeDtypeStruct((C, 9 * C), F32), VM
    return pl.pallas_call(
        functools.partial(conv_dw_kernel, z_size),
        out_shape=shapes,
        in_specs=[SMEM, VM, VM],
        out_specs=specs,
        scratch_shapes=scratch,
        compiler_params=PARAMS,
        cost_estimate=cost(2 * CONV_FLOPS, 12 << 20),
        name="conv_dw",
    )(info, dt, a3)


def conv_dx_kernel(n_weight, has_res, info_ref, dt_ref, x_ref, gain_ref, *rest):
    weight, rest = rest[:n_weight], rest[n_weight:]
    if has_res:
        res_ref, *rest = rest
    dx_ref, dgain_ref, wt_ref, d3_ref, mean_ref, rstd_ref, ds_ref, sems = rest
    copies = weight_copies(info_ref, weight, wt_ref, sems)
    for copy in copies:
        copy.start()
    group = info_ref[0]
    side = 8 << group
    clear_pads(d3_ref)

    def body(y, carry):
        val = dt_ref[pl.ds(pl.multiple_of(y * 32, 32), 32), :].astype(F32)
        store_shifts(d3_ref, y, val, side)
        return carry

    lax.fori_loop(0, 32, body, 0, unroll=2)
    norm_stats(x_ref, group, mean_ref, rstd_ref)
    for copy in copies:
        copy.wait()
    for dy in (0, -1, 1):
        part = None
        for dx in (-1, 0, 1):
            t = 3 * (dy + 1) + dx + 1
            one = nn(
                d3_ref[PAD - 32 * dy : PAD - 32 * dy + ROWS, (1 - dx) * C : (2 - dx) * C],
                wt_ref[:, t * C : (t + 1) * C],
            )
            part = one if part is None else part + one
        if dy == 0:
            ds_ref[...] = part
        else:
            ds_ref[...] += jnp.where(row_mask((ROWS, 1), 0, -dy, side), part, 0.0)
    gamma = gain_ref[0:1, :]
    beta = gain_ref[1:2, :]
    first, second = [], []
    for ty in range(4):
        mu, rs = mean_ref[ty], rstd_ref[ty]

        def step(y, carry, ty=ty, mu=mu, rs=rs):
            one, two = carry
            rows = pl.ds(pl.multiple_of(ty * 256 + y * 32, 32), 32)
            xh = (x_ref[rows, :] - mu) * rs
            v = xh * gamma + beta
            sg = sigmoid(v)
            ds = ds_ref[rows, :] * (sg * (1.0 + v * (1.0 - sg)))
            ds_ref[rows, :] = ds
            return (one + ds, two + ds * xh)

        zero = jnp.zeros((32, C), F32)
        one, two = lax.fori_loop(0, 8, step, (zero, zero))
        first.append(tile_rows(one))
        second.append(tile_rows(two))
    first = jnp.concatenate(first, axis=0)
    second = jnp.concatenate(second, axis=0)
    dgain_ref[0:1, :] = jnp.sum(second, axis=0, keepdims=True)
    dgain_ref[1:2, :] = jnp.sum(first, axis=0, keepdims=True)
    m_one = image_mean(first * gamma, group)
    m_two = image_mean(second * gamma, group)
    for ty in range(4):
        mu, rs = mean_ref[ty], rstd_ref[ty]
        one = jnp.concatenate([jnp.broadcast_to(m_one[4 * ty + tx : 4 * ty + tx + 1, :], (8, C)) for tx in range(4)], axis=0)
        two = jnp.concatenate([jnp.broadcast_to(m_two[4 * ty + tx : 4 * ty + tx + 1, :], (8, C)) for tx in range(4)], axis=0)

        def step(y, carry, ty=ty, mu=mu, rs=rs, one=one, two=two):
            rows = pl.ds(pl.multiple_of(ty * 256 + y * 32, 32), 32)
            xh = (x_ref[rows, :] - mu) * rs
            dx = rs * (ds_ref[rows, :] * gamma - one - xh * two)
            if has_res:
                dx = dx + res_ref[rows, :]
            dx_ref[rows, :] = dx.astype(dx_ref.dtype)
            return carry

        lax.fori_loop(0, 8, step, 0)


def conv_dx(info, dt, x, gains, weight, res=None, low=True):
    args = [info, dt, x, gains, *weight] + ([] if res is None else [res])
    return pl.pallas_call(
        functools.partial(conv_dx_kernel, len(weight), res is not None),
        out_shape=(
            jax.ShapeDtypeStruct((ROWS, C), BF16 if low else F32),
            jax.ShapeDtypeStruct((2, C), F32),
        ),
        in_specs=[SMEM, VM, VM, VM] + [ANY] * len(weight) + ([] if res is None else [VM]),
        out_specs=(VM, VM),
        scratch_shapes=[
            pltpu.VMEM((C, 9 * C), BF16),
            pltpu.VMEM((ROWS + 2 * PAD, 3 * C), BF16),
            pltpu.VMEM((4, 32, C), F32),
            pltpu.VMEM((4, 32, C), F32),
            pltpu.VMEM((ROWS, C), F32),
            weight_sems(weight),
        ],
        compiler_params=PARAMS,
        cost_estimate=cost(3 * CONV_FLOPS, 12 << 20),
        name="conv_dx",
    )(*args)


def silu_slope(value):
    gate = sigmoid(value)
    return gate * (1.0 + value * (1.0 - gate))


def transposed(value):
    return value.astype(F32).T.astype(BF16)


HALF = SIDE // 2
LAT = HALF * HALF


def to_depth(src_ref, lanes_ref, dst_ref):
    for k in range(C // 128):
        lanes_ref[k] = src_ref[:, k * 128 : (k + 1) * 128]
    for k in range(C // 128):
        for b in range(2):
            block = lanes_ref[k, pl.ds(b, ROWS // 2, stride=2), :].reshape(HALF, 2, HALF, 128)
            for a in range(2):
                at = (2 * a + b) * C + k * 128
                dst_ref[:, at : at + 128] = block[:, a].reshape(LAT, 128).astype(dst_ref.dtype)


def from_depth(src_ref, lanes_ref, dst_ref):
    for k in range(C // 128):
        for b in range(2):
            pair = [
                src_ref[:, (2 * a + b) * C + k * 128 : (2 * a + b) * C + (k + 1) * 128].reshape(HALF, 1, HALF, 128)
                for a in range(2)
            ]
            lanes_ref[k, pl.ds(b, ROWS // 2, stride=2), :] = jnp.concatenate(pair, axis=1).reshape(ROWS // 2, 128)
    for k in range(C // 128):
        dst_ref[:, k * 128 : (k + 1) * 128] = lanes_ref[k]


def mid_fwd_kernel(
    h_ref, ws0_ref, wl0_ref, code_ref, wl1_ref, ws1_ref,
    e_ref, d_ref, s_ref, q_ref, y_ref, s2_ref, g_ref, commit_ref, dcom_ref, resid_ref, u_ref, lanes_ref,
):
    to_depth(h_ref, lanes_ref, e_ref)
    d = nt(e_ref[...], ws0_ref[...])
    d_ref[...] = d
    s = (d * sigmoid(d)).astype(BF16)
    s_ref[...] = s
    z = nt(s, wl0_ref[...])
    q = jnp.zeros((LAT, ZD), F32)
    commit = jnp.zeros((LAT, ZD), F32)
    dcom = jnp.zeros((LAT, ZD), F32)
    for k in range(4):
        resid_ref[k * LAT : (k + 1) * LAT, :] = (z - q).astype(BF16)
        q = q + code_ref[k * LAT : (k + 1) * LAT, :].astype(F32)
        diff = z - q
        commit = commit + diff * diff
        dcom = dcom + diff
    commit_ref[...] = jnp.sum(commit, axis=0, keepdims=True)
    dcom_ref[...] = dcom
    quant = (z + (q - z)).astype(BF16)
    q_ref[...] = quant
    y = nn(quant, wl1_ref[...])
    y_ref[...] = y
    s2 = (y * sigmoid(y)).astype(BF16)
    s2_ref[...] = s2
    u_ref[...] = nn(s2, ws1_ref[...])
    from_depth(u_ref, lanes_ref, g_ref)


def mid_fwd(h, ws0, wl0, codes, wl1, ws1):
    shape = jax.ShapeDtypeStruct
    return pl.pallas_call(
        mid_fwd_kernel,
        out_shape=(
            shape((LAT, 4 * C), BF16),
            shape((LAT, C), F32),
            shape((LAT, C), BF16),
            shape((LAT, ZD), BF16),
            shape((LAT, C), F32),
            shape((LAT, C), BF16),
            shape((ROWS, C), F32),
            shape((1, ZD), F32),
            shape((LAT, ZD), F32),
            shape((4 * LAT, ZD), BF16),
        ),
        in_specs=[VM] * 6,
        out_specs=(VM,) * 10,
        scratch_shapes=[pltpu.VMEM((LAT, 4 * C), F32), pltpu.VMEM((C // 128, ROWS, 128), F32)],
        compiler_params=PARAMS,
        cost_estimate=cost(4 << 30, 12 << 20),
        name="mid_fwd",
    )(h, ws0, wl0, codes, wl1, ws1)


def mid_bwd_kernel(
    split, scale, info_ref, dg_ref, e_ref, d_ref, s_ref, q_ref, y_ref, s2_ref, dcom_ref, ws0_ref, wl0_ref, wl1_ref,
    ws1_ref, *rest,
):
    if split:
        keep_ref, send_ref, dh_ref, *wholes, du_ref, de_ref, lanes_ref, sems = rest
    else:
        *wholes, dh_ref, du_ref, de_ref, lanes_ref = rest
    dws0_ref, dws1_ref, dwl0_ref, dwl1_ref = wholes
    to_depth(dg_ref, lanes_ref, du_ref)
    out = dws0_ref.dtype
    ds2 = nt(du_ref[...], ws1_ref[...])
    dy = (ds2 * silu_slope(y_ref[...])).astype(BF16)
    dws1_ref[...] = nn(transposed(s2_ref[...]), du_ref[...]).astype(out)
    dwl1_ref[...] = nn(transposed(q_ref[...]), dy).astype(out)
    dz = (nt(dy, wl1_ref[...]) + scale * dcom_ref[...]).astype(BF16)
    dwl0_ref[...] = nn(transposed(dz), s_ref[...]).astype(out)
    ds = nn(dz, wl0_ref[...])
    dd = (ds * silu_slope(d_ref[...])).astype(BF16)
    dws0_ref[...] = nn(transposed(dd), e_ref[...]).astype(out)
    copies = []
    if split:
        copies = block_copies(MIX, info_ref, (keep_ref, send_ref), wholes, sems, False)
    for copy in copies:
        copy.start()
    de_ref[...] = nn(dd, ws0_ref[...])
    from_depth(de_ref, lanes_ref, dh_ref)
    for copy in copies:
        copy.wait()


def mid_bwd(info, scale, dg, e, d, s, q, y, s2, dcom, ws0, wl0, wl1, ws1, z_size):
    shape = jax.ShapeDtypeStruct
    wholes = [(C, 4 * C), (C, 4 * C), (ZD, C), (ZD, C)]
    scratch = [
        pltpu.VMEM((LAT, 4 * C), BF16),
        pltpu.VMEM((LAT, 4 * C), F32),
        pltpu.VMEM((C // 128, ROWS, 128), F32),
    ]
    field = shape((ROWS, C), F32)
    if z_size:
        block = shape((4 * z_size, SHARD, 1152), BF16)
        shapes, specs = (block, block, field), (ANY, ANY, VM)
        scratch = [pltpu.VMEM(one, BF16) for one in wholes] + scratch
        scratch += [pltpu.SemaphoreType.DMA((copy_count(MIX, z_size),))]
    else:
        shapes, specs = tuple(shape(one, F32) for one in wholes) + (field,), (VM,) * 5
    out = pl.pallas_call(
        functools.partial(mid_bwd_kernel, z_size, scale),
        out_shape=shapes,
        in_specs=[SMEM] + [VM] * 12,
        out_specs=specs,
        scratch_shapes=scratch,
        compiler_params=PARAMS,
        cost_estimate=cost(4 << 30, 12 << 20),
        name="mid_bwd",
    )(info, dg, e, d, s, q, y, s2, dcom, ws0, wl0, wl1, ws1)
    return out[-1], out[:-1]


def head_kernel(total_ref, g_ref, wp_ref, pix_ref, mask_ref, dw_ref, dg_ref, loss_ref, o_ref, dr_ref):
    inv = total_ref[0]
    loss = jnp.zeros((1, pix_ref.shape[1]), F32)
    for i in range(4):
        rows = pl.ds(i * 256, 256)
        g = g_ref[rows, :]
        gate = sigmoid(g)
        o = (g * gate).astype(BF16)
        o_ref[rows, :] = o
        err = nn(o, wp_ref[...]) - pix_ref[rows, :].astype(F32)
        keep = mask_ref[rows, :].astype(F32)
        smooth = jnp.sqrt(err * err + 1.0)
        loss = loss + jnp.sum(keep * (smooth - 1.0), axis=0, keepdims=True)
        dr = (keep * err / smooth / inv).astype(BF16)
        dr_ref[rows, :] = dr
        do = nt(dr, wp_ref[...])
        dg_ref[rows, :] = do * (gate * (1.0 + g * (1.0 - gate)))
    loss_ref[...] = loss
    dw_ref[...] = nn(transposed(o_ref[...]), dr_ref[...]).astype(dw_ref.dtype)


def head(total, g, wp, pix, mask, grad_type=BF16):
    shape = jax.ShapeDtypeStruct
    width = pix.shape[1]
    return pl.pallas_call(
        head_kernel,
        out_shape=(shape((C, width), grad_type), shape((ROWS, C), F32), shape((1, width), F32)),
        in_specs=[SMEM, VM, VM, VM, VM],
        out_specs=(VM,) * 3,
        scratch_shapes=[pltpu.VMEM((ROWS, C), BF16), pltpu.VMEM((ROWS, width), BF16)],
        compiler_params=PARAMS,
        cost_estimate=cost(6 << 30, 12 << 20),
        name="head",
    )(total, g, wp, pix, mask)


BOTH = ("z", "core", "fsdp")
COLS = ("z", "core")


def swap(shard):
    return jnp.swapaxes(shard, -1, -2).astype(BF16)


def across(x, near):
    n = lax.axis_size("fsdp")
    masks = (2, 1) if near else (1, 2)
    return lax.ppermute(x, ("core", "fsdp"), [(c * n + f, c * n + (f ^ masks[c])) for c in range(2) for f in range(n)])


def partner(x):
    return lax.ppermute(x, "core", [(0, 1), (1, 0)])


def everyone(x):
    n = lax.axis_size("z") * lax.axis_size("core") * lax.axis_size("fsdp")
    return lax.all_to_all(jnp.broadcast_to(x[None], (n,) + x.shape), BOTH, 0, 0, tiled=True)


def along_z(x, step):
    n = lax.axis_size("z")
    return lax.ppermute(x, "z", [(i, i ^ step) for i in range(n)])


def shuffle(x, axis):
    return lax.all_to_all(x, axis, 0, 0, tiled=True)


def assemble_kernel(parts, info_ref, own, other, *rest):
    copies = block_copies(parts, info_ref, (own, other), rest[:-1], rest[-1], True)
    for copy in copies:
        copy.start()
    for copy in copies:
        copy.wait()


def assemble(info, pieces, parts):
    z_size = pieces[0].shape[0] // 4
    shapes = [s for kind, _, lanes in parts for s in part_shapes(kind, lanes, z_size, BF16)]
    return pl.pallas_call(
        functools.partial(assemble_kernel, parts),
        out_shape=tuple(jax.ShapeDtypeStruct(*s) for s in shapes),
        in_specs=[SMEM] + [ANY] * 2,
        out_specs=(VM,) * len(shapes),
        scratch_shapes=[pltpu.SemaphoreType.DMA((copy_count(parts, z_size),))],
        compiler_params=PARAMS,
        cost_estimate=cost(1 << 30, 10 << 20),
        name="assemble",
    )(info, *pieces)


def gather_all(shards, others):
    z_size = lax.axis_size("z")
    count = len(shards)
    shards = list(shards)
    z_done, near_done, far_done, pieces, side = {}, {}, {}, {}, {}
    for step in range(max([count + 2] + list(others)) + 1):
        new = {}
        if step < count:
            new["z"] = shuffle(jnp.broadcast_to(shards[step][None], (z_size,) + shards[step].shape), "z")
        if 0 <= step - 1 < count:
            new["near"] = across(z_done[step - 1], True)
        if 0 <= step - 2 < count:
            new["far"] = across(near_done[step - 2], False)
        if 0 <= step - 3 < count:
            new["core"] = partner(far_done[step - 3])
        if step in others:
            side = {**side, **others[step](pieces, side)}
        new, shards[step + 1 :], side = lax.optimization_barrier((new, shards[step + 1 :], side))
        if "z" in new:
            z_done[step] = new["z"]
        if "near" in new:
            near_done[step - 1] = jnp.concatenate([z_done[step - 1], new["near"]])
        if "far" in new:
            far_done[step - 2] = jnp.concatenate([near_done[step - 2], new["far"]])
        if "core" in new:
            pieces[step - 3] = (far_done[step - 3], new["core"])
    return pieces, side


def add_up(parts):
    total = parts[0].astype(F32)
    for part in parts[1:]:
        total = total + part.astype(F32)
    return total


def scatter_stages(keep, send, out):
    half = keep.shape[0] // 2
    keep, got = yield keep, partner(send)
    parts = [keep, got]
    for near in (False, True):
        *parts, got = yield *parts, across(add_up([p[half : 2 * half] for p in parts]).astype(BF16), near)
        parts.append(got)
        half = half // 2
    away = [along_z(add_up([p[k] for p in parts]).astype(BF16), k) for k in range(1, 2 * half)]
    *both, = yield *parts, *away
    out.append(add_up([p[0] for p in both[: len(parts)]] + both[len(parts) :]))


def scatter_direct(blocks, out):
    got = yield shuffle(blocks, BOTH)
    out.append(jnp.sum(got.astype(F32), axis=0))


class Overlap:
    def __init__(self):
        self.live = []

    def add(self, stages, *args, late=0):
        out = []
        stages = stages(*args, out)
        self.live.append((stages, next(stages), late))
        return out

    def step(self, values):
        due = [value for _, value, late in self.live if not late]
        values, due = lax.optimization_barrier((values, due))
        live, at = [], 0
        for stages, value, late in self.live:
            if late:
                live.append((stages, value, late - 1))
                continue
            try:
                live.append((stages, stages.send(due[at]), 0))
            except StopIteration:
                pass
            at += 1
        self.live = live
        return values


def fetch_whole(shard):
    cols = lax.all_gather(shard.astype(BF16), COLS, axis=1, tiled=True)
    return jnp.swapaxes(lax.all_gather(cols, "fsdp", axis=0, tiled=True), 0, 1)


def reduce_whole(grad):
    rows = lax.psum_scatter(jnp.swapaxes(grad, 0, 1), "fsdp", scatter_dimension=0, tiled=True)
    return jnp.swapaxes(lax.psum_scatter(rows, COLS, scatter_dimension=1, tiled=True), 0, 1)


def widen(block, width):
    return jnp.pad(block, ((0, 0),) * (block.ndim - 1) + ((0, width - block.shape[-1]),))


def pix_matrix(blocks, width):
    return blocks[:, :, :width].transpose(1, 0, 2).reshape(C, 4 * width)


def pix_blocks(matrix, shard):
    rows, cols = shard
    return matrix.reshape(-1, cols, matrix.shape[1] // rows, rows).transpose(0, 2, 1, 3).reshape(-1, cols, rows)


def adam_step(weight, moment, second, grad, rate):
    moment_new = 0.5 * moment + 0.5 * grad
    second_new = 0.5 * second + 0.5 * grad * grad
    fix = 1.0 - 0.5**STEP
    weight_new = weight - rate * (
        moment_new / fix / (jnp.sqrt(second_new / fix) + 1e-12) + 0.01 * weight
    )
    return (weight_new, moment_new, second_new)


def exact(left, right, dims):
    return lax.dot_general(left, right, (dims, ((), ())), preferred_element_type=F32)


def code_slots(codes, devices, capacity, rows):
    n = codes.shape[0]
    owner = codes // rows
    hot = (owner[:, None] == jnp.arange(devices, dtype=jnp.int32)[None, :]).astype(BF16)
    at = jnp.arange(n, dtype=jnp.int32)
    before = (at[None, :] < at[:, None]).astype(BF16)
    rank = exact(before, hot, ((1,), (0,)))
    place = jnp.sum(rank * hot.astype(F32), axis=1).astype(jnp.int32)
    slot = owner * capacity + place
    return (jnp.arange(devices * capacity, dtype=jnp.int32)[:, None] == slot[None, :]).astype(BF16)


def on_device(
    pixels,
    valid_mask,
    size_groups,
    code_index,
    w_pixel,
    w_res,
    w_scale,
    w_latent,
    norm_gains,
    moment_pixel,
    moment_res,
    moment_scale,
    moment_latent,
    moment_gains,
    second_pixel,
    second_res,
    second_scale,
    second_latent,
    second_gains,
    ema_counts,
    ema_sums,
):
    n_inner = lax.axis_size("fsdp")
    z_size = lax.axis_size("z")
    devices = 2 * z_size * n_inner
    latent_all = code_index.shape[1] * devices
    rows = ema_sums.shape[0]
    paired = n_inner == 4 and w_res.shape[1] == 1152 and w_res.shape[2] == SHARD
    blocks = z_size if paired else 0
    place = [lax.axis_index("core"), lax.axis_index("fsdp"), lax.axis_index("z")]
    info = jnp.stack([size_groups[0]] + [one.astype(jnp.int32) for one in place])

    codes = code_index.reshape(-1)
    capacity = max(2, 2 * codes.shape[0] // devices)
    pick = code_slots(codes, devices, capacity, rows)
    local = codes % rows
    cols = jnp.stack([local // 16, local % 16, jnp.ones_like(local)], axis=1).astype(BF16)
    want = exact(pick, cols, ((1,), (0,)))
    wanted = jnp.where(want[:, 2] > 0.5, want[:, 0] * 16.0 + want[:, 1], -1.0).astype(jnp.int32)
    book = (ema_sums / ema_counts[:, None]).astype(BF16)
    valid = jnp.sum(valid_mask.astype(F32).reshape(-1, 128), axis=0, keepdims=True)

    def row_hot(asked):
        return (asked[:, None] == jnp.arange(rows, dtype=jnp.int32)[None, :]).astype(BF16)

    def ask(pieces, side):
        wide = -(-capacity // 128) * 128
        request = widen(wanted.astype(F32).reshape(devices, 1, capacity), wide)
        count = jnp.broadcast_to(widen(valid, wide)[None], (devices, 1, wide))
        got = shuffle(jnp.concatenate([request, count], axis=1), BOTH)
        return {"asked": got[:, 0, :capacity].reshape(-1).astype(jnp.int32), "count": jnp.sum(got[:, 1])}

    def reply(pieces, side):
        answer = exact(row_hot(side["asked"]), book, ((1,), (0,))).astype(BF16)
        return {"replies": shuffle(answer.reshape(devices, capacity, ZD), BOTH)}

    gains = [jnp.stack([norm_gains[j], norm_gains[4 + j]]) for j in range(4)]
    width = w_pixel.shape[1]

    def run_conv0(pieces, side):
        if paired:
            (pix,) = assemble(info, pieces[0], (("pix", RES[0][2], 256),))
            h0 = nt(pixels, pix_matrix(pix, width))
            weight = pieces[0]
        else:
            h0 = nt(pixels, fetch_whole(w_pixel[0]))
            weight = (fetch_whole(w_res[0]),)
        t1, a1 = conv_fwd(info, h0, gains[0], weight)
        return {"h0": h0, "t1": t1, "a1": a1, "res0": weight}

    def run_conv1(pieces, side):
        weight = pieces[1] if paired else (fetch_whole(w_res[1]),)
        h1, a2 = conv_fwd(info, side["t1"], gains[1], weight, side["h0"])
        return {"h1": h1, "a2": a2, "res1": weight, **reply(pieces, side)}

    def run_mid(pieces, side):
        if paired:
            mats = assemble(info, pieces[2], MIX)
        else:
            mats = [fetch_whole(w_scale[i]) for i in range(2)] + [fetch_whole(w_latent[i]) for i in range(2)]
        scale0, scale1, lat0, lat1 = mats
        picked = exact(pick, side["replies"].reshape(-1, ZD), ((0,), (0,))).astype(BF16)
        return {"mid": mid_fwd(side["h1"], scale0, lat0, picked, lat1, scale1), "mats": mats}

    def run_conv2(pieces, side):
        weight = pieces[3] if paired else (fetch_whole(w_res[2]),)
        t3, a3 = conv_fwd(info, side["mid"][6], gains[2], weight)
        return {"t3": t3, "a3": a3, "res2": weight}

    def run_conv3(pieces, side):
        sent = exact(pick, side["mid"][9], ((1,), (0,))).astype(BF16)
        held = shuffle(sent.reshape(devices, capacity, ZD), BOTH)
        if paired:
            (pix,) = assemble(info, pieces[4], (("pix", RES[0][2], 256),))
            pix = pix_matrix(pix, width)
            weight = pieces[4]
        else:
            pix, weight = fetch_whole(w_pixel[1]), (fetch_whole(w_res[3]),)
        g1, a4 = conv_fwd(info, side["t3"], gains[3], weight, side["mid"][6])
        out = BF16 if paired else F32
        d_head, dg1, loss = head(side["count"].reshape(1), g1, pix, pixels, valid_mask, out)
        return {"held": held, "a4": a4, "res3": weight, "d_head": d_head, "dg1": dg1, "loss": loss}

    others = {2: ask, 4: run_conv0, 5: run_conv1, 6: run_mid, 7: run_conv2, 8: run_conv3}
    shards = []
    if paired:
        res_t, pix_t, scale_t, lat_t = swap(w_res), swap(w_pixel), swap(w_scale), swap(w_latent)
        mix = jnp.concatenate([scale_t[0], scale_t[1], lat_t.reshape(-1, lat_t.shape[2])], axis=1)
        first, last = [jnp.concatenate([res_t[3 * i], widen(pix_t[i], 256)], axis=1) for i in range(2)]
        shards = [first, res_t[1], mix, res_t[2], last]
    _, side = gather_all(shards, others)
    total_valid = side["count"]
    e, d, s, quant, y, s2, g0, commit, dcom, _ = side["mid"]
    h0, t1, a1, h1, a2, t3, a3, a4 = [side[name] for name in ("h0", "t1", "a1", "h1", "a2", "t3", "a3", "a4")]
    res_w = [side["res0"], side["res1"], side["res2"], side["res3"]]
    scale0, scale1, lat0, lat1 = side["mats"]
    d_head, dg1, loss = side["d_head"], side["dg1"], side["loss"]

    hot_rows = row_hot(side["asked"])
    held = side["held"].reshape(-1, ZD)
    my_sums = exact(hot_rows, held, ((0,), (0,)))
    my_counts = jnp.sum(hot_rows.astype(F32), axis=0)
    counts_new = EMA_DECAY * ema_counts + (1.0 - EMA_DECAY) * my_counts
    sums_new = EMA_DECAY * ema_sums + (1.0 - EMA_DECAY) * my_sums
    book_new = sums_new / counts_new[:, None]

    scale = 2.0 * COMMIT_WEIGHT / (latent_all * ZD)
    if paired:
        overlap = Overlap()
        shard = w_pixel.shape[1:]
        sum_head = overlap.add(scatter_direct, pix_blocks(d_head, shard), late=1)
        dw, dg1 = overlap.step((conv_dw(info, dg1, a4, z_size), dg1))
        sum_res3 = overlap.add(scatter_stages, *dw)
        dt3, dn3 = overlap.step(conv_dx(info, dg1, t3, gains[3], res_w[3]))
        dw, dt3 = overlap.step((conv_dw(info, dt3, a3, z_size), dt3))
        sum_res2 = overlap.add(scatter_stages, *dw)
        dg0, dn2 = overlap.step(conv_dx(info, dt3, g0, gains[2], res_w[2], dg1, False))
        dh1, dw = overlap.step(
            mid_bwd(info, scale, dg0, e, d, s, quant, y, s2, dcom, scale0, lat0, lat1, scale1, z_size)
        )
        sum_mix = overlap.add(scatter_stages, *dw)
        dw, dh1 = overlap.step((conv_dw(info, dh1, a2, z_size), dh1))
        sum_res1 = overlap.add(scatter_stages, *dw)
        dt1, dn1 = overlap.step(conv_dx(info, dh1, t1, gains[1], res_w[1]))
        dw, dt1 = overlap.step((conv_dw(info, dt1, a1, z_size), dt1))
        sum_res0 = overlap.add(scatter_stages, *dw)
        dh0, dn0 = overlap.step(conv_dx(info, dt1, h0, gains[0], res_w[0], dh1))
        d_patch = exact(dh0, pixels, ((0,), (0,))).astype(BF16)
        d_patch = overlap.step(pix_blocks(d_patch, shard))
        sum_patch = overlap.add(scatter_direct, d_patch)
        overlap.step(())
        overlap.step(())
        grad_pixel = jnp.stack([sum_patch[0], sum_head[0]])
        grad_res = jnp.stack([sum_res0[0], sum_res1[0], sum_res2[0], sum_res3[0]])
        grad_scale = jnp.stack([sum_mix[0][:, :512], sum_mix[0][:, 512:1024]])
        grad_latent = sum_mix[0][:, 1024:].reshape(2, SHARD // 2, -1)
    else:
        d_res3 = conv_dw(info, dg1, a4, 0)
        dt3, dn3 = conv_dx(info, dg1, t3, gains[3], res_w[3])
        d_res2 = conv_dw(info, dt3, a3, 0)
        dg0, dn2 = conv_dx(info, dt3, g0, gains[2], res_w[2], dg1, False)
        dh1, (d_scale0, d_scale1, d_lat0, d_lat1) = mid_bwd(
            info, scale, dg0, e, d, s, quant, y, s2, dcom, scale0, lat0, lat1, scale1, 0
        )
        d_res1 = conv_dw(info, dh1, a2, 0)
        dt1, dn1 = conv_dx(info, dh1, t1, gains[1], res_w[1])
        d_res0 = conv_dw(info, dt1, a1, 0)
        dh0, dn0 = conv_dx(info, dt1, h0, gains[0], res_w[0], dh1)
        d_patch = exact(dh0, pixels, ((0,), (0,)))
        grad_pixel = jnp.stack([reduce_whole(g) for g in (d_patch, d_head)])
        grad_res = jnp.stack([reduce_whole(g) for g in (d_res0, d_res1, d_res2, d_res3)])
        grad_scale = jnp.stack([reduce_whole(g) for g in (d_scale0, d_scale1)])
        grad_latent = jnp.stack([reduce_whole(g) for g in (d_lat0, d_lat1)])

    gain_local = jnp.stack([dn0[0], dn1[0], dn2[0], dn3[0], dn0[1], dn1[1], dn2[1], dn3[1]])
    sums_local = jnp.concatenate(
        [
            gain_local.reshape(-1, 128),
            jnp.sum(loss.reshape(-1, 128), axis=0, keepdims=True),
            jnp.sum(commit.reshape(-1, 128), axis=0, keepdims=True),
        ]
    )
    sums_all = jnp.sum(everyone(sums_local), axis=0)
    grad_gains = sums_all[:-2].reshape(8, C)
    smooth_sum = jnp.sum(sums_all[-2])
    commit_sum = jnp.sum(sums_all[-1])

    squares = jnp.sum(grad_pixel * grad_pixel) + jnp.sum(grad_res * grad_res)
    squares = squares + jnp.sum(grad_scale * grad_scale) + jnp.sum(grad_latent * grad_latent)
    total_squares = jnp.sum(everyone(jnp.broadcast_to(squares, (1, 128)))[:, 0, 0]) + jnp.sum(grad_gains * grad_gains)
    norm = jnp.sqrt(total_squares)
    factor = CLIP_AT / jnp.maximum(norm, CLIP_AT)
    groups_all = [
        (w_pixel, moment_pixel, second_pixel, grad_pixel),
        (w_res, moment_res, second_res, grad_res),
        (w_scale, moment_scale, second_scale, grad_scale),
        (w_latent, moment_latent, second_latent, grad_latent),
    ]
    outputs = [jnp.stack([smooth_sum, total_valid, commit_sum]), norm.reshape(1)]
    for weight, moment, second, grad in groups_all:
        grad = jnp.swapaxes(grad * factor, 1, 2)
        weight_new, moment_new, second_new = adam_step(weight, moment, second, grad, WEIGHT_RATE)
        outputs += [weight_new, moment_new, second_new, weight_new.astype(BF16)]
    outputs += list(adam_step(norm_gains, moment_gains, second_gains, grad_gains * factor, GAIN_RATE))
    outputs += [counts_new, sums_new, book_new, book_new.astype(BF16)]
    return tuple(outputs)


def solution(mesh):
    outer, inner = mesh.shape["dp"], mesh.shape["fsdp"]
    fine = Mesh(mesh.devices.reshape(outer // 2, 2, inner), BOTH)
    placed = (
        P(BOTH, None),
        P(BOTH, None),
        P(BOTH),
        P(None, BOTH),
        P(None, "fsdp", COLS),
        P(None, "fsdp", COLS),
        P(None, "fsdp", COLS),
        P(None, "fsdp", COLS),
        P(),
        P(None, "fsdp", COLS),
        P(None, "fsdp", COLS),
        P(None, "fsdp", COLS),
        P(None, "fsdp", COLS),
        P(),
        P(None, "fsdp", COLS),
        P(None, "fsdp", COLS),
        P(None, "fsdp", COLS),
        P(None, "fsdp", COLS),
        P(),
        P(BOTH),
        P(BOTH, None),
    )
    return jax.shard_map(
        on_device,
        mesh=fine,
        in_specs=placed,
        out_specs=(
            P(),
            P(),
            P(None, "fsdp", COLS),
            P(None, "fsdp", COLS),
            P(None, "fsdp", COLS),
            P(None, "fsdp", COLS),
            P(None, "fsdp", COLS),
            P(None, "fsdp", COLS),
            P(None, "fsdp", COLS),
            P(None, "fsdp", COLS),
            P(None, "fsdp", COLS),
            P(None, "fsdp", COLS),
            P(None, "fsdp", COLS),
            P(None, "fsdp", COLS),
            P(None, "fsdp", COLS),
            P(None, "fsdp", COLS),
            P(None, "fsdp", COLS),
            P(None, "fsdp", COLS),
            P(),
            P(),
            P(),
            P(BOTH),
            P(BOTH, None),
            P(BOTH, None),
            P(BOTH, None),
        ),
        check_vma=False,
    )
```

```python
import functools
import jax
import jax.numpy as jnp
from jax import lax
from jax.experimental import pallas as pl
from jax.experimental.pallas import tpu as pltpu
from jax.sharding import Mesh
from jax.sharding import PartitionSpec as P

C = 512
ZD = 256
GROUPS = 32
SIDE = 32
STEP = 5
COMMIT_WEIGHT = 0.25
CLIP_AT = 1e-05
EMA_DECAY = 0.8
WEIGHT_RATE = 0.03
GAIN_RATE = 0.4
ROWS = SIDE * SIDE
PAD = SIDE
HIGH = lax.Precision.HIGHEST
F32 = jnp.float32
BF16 = jnp.bfloat16
VMEM_LIMIT = 60 * 1024 * 1024


def sigmoid(v):
    return 0.5 * jnp.tanh(0.5 * v) + 0.5


def nt(left, right):
    return lax.dot_general(left, right, (((1,), (1,)), ((), ())), preferred_element_type=F32)


def nn(left, right):
    return lax.dot_general(left, right, (((1,), (0,)), ((), ())), preferred_element_type=F32)


def image_mean(sums, group):
    width = C // GROUPS
    row = lax.broadcasted_iota(jnp.int32, (C, C), 0) // width
    col = lax.broadcasted_iota(jnp.int32, (C, C), 1) // width
    same_group = (row == col).astype(F32)
    left = lax.broadcasted_iota(jnp.int32, (16, 16), 0)
    right = lax.broadcasted_iota(jnp.int32, (16, 16), 1)
    same_image = (((left >> 2) >> group) == ((right >> 2) >> group)) & (
        ((left & 3) >> group) == ((right & 3) >> group)
    )
    side = 8 << group
    count = (side * side * width).astype(F32)
    spread = lax.dot_general(
        sums, same_group, (((1,), (0,)), ((), ())), precision=HIGH, preferred_element_type=F32
    )
    total = lax.dot_general(
        same_image.astype(F32), spread, (((1,), (0,)), ((), ())), precision=HIGH, preferred_element_type=F32
    )
    return total / count


def tile_rows(block):
    return jnp.sum(block.reshape(4, 8, C), axis=1)


def spread_rows(ref, tiles):
    for ty in range(4):
        for tx in range(4):
            t = 4 * ty + tx
            ref[ty, 8 * tx : 8 * tx + 8, :] = jnp.broadcast_to(tiles[t : t + 1, :], (8, C))


def norm_stats(x_ref, group, mean_ref, rstd_ref):
    parts = []
    for ty in range(4):
        acc = x_ref[pl.ds(ty * 256, 32), :]
        for y in range(1, 8):
            acc = acc + x_ref[pl.ds(ty * 256 + y * 32, 32), :]
        parts.append(tile_rows(acc))
    spread_rows(mean_ref, image_mean(jnp.concatenate(parts, axis=0), group))
    parts = []
    for ty in range(4):
        mu = mean_ref[ty]
        acc = jnp.zeros((32, C), F32)
        for y in range(8):
            cen = x_ref[pl.ds(ty * 256 + y * 32, 32), :] - mu
            acc = acc + cen * cen
        parts.append(tile_rows(acc))
    var = image_mean(jnp.concatenate(parts, axis=0), group)
    spread_rows(rstd_ref, lax.rsqrt(var + 1e-05))


def store_shifts(ref, y, val, side):
    x = lax.broadcasted_iota(jnp.int32, (32, C), 0) & (side - 1)
    zero = jnp.zeros((32, C), F32)
    left = jnp.where(x != 0, pltpu.roll(val, 1, 0), zero)
    right = jnp.where(x != side - 1, pltpu.roll(val, 31, 0), zero)
    rows = pl.ds(pl.multiple_of(PAD + y * 32, 32), 32)
    ref[rows, 0:C] = left.astype(BF16)
    ref[rows, C : 2 * C] = val.astype(BF16)
    ref[rows, 2 * C : 3 * C] = right.astype(BF16)


def clear_pads(ref):
    ref[0:PAD, :] = jnp.zeros((PAD, 3 * C), BF16)
    ref[PAD + ROWS : 2 * PAD + ROWS, :] = jnp.zeros((PAD, 3 * C), BF16)


def row_mask(shape, dim, dy, side):
    y = (lax.broadcasted_iota(jnp.int32, shape, dim) // 32) & (side - 1)
    return y != 0 if dy < 0 else y != side - 1


SHARD = 64
RES = (("mat", 0, 1152),)
MIX = (("mat", 0, 512), ("mat", 512, 512), ("lat", 1024, 128))


def part_shapes(kind, lanes, z_size, dtype):
    rows = 2 * SHARD * z_size
    if kind == "mat":
        return [((rows, 4 * lanes), dtype)]
    if kind == "lat":
        return [((rows // 2, 4 * lanes), dtype)] * 2
    return [((4, rows, lanes), dtype)]


def part_blocks(kind, refs, lanes, dp, f):
    cols = pl.ds(pl.multiple_of(f * lanes, 128), lanes)
    if kind == "lat":
        half = SHARD // 2
        at = pl.ds(pl.multiple_of(dp * half, half), half)
        return [(pl.ds(i * half, half), refs[i].at[at, cols]) for i in range(2)]
    at = pl.ds(pl.multiple_of(dp * SHARD, SHARD), SHARD)
    where = refs[0].at[at, cols] if kind == "mat" else refs[0].at[f, at, :]
    return [(pl.ds(0, SHARD), where)]


def part_count(kind):
    return 2 if kind == "lat" else 1


def copy_count(parts, z_size):
    return 8 * z_size * sum(part_count(kind) for kind, _, _ in parts)


def block_copies(parts, info_ref, pieces, wholes, sems, inward):
    core, f = info_ref[1], info_ref[2]
    z_size = pieces[0].shape[0] // 4
    copies = []
    for side in range(2):
        owner = core if side == 0 else 1 - core
        for far in range(2):
            for near in range(2):
                for z in range(z_size):
                    at_f = f ^ ((2 - owner) * near) ^ ((1 + owner) * far)
                    at_dp = 2 * z + owner
                    first = 0
                    for kind, lane, lanes in parts:
                        refs = wholes[first : first + part_count(kind)]
                        for rows, where in part_blocks(kind, refs, lanes, at_dp, at_f):
                            piece = pieces[side].at[(2 * far + near) * z_size + z, rows, pl.ds(lane, lanes)]
                            ends = (piece, where) if inward else (where, piece)
                            copies.append(pltpu.make_async_copy(*ends, sems.at[len(copies)]))
                        first += part_count(kind)
    return copies


def weight_copies(info_ref, refs, dst_ref, sems):
    if len(refs) == 1:
        return [pltpu.make_async_copy(refs[0], dst_ref, sems.at[0])]
    return block_copies(RES, info_ref, refs, (dst_ref,), sems, True)


def weight_sems(weight):
    return pltpu.SemaphoreType.DMA((1 if len(weight) == 1 else copy_count(RES, weight[0].shape[0] // 4),))


def conv_fwd_kernel(n_weight, has_res, info_ref, x_ref, gain_ref, *rest):
    weight, rest = rest[:n_weight], rest[n_weight:]
    if has_res:
        res_ref, *rest = rest
    t_ref, a3_ref, wt_ref, mean_ref, rstd_ref, sems = rest
    copies = weight_copies(info_ref, weight, wt_ref, sems)
    for copy in copies:
        copy.start()
    group = info_ref[0]
    side = 8 << group
    norm_stats(x_ref, group, mean_ref, rstd_ref)
    clear_pads(a3_ref)
    gamma = gain_ref[0:1, :]
    beta = gain_ref[1:2, :]

    def body(y, carry):
        ty = y // 8
        v = (x_ref[pl.ds(pl.multiple_of(y * 32, 32), 32), :] - mean_ref[ty]) * rstd_ref[ty] * gamma + beta
        store_shifts(a3_ref, y, v * sigmoid(v), side)
        return carry

    lax.fori_loop(0, 32, body, 0, unroll=4)
    for copy in copies:
        copy.wait()
    out = nt(a3_ref[PAD : PAD + ROWS, :], wt_ref[:, 3 * C : 6 * C])
    if has_res:
        out = out + res_ref[...]
    t_ref[...] = out
    for dy in (-1, 1):
        part = nt(a3_ref[PAD + 32 * dy : PAD + 32 * dy + ROWS, :], wt_ref[:, (dy + 1) * 3 * C : (dy + 2) * 3 * C])
        t_ref[...] += jnp.where(row_mask((ROWS, 1), 0, dy, side), part, 0.0)


SMEM = pl.BlockSpec(memory_space=pltpu.SMEM)
VM = pl.BlockSpec(memory_space=pltpu.VMEM)
ANY = pl.BlockSpec(memory_space=pl.ANY)
PARAMS = pltpu.CompilerParams(vmem_limit_bytes=VMEM_LIMIT)
CONV_FLOPS = 2 * ROWS * 9 * C * C


def cost(flops, size):
    return pl.CostEstimate(flops=flops, bytes_accessed=size, transcendentals=0)


def conv_fwd(info, x, gains, weight, res=None):
    args = [info, x, gains, *weight] + ([] if res is None else [res])
    return pl.pallas_call(
        functools.partial(conv_fwd_kernel, len(weight), res is not None),
        out_shape=(
            jax.ShapeDtypeStruct((ROWS, C), F32),
            jax.ShapeDtypeStruct((ROWS + 2 * PAD, 3 * C), BF16),
        ),
        in_specs=[SMEM, VM, VM] + [ANY] * len(weight) + ([] if res is None else [VM]),
        out_specs=(VM, VM),
        scratch_shapes=[
            pltpu.VMEM((C, 9 * C), BF16),
            pltpu.VMEM((4, 32, C), F32),
            pltpu.VMEM((4, 32, C), F32),
            weight_sems(weight),
        ],
        compiler_params=PARAMS,
        cost_estimate=cost(2 * CONV_FLOPS, 12 << 20),
        name="conv_fwd",
    )(*args)


def conv_dw_kernel(split, info_ref, dt_ref, a3_ref, *rest):
    if split:
        keep_ref, send_ref, dw_ref, dtt_ref, sems = rest
    else:
        dw_ref, dtt_ref = rest
    side = 8 << info_ref[0]
    dtt_ref[1] = dt_ref[...].astype(F32).T.astype(BF16)
    flat = dtt_ref[1]
    for dy in (-1, 1):
        keep = row_mask((1, ROWS), 1, dy, side).astype(BF16)
        dtt_ref[dy + 1] = flat * keep
    for dy in (-1, 0, 1):
        dw = nn(dtt_ref[dy + 1], a3_ref[PAD + 32 * dy : PAD + 32 * dy + ROWS, :])
        dw_ref[:, (dy + 1) * 3 * C : (dy + 2) * 3 * C] = dw.astype(dw_ref.dtype)
    if split:
        copies = block_copies(RES, info_ref, (keep_ref, send_ref), (dw_ref,), sems, False)
        for copy in copies:
            copy.start()
        for copy in copies:
            copy.wait()


def conv_dw(info, dt, a3, z_size):
    scratch = [pltpu.VMEM((3, C, ROWS), BF16)]
    if z_size:
        block = jax.ShapeDtypeStruct((4 * z_size, SHARD, 9 * C // 4), BF16)
        shapes, specs = (block, block), (ANY, ANY)
        scratch = [pltpu.VMEM((C, 9 * C), BF16)] + scratch + [pltpu.SemaphoreType.DMA((copy_count(RES, z_size),))]
    else:
        shapes, specs = jax.ShapeDtypeStruct((C, 9 * C), F32), VM
    return pl.pallas_call(
        functools.partial(conv_dw_kernel, z_size),
        out_shape=shapes,
        in_specs=[SMEM, VM, VM],
        out_specs=specs,
        scratch_shapes=scratch,
        compiler_params=PARAMS,
        cost_estimate=cost(2 * CONV_FLOPS, 12 << 20),
        name="conv_dw",
    )(info, dt, a3)


def conv_dx_kernel(n_weight, has_res, info_ref, dt_ref, x_ref, gain_ref, *rest):
    weight, rest = rest[:n_weight], rest[n_weight:]
    if has_res:
        res_ref, *rest = rest
    dx_ref, dgain_ref, wt_ref, d3_ref, mean_ref, rstd_ref, ds_ref, sems = rest
    copies = weight_copies(info_ref, weight, wt_ref, sems)
    for copy in copies:
        copy.start()
    group = info_ref[0]
    side = 8 << group
    clear_pads(d3_ref)

    def body(y, carry):
        val = dt_ref[pl.ds(pl.multiple_of(y * 32, 32), 32), :].astype(F32)
        store_shifts(d3_ref, y, val, side)
        return carry

    lax.fori_loop(0, 32, body, 0, unroll=4)
    norm_stats(x_ref, group, mean_ref, rstd_ref)
    for copy in copies:
        copy.wait()
    for dy in (0, -1, 1):
        part = None
        for dx in (-1, 0, 1):
            t = 3 * (dy + 1) + dx + 1
            one = nn(
                d3_ref[PAD - 32 * dy : PAD - 32 * dy + ROWS, (1 - dx) * C : (2 - dx) * C],
                wt_ref[:, t * C : (t + 1) * C],
            )
            part = one if part is None else part + one
        if dy == 0:
            ds_ref[...] = part
        else:
            ds_ref[...] += jnp.where(row_mask((ROWS, 1), 0, -dy, side), part, 0.0)
    gamma = gain_ref[0:1, :]
    beta = gain_ref[1:2, :]
    first, second = [], []
    for ty in range(4):
        mu, rs = mean_ref[ty], rstd_ref[ty]

        def step(y, carry, ty=ty, mu=mu, rs=rs):
            one, two = carry
            rows = pl.ds(pl.multiple_of(ty * 256 + y * 32, 32), 32)
            xh = (x_ref[rows, :] - mu) * rs
            v = xh * gamma + beta
            sg = sigmoid(v)
            ds = ds_ref[rows, :] * (sg * (1.0 + v * (1.0 - sg)))
            ds_ref[rows, :] = ds
            return (one + ds, two + ds * xh)

        zero = jnp.zeros((32, C), F32)
        one, two = lax.fori_loop(0, 8, step, (zero, zero), unroll=2)
        first.append(tile_rows(one))
        second.append(tile_rows(two))
    first = jnp.concatenate(first, axis=0)
    second = jnp.concatenate(second, axis=0)
    dgain_ref[0:1, :] = jnp.sum(second, axis=0, keepdims=True)
    dgain_ref[1:2, :] = jnp.sum(first, axis=0, keepdims=True)
    m_one = image_mean(first * gamma, group)
    m_two = image_mean(second * gamma, group)
    for ty in range(4):
        mu, rs = mean_ref[ty], rstd_ref[ty]
        one = jnp.concatenate([jnp.broadcast_to(m_one[4 * ty + tx : 4 * ty + tx + 1, :], (8, C)) for tx in range(4)], axis=0)
        two = jnp.concatenate([jnp.broadcast_to(m_two[4 * ty + tx : 4 * ty + tx + 1, :], (8, C)) for tx in range(4)], axis=0)

        def step(y, carry, ty=ty, mu=mu, rs=rs, one=one, two=two):
            rows = pl.ds(pl.multiple_of(ty * 256 + y * 32, 32), 32)
            xh = (x_ref[rows, :] - mu) * rs
            dx = rs * (ds_ref[rows, :] * gamma - one - xh * two)
            if has_res:
                dx = dx + res_ref[rows, :]
            dx_ref[rows, :] = dx.astype(dx_ref.dtype)
            return carry

        lax.fori_loop(0, 8, step, 0, unroll=2)


def conv_dx(info, dt, x, gains, weight, res=None, low=True):
    args = [info, dt, x, gains, *weight] + ([] if res is None else [res])
    return pl.pallas_call(
        functools.partial(conv_dx_kernel, len(weight), res is not None),
        out_shape=(
            jax.ShapeDtypeStruct((ROWS, C), BF16 if low else F32),
            jax.ShapeDtypeStruct((2, C), F32),
        ),
        in_specs=[SMEM, VM, VM, VM] + [ANY] * len(weight) + ([] if res is None else [VM]),
        out_specs=(VM, VM),
        scratch_shapes=[
            pltpu.VMEM((C, 9 * C), BF16),
            pltpu.VMEM((ROWS + 2 * PAD, 3 * C), BF16),
            pltpu.VMEM((4, 32, C), F32),
            pltpu.VMEM((4, 32, C), F32),
            pltpu.VMEM((ROWS, C), F32),
            weight_sems(weight),
        ],
        compiler_params=PARAMS,
        cost_estimate=cost(3 * CONV_FLOPS, 12 << 20),
        name="conv_dx",
    )(*args)


def silu_slope(value):
    gate = sigmoid(value)
    return gate * (1.0 + value * (1.0 - gate))


def transposed(value):
    return value.astype(F32).T.astype(BF16)


HALF = SIDE // 2
LAT = HALF * HALF


def to_depth(src_ref, lanes_ref, dst_ref):
    for k in range(C // 128):
        lanes_ref[k] = src_ref[:, k * 128 : (k + 1) * 128]
    for k in range(C // 128):
        for b in range(2):
            block = lanes_ref[k, pl.ds(b, ROWS // 2, stride=2), :].reshape(HALF, 2, HALF, 128)
            for a in range(2):
                at = (2 * a + b) * C + k * 128
                dst_ref[:, at : at + 128] = block[:, a].reshape(LAT, 128).astype(dst_ref.dtype)


def from_depth(src_ref, lanes_ref, dst_ref):
    for k in range(C // 128):
        for b in range(2):
            pair = [
                src_ref[:, (2 * a + b) * C + k * 128 : (2 * a + b) * C + (k + 1) * 128].reshape(HALF, 1, HALF, 128)
                for a in range(2)
            ]
            lanes_ref[k, pl.ds(b, ROWS // 2, stride=2), :] = jnp.concatenate(pair, axis=1).reshape(ROWS // 2, 128)
    for k in range(C // 128):
        dst_ref[:, k * 128 : (k + 1) * 128] = lanes_ref[k]


def mid_fwd_kernel(
    h_ref, ws0_ref, wl0_ref, code_ref, wl1_ref, ws1_ref,
    e_ref, d_ref, s_ref, q_ref, y_ref, s2_ref, g_ref, commit_ref, dcom_ref, resid_ref, u_ref, lanes_ref,
):
    to_depth(h_ref, lanes_ref, e_ref)
    d = nt(e_ref[...], ws0_ref[...])
    d_ref[...] = d
    s = (d * sigmoid(d)).astype(BF16)
    s_ref[...] = s
    z = nt(s, wl0_ref[...])
    q = jnp.zeros((LAT, ZD), F32)
    commit = jnp.zeros((LAT, ZD), F32)
    dcom = jnp.zeros((LAT, ZD), F32)
    for k in range(4):
        resid_ref[k * LAT : (k + 1) * LAT, :] = (z - q).astype(BF16)
        q = q + code_ref[k * LAT : (k + 1) * LAT, :].astype(F32)
        diff = z - q
        commit = commit + diff * diff
        dcom = dcom + diff
    commit_ref[...] = jnp.sum(commit, axis=0, keepdims=True)
    dcom_ref[...] = dcom
    quant = (z + (q - z)).astype(BF16)
    q_ref[...] = quant
    y = nn(quant, wl1_ref[...])
    y_ref[...] = y
    s2 = (y * sigmoid(y)).astype(BF16)
    s2_ref[...] = s2
    u_ref[...] = nn(s2, ws1_ref[...])
    from_depth(u_ref, lanes_ref, g_ref)


def mid_fwd(h, ws0, wl0, codes, wl1, ws1):
    shape = jax.ShapeDtypeStruct
    return pl.pallas_call(
        mid_fwd_kernel,
        out_shape=(
            shape((LAT, 4 * C), BF16),
            shape((LAT, C), F32),
            shape((LAT, C), BF16),
            shape((LAT, ZD), BF16),
            shape((LAT, C), F32),
            shape((LAT, C), BF16),
            shape((ROWS, C), F32),
            shape((1, ZD), F32),
            shape((LAT, ZD), F32),
            shape((4 * LAT, ZD), BF16),
        ),
        in_specs=[VM] * 6,
        out_specs=(VM,) * 10,
        scratch_shapes=[pltpu.VMEM((LAT, 4 * C), F32), pltpu.VMEM((C // 128, ROWS, 128), F32)],
        compiler_params=PARAMS,
        cost_estimate=cost(4 << 30, 12 << 20),
        name="mid_fwd",
    )(h, ws0, wl0, codes, wl1, ws1)


def mid_bwd_kernel(
    split, scale, info_ref, dg_ref, e_ref, d_ref, s_ref, q_ref, y_ref, s2_ref, dcom_ref, ws0_ref, wl0_ref, wl1_ref,
    ws1_ref, *rest,
):
    if split:
        keep_ref, send_ref, dh_ref, *wholes, du_ref, de_ref, lanes_ref, sems = rest
    else:
        *wholes, dh_ref, du_ref, de_ref, lanes_ref = rest
    dws0_ref, dws1_ref, dwl0_ref, dwl1_ref = wholes
    to_depth(dg_ref, lanes_ref, du_ref)
    out = dws0_ref.dtype
    ds2 = nt(du_ref[...], ws1_ref[...])
    dy = (ds2 * silu_slope(y_ref[...])).astype(BF16)
    dws1_ref[...] = nn(transposed(s2_ref[...]), du_ref[...]).astype(out)
    dwl1_ref[...] = nn(transposed(q_ref[...]), dy).astype(out)
    dz = (nt(dy, wl1_ref[...]) + scale * dcom_ref[...]).astype(BF16)
    dwl0_ref[...] = nn(transposed(dz), s_ref[...]).astype(out)
    ds = nn(dz, wl0_ref[...])
    dd = (ds * silu_slope(d_ref[...])).astype(BF16)
    dws0_ref[...] = nn(transposed(dd), e_ref[...]).astype(out)
    copies = []
    if split:
        copies = block_copies(MIX, info_ref, (keep_ref, send_ref), wholes, sems, False)
    for copy in copies:
        copy.start()
    de_ref[...] = nn(dd, ws0_ref[...])
    from_depth(de_ref, lanes_ref, dh_ref)
    for copy in copies:
        copy.wait()


def mid_bwd(info, scale, dg, e, d, s, q, y, s2, dcom, ws0, wl0, wl1, ws1, z_size):
    shape = jax.ShapeDtypeStruct
    wholes = [(C, 4 * C), (C, 4 * C), (ZD, C), (ZD, C)]
    scratch = [
        pltpu.VMEM((LAT, 4 * C), BF16),
        pltpu.VMEM((LAT, 4 * C), F32),
        pltpu.VMEM((C // 128, ROWS, 128), F32),
    ]
    field = shape((ROWS, C), F32)
    if z_size:
        block = shape((4 * z_size, SHARD, 1152), BF16)
        shapes, specs = (block, block, field), (ANY, ANY, VM)
        scratch = [pltpu.VMEM(one, BF16) for one in wholes] + scratch
        scratch += [pltpu.SemaphoreType.DMA((copy_count(MIX, z_size),))]
    else:
        shapes, specs = tuple(shape(one, F32) for one in wholes) + (field,), (VM,) * 5
    out = pl.pallas_call(
        functools.partial(mid_bwd_kernel, z_size, scale),
        out_shape=shapes,
        in_specs=[SMEM] + [VM] * 12,
        out_specs=specs,
        scratch_shapes=scratch,
        compiler_params=PARAMS,
        cost_estimate=cost(4 << 30, 12 << 20),
        name="mid_bwd",
    )(info, dg, e, d, s, q, y, s2, dcom, ws0, wl0, wl1, ws1)
    return out[-1], out[:-1]


def head_kernel(total_ref, g_ref, wp_ref, pix_ref, mask_ref, dw_ref, dg_ref, loss_ref, o_ref, dr_ref):
    inv = total_ref[0]
    loss = jnp.zeros((1, pix_ref.shape[1]), F32)
    for i in range(4):
        rows = pl.ds(i * 256, 256)
        g = g_ref[rows, :]
        gate = sigmoid(g)
        o = (g * gate).astype(BF16)
        o_ref[rows, :] = o
        err = nn(o, wp_ref[...]) - pix_ref[rows, :].astype(F32)
        keep = mask_ref[rows, :].astype(F32)
        smooth = jnp.sqrt(err * err + 1.0)
        loss = loss + jnp.sum(keep * (smooth - 1.0), axis=0, keepdims=True)
        dr = (keep * err / smooth / inv).astype(BF16)
        dr_ref[rows, :] = dr
        do = nt(dr, wp_ref[...])
        dg_ref[rows, :] = do * (gate * (1.0 + g * (1.0 - gate)))
    loss_ref[...] = loss
    dw_ref[...] = nn(transposed(o_ref[...]), dr_ref[...]).astype(dw_ref.dtype)


def head(total, g, wp, pix, mask, grad_type=BF16):
    shape = jax.ShapeDtypeStruct
    width = pix.shape[1]
    return pl.pallas_call(
        head_kernel,
        out_shape=(shape((C, width), grad_type), shape((ROWS, C), F32), shape((1, width), F32)),
        in_specs=[SMEM, VM, VM, VM, VM],
        out_specs=(VM,) * 3,
        scratch_shapes=[pltpu.VMEM((ROWS, C), BF16), pltpu.VMEM((ROWS, width), BF16)],
        compiler_params=PARAMS,
        cost_estimate=cost(6 << 30, 12 << 20),
        name="head",
    )(total, g, wp, pix, mask)


BOTH = ("z", "core", "fsdp")
COLS = ("z", "core")


def swap(shard):
    return jnp.swapaxes(shard, -1, -2).astype(BF16)


def across(x, near):
    n = lax.axis_size("fsdp")
    masks = (2, 1) if near else (1, 2)
    return lax.ppermute(x, ("core", "fsdp"), [(c * n + f, c * n + (f ^ masks[c])) for c in range(2) for f in range(n)])


def partner(x):
    return lax.ppermute(x, "core", [(0, 1), (1, 0)])


def everyone(x):
    n = lax.axis_size("z") * lax.axis_size("core") * lax.axis_size("fsdp")
    return lax.all_to_all(jnp.broadcast_to(x[None], (n,) + x.shape), BOTH, 0, 0, tiled=True)


def along_z(x, step):
    n = lax.axis_size("z")
    return lax.ppermute(x, "z", [(i, i ^ step) for i in range(n)])


def shuffle(x, axis):
    return lax.all_to_all(x, axis, 0, 0, tiled=True)


def assemble_kernel(parts, info_ref, own, other, *rest):
    copies = block_copies(parts, info_ref, (own, other), rest[:-1], rest[-1], True)
    for copy in copies:
        copy.start()
    for copy in copies:
        copy.wait()


def assemble(info, pieces, parts):
    z_size = pieces[0].shape[0] // 4
    shapes = [s for kind, _, lanes in parts for s in part_shapes(kind, lanes, z_size, BF16)]
    return pl.pallas_call(
        functools.partial(assemble_kernel, parts),
        out_shape=tuple(jax.ShapeDtypeStruct(*s) for s in shapes),
        in_specs=[SMEM] + [ANY] * 2,
        out_specs=(VM,) * len(shapes),
        scratch_shapes=[pltpu.SemaphoreType.DMA((copy_count(parts, z_size),))],
        compiler_params=PARAMS,
        cost_estimate=cost(1 << 30, 10 << 20),
        name="assemble",
    )(info, *pieces)


def gather_all(shards, others, slow):
    z_size = lax.axis_size("z")
    count = len(shards)
    shards = list(shards)
    done = [{} for _ in shards]
    pieces, side, waiting = {}, {}, {}
    groups = [(1, 3), (3, count)] if count else []
    bulks = {}
    for first, last in groups:
        bulks[first] = lax.all_gather(jnp.concatenate(shards[first:last], axis=1), "z")
    for step in range(max([count + 2] + list(others)) + 1):
        new = {}
        if 0 <= step - 2 < count:
            new["both", step - 2] = across(done[step - 2]["near"], False)
        if 0 <= step - 1 < count:
            new["far", step - 1] = across(done[step - 1]["z"], False)
            new["near", step - 1] = across(done[step - 1]["z"], True)
        if step < min(count, 1):
            new["z", step] = shuffle(jnp.broadcast_to(shards[step][None], (z_size,) + shards[step].shape), "z")
        for i, (first, last) in enumerate(groups):
            if step == i + 1:
                new["bulk", first] = bulks[first]
        if 0 <= step - 3 < count:
            own = jnp.concatenate([done[step - 3][name] for name in ("z", "near", "far", "both")])
            new["own", step - 3] = own
            new["core", step - 3] = partner(own)
        if step in slow:
            due, function = slow[step]
            waiting[due] = function(pieces, side)
        if step in waiting:
            side = {**side, **waiting.pop(step)}
        if step in others:
            side = {**side, **others[step](pieces, side)}
        names = list(new)
        values, shards[step + 1 :], side = lax.optimization_barrier((list(new.values()), shards[step + 1 :], side))
        for (name, i), value in zip(names, values):
            done[i][name] = value
        for i, (first, last) in enumerate(groups):
            if step == i + 1:
                at = 0
                for j in range(first, last):
                    done[j]["z"] = done[first]["bulk"][:, :, at : at + shards[j].shape[1]]
                    at += shards[j].shape[1]
        if 0 <= step - 3 < count:
            pieces[step - 3] = (done[step - 3]["own"], done[step - 3]["core"])
    return pieces, side


def add_up(parts):
    total = parts[0].astype(F32)
    for part in parts[1:]:
        total = total + part.astype(F32)
    return total


class Slow:
    def __init__(self, value):
        self.value = value


def scatter_stages(keep, send, tie, bulk, out):
    half = keep.shape[0] // 2
    keep, got = yield keep, partner(send)
    parts = [keep, got]
    for near in (False, True):
        away = add_up([p[half : 2 * half] for p in parts]).astype(BF16)
        if near and tie:
            away, tie[0] = lax.optimization_barrier((away, tie[0]))
        *parts, got = yield *parts, across(away, near)
        parts.append(got)
        half = half // 2
    sums = add_up([p[: 2 * half] for p in parts]).astype(BF16)
    if bulk:
        got = yield Slow(lax.psum_scatter(sums, "z", scatter_dimension=0))
        out.append(got.astype(F32))
    else:
        got = yield shuffle(sums, "z")
        out.append(jnp.sum(got.astype(F32), axis=0))


def scatter_pair(blocks, out):
    got = yield shuffle(blocks, ("core", "fsdp"))
    sums = jnp.sum(got.astype(F32), axis=0)
    me = lax.axis_index("z")
    away = [along_z(lax.dynamic_index_in_dim(sums, me ^ k, keepdims=False).astype(BF16), k) for k in range(1, sums.shape[0])]
    away = yield away
    out.append(add_up([lax.dynamic_index_in_dim(sums, me, keepdims=False)] + away))


def scatter_direct(blocks, out):
    got = yield shuffle(blocks, BOTH)
    out.append(jnp.sum(got.astype(F32), axis=0))


class Overlap:
    def __init__(self):
        self.live = []

    def add(self, stages, *args, late=0):
        out = []
        stages = stages(*args, out)
        self.live.append((stages, next(stages), late))
        return out

    def finish(self):
        for stages, value, _ in self.live:
            try:
                while True:
                    value = stages.send(value.value if isinstance(value, Slow) else value)
            except StopIteration:
                pass
        self.live = []

    def push(self, values):
        stages, value, _ = self.live[-1]
        values, value = lax.optimization_barrier((values, value))
        self.live[-1] = (stages, stages.send(value), 0)
        return values

    def step(self, values, use=None):
        due = [value for _, value, late in self.live if not late]
        values, due = lax.optimization_barrier((values, due))
        if use is not None:
            use(values)
        live, at = [], 0
        for stages, value, late in self.live:
            if late:
                live.append((stages, value, late - 1))
                continue
            try:
                value = stages.send(due[at])
                live.append((stages, value.value, 1) if isinstance(value, Slow) else (stages, value, 0))
            except StopIteration:
                pass
            at += 1
        self.live = live
        return values


def fetch_whole(shard):
    cols = lax.all_gather(shard.astype(BF16), COLS, axis=1, tiled=True)
    return jnp.swapaxes(lax.all_gather(cols, "fsdp", axis=0, tiled=True), 0, 1)


def reduce_whole(grad):
    rows = lax.psum_scatter(jnp.swapaxes(grad, 0, 1), "fsdp", scatter_dimension=0, tiled=True)
    return jnp.swapaxes(lax.psum_scatter(rows, COLS, scatter_dimension=1, tiled=True), 0, 1)


def widen(block, width):
    return jnp.pad(block, ((0, 0),) * (block.ndim - 1) + ((0, width - block.shape[-1]),))


def pix_matrix(blocks, width):
    return blocks[:, :, :width].transpose(1, 0, 2).reshape(C, 4 * width)


def pix_blocks(matrix, shard):
    rows, cols = shard
    return matrix.reshape(-1, cols, matrix.shape[1] // rows, rows).transpose(0, 2, 1, 3).reshape(-1, cols, rows)


def adam_step(weight, moment, second, grad, rate):
    moment_new = 0.5 * moment + 0.5 * grad
    second_new = 0.5 * second + 0.5 * grad * grad
    fix = 1.0 - 0.5**STEP
    weight_new = weight - rate * (
        moment_new / fix / (jnp.sqrt(second_new / fix) + 1e-12) + 0.01 * weight
    )
    return (weight_new, moment_new, second_new)


def small_blocks(values, devices):
    flat = jnp.concatenate([value.reshape(-1) for value in values])
    lanes = -(-flat.shape[0] // (128 * devices)) * 128
    return jnp.pad(flat, (0, devices * lanes - flat.shape[0])).reshape(devices, 1, lanes)


def exact(left, right, dims):
    return lax.dot_general(left, right, (dims, ((), ())), preferred_element_type=F32)


def code_slots(codes, devices, capacity, rows):
    n = codes.shape[0]
    owner = codes // rows
    hot = (owner[:, None] == jnp.arange(devices, dtype=jnp.int32)[None, :]).astype(BF16)
    at = jnp.arange(n, dtype=jnp.int32)
    before = (at[None, :] < at[:, None]).astype(BF16)
    rank = exact(before, hot, ((1,), (0,)))
    place = jnp.sum(rank * hot.astype(F32), axis=1).astype(jnp.int32)
    slot = owner * capacity + place
    return (jnp.arange(devices * capacity, dtype=jnp.int32)[:, None] == slot[None, :]).astype(BF16)


def on_device(
    pixels,
    valid_mask,
    size_groups,
    code_index,
    w_pixel,
    w_res,
    w_scale,
    w_latent,
    norm_gains,
    moment_pixel,
    moment_res,
    moment_scale,
    moment_latent,
    moment_gains,
    second_pixel,
    second_res,
    second_scale,
    second_latent,
    second_gains,
    ema_counts,
    ema_sums,
):
    n_inner = lax.axis_size("fsdp")
    z_size = lax.axis_size("z")
    devices = 2 * z_size * n_inner
    latent_all = code_index.shape[1] * devices
    rows = ema_sums.shape[0]
    paired = n_inner == 4 and w_res.shape[1] == 1152 and w_res.shape[2] == SHARD
    blocks = z_size if paired else 0
    place = [lax.axis_index("core"), lax.axis_index("fsdp")]
    info = jnp.stack([size_groups[0]] + [one.astype(jnp.int32) for one in place])

    codes = code_index.reshape(-1)
    capacity = max(2, 2 * codes.shape[0] // devices)
    pick = code_slots(codes, devices, capacity, rows)
    local = codes % rows
    cols = jnp.stack([local // 16, local % 16, jnp.ones_like(local)], axis=1).astype(BF16)
    want = exact(pick, cols, ((1,), (0,)))
    wanted = jnp.where(want[:, 2] > 0.5, want[:, 0] * 16.0 + want[:, 1], -1.0).astype(jnp.int32)
    book = (ema_sums / ema_counts[:, None]).astype(BF16)
    valid = jnp.sum(valid_mask.astype(F32).reshape(-1, 128), axis=0, keepdims=True)

    def row_hot(asked):
        return (asked[:, None] == jnp.arange(rows, dtype=jnp.int32)[None, :]).astype(BF16)

    def prepare(pieces, side):
        wide = -(-capacity // 128) * 128
        request = widen(wanted.astype(F32).reshape(devices, 1, capacity), wide)
        count = jnp.broadcast_to(widen(valid, wide)[None], (devices, 1, wide))
        return {"request": jnp.concatenate([request, count], axis=1)}

    def ask(pieces, side):
        got = shuffle(side["request"], BOTH)
        return {"asked": got[:, 0, :capacity].reshape(-1).astype(jnp.int32), "count": jnp.sum(got[:, 1])}

    def reply(pieces, side):
        answer = exact(row_hot(side["asked"]), book, ((1,), (0,))).astype(BF16)
        return {"replies": shuffle(answer.reshape(devices, capacity, ZD), BOTH)}

    gains = [jnp.stack([norm_gains[j], norm_gains[4 + j]]) for j in range(4)]
    width = w_pixel.shape[1]

    def run_conv0(pieces, side):
        if paired:
            (pix,) = assemble(info, pieces[0], (("pix", RES[0][2], 256),))
            h0 = nt(pixels, pix_matrix(pix, width))
            weight = pieces[0]
        else:
            h0 = nt(pixels, fetch_whole(w_pixel[0]))
            weight = (fetch_whole(w_res[0]),)
        t1, a1 = conv_fwd(info, h0, gains[0], weight)
        return {"h0": h0, "t1": t1, "a1": a1, "res0": weight}

    def run_conv1(pieces, side):
        weight = pieces[1] if paired else (fetch_whole(w_res[1]),)
        h1, a2 = conv_fwd(info, side["t1"], gains[1], weight, side["h0"])
        return {"h1": h1, "a2": a2, "res1": weight}

    def run_mid(pieces, side):
        if paired:
            mats = assemble(info, pieces[2], MIX)
        else:
            mats = [fetch_whole(w_scale[i]) for i in range(2)] + [fetch_whole(w_latent[i]) for i in range(2)]
        scale0, scale1, lat0, lat1 = mats
        picked = exact(pick, side["replies"].reshape(-1, ZD), ((0,), (0,))).astype(BF16)
        return {"mid": mid_fwd(side["h1"], scale0, lat0, picked, lat1, scale1), "mats": mats}

    def run_conv2(pieces, side):
        weight = pieces[3] if paired else (fetch_whole(w_res[2]),)
        t3, a3 = conv_fwd(info, side["mid"][6], gains[2], weight)
        return {"t3": t3, "a3": a3, "res2": weight}

    def run_conv3(pieces, side):
        sent = exact(pick, side["mid"][9], ((1,), (0,))).astype(BF16)
        held = shuffle(sent.reshape(devices, capacity, ZD), BOTH)
        if paired:
            (pix,) = assemble(info, pieces[4], (("pix", RES[0][2], 256),))
            pix = pix_matrix(pix, width)
            weight = pieces[4]
        else:
            pix, weight = fetch_whole(w_pixel[1]), (fetch_whole(w_res[3]),)
        g1, a4 = conv_fwd(info, side["t3"], gains[3], weight, side["mid"][6])
        out = BF16 if paired else F32
        d_head, dg1, loss = head(side["count"].reshape(1), g1, pix, pixels, valid_mask, out)
        return {"held": held, "a4": a4, "res3": weight, "d_head": d_head, "dg1": dg1, "loss": loss}

    others = {0: prepare, 2: ask, 4: run_conv0, 5: run_conv1, 6: run_mid, 7: run_conv2, 8: run_conv3}
    shards = []
    if paired:
        first = jnp.concatenate([swap(w_res[0]), widen(swap(w_pixel[0]), 256)], axis=1)
        first, res, pix, scale, latent = lax.optimization_barrier((first, w_res, w_pixel, w_scale, w_latent))
        scale, latent = swap(scale), swap(latent)
        mix = jnp.concatenate([scale[0], scale[1], latent.reshape(-1, latent.shape[2])], axis=1)
        last = jnp.concatenate([swap(res[3]), widen(swap(pix[1]), 256)], axis=1)
        shards = [first, swap(res[1]), mix, swap(res[2]), last]
    _, side = gather_all(shards, others, {3: (4, reply)})
    total_valid = side["count"]
    e, d, s, quant, y, s2, g0, commit, dcom, _ = side["mid"]
    h0, t1, a1, h1, a2, t3, a3, a4 = [side[name] for name in ("h0", "t1", "a1", "h1", "a2", "t3", "a3", "a4")]
    res_w = [side["res0"], side["res1"], side["res2"], side["res3"]]
    scale0, scale1, lat0, lat1 = side["mats"]
    d_head, dg1, loss = side["d_head"], side["dg1"], side["loss"]

    hot_rows = row_hot(side["asked"])
    held = side["held"].reshape(-1, ZD)
    my_sums = exact(hot_rows, held, ((0,), (0,)))
    my_counts = jnp.sum(hot_rows.astype(F32), axis=0)
    counts_new = EMA_DECAY * ema_counts + (1.0 - EMA_DECAY) * my_counts
    sums_new = EMA_DECAY * ema_sums + (1.0 - EMA_DECAY) * my_sums
    book_new = sums_new / counts_new[:, None]

    scale = 2.0 * COMMIT_WEIGHT / (latent_all * ZD)
    loss_rows = jnp.stack([jnp.sum(one.reshape(-1, 128), axis=0) for one in (loss, commit)])
    if paired:
        overlap = Overlap()
        shard = w_pixel.shape[1:]
        sum_head = overlap.add(scatter_direct, pix_blocks(d_head, shard), late=2)
        dw, dg1 = overlap.step((conv_dw(info, dg1, a4, z_size), dg1))
        sum_res3 = overlap.add(scatter_stages, *dw, (), True)
        dt3, dn3 = overlap.step(conv_dx(info, dg1, t3, gains[3], res_w[3]))
        dw, dt3 = overlap.step((conv_dw(info, dt3, a3, z_size), dt3))
        sum_res2 = overlap.add(scatter_stages, *dw, (), True)
        dg0, dn2 = overlap.step(conv_dx(info, dt3, g0, gains[2], res_w[2], dg1, False))
        dh1, dw = overlap.step(
            mid_bwd(info, scale, dg0, e, d, s, quant, y, s2, dcom, scale0, lat0, lat1, scale1, z_size)
        )
        sum_mix = overlap.add(scatter_stages, *dw, (), True)
        dw, dh1 = overlap.step((conv_dw(info, dh1, a2, z_size), dh1))
        sum_res1 = overlap.add(scatter_stages, *dw, (), True)
        dh1 = overlap.push(dh1)
        dt1, dn1 = overlap.step(conv_dx(info, dh1, t1, gains[1], res_w[1]))
        dw, dt1 = overlap.step((conv_dw(info, dt1, a1, z_size), dt1))
        tie = []
        sum_res0 = overlap.add(scatter_stages, *dw, tie, True)
        dt1 = overlap.push(dt1)
        _, dn0 = overlap.step(conv_dx(info, dt1, h0, gains[0], res_w[0], dh1), lambda got: tie.append(got[0]))
        d_patch = exact(tie[0], pixels, ((0,), (0,))).astype(BF16)
        d_patch = pix_blocks(d_patch, shard).reshape(z_size, 2 * n_inner, *shard[::-1])
        sum_patch = overlap.add(scatter_pair, d_patch.transpose(1, 0, 2, 3))
        small = overlap.add(scatter_direct, small_blocks([dn0, dn1, dn2, dn3, loss_rows], devices))
        overlap.finish()
        small = small[0]
        grad_pixel = jnp.stack([sum_patch[0], sum_head[0]])
        grad_res = jnp.stack([sum_res0[0], sum_res1[0], sum_res2[0], sum_res3[0]])
        grad_scale = jnp.stack([sum_mix[0][:, :512], sum_mix[0][:, 512:1024]])
        grad_latent = sum_mix[0][:, 1024:].reshape(2, SHARD // 2, -1)
    else:
        d_res3 = conv_dw(info, dg1, a4, 0)
        dt3, dn3 = conv_dx(info, dg1, t3, gains[3], res_w[3])
        d_res2 = conv_dw(info, dt3, a3, 0)
        dg0, dn2 = conv_dx(info, dt3, g0, gains[2], res_w[2], dg1, False)
        dh1, (d_scale0, d_scale1, d_lat0, d_lat1) = mid_bwd(
            info, scale, dg0, e, d, s, quant, y, s2, dcom, scale0, lat0, lat1, scale1, 0
        )
        d_res1 = conv_dw(info, dh1, a2, 0)
        dt1, dn1 = conv_dx(info, dh1, t1, gains[1], res_w[1])
        d_res0 = conv_dw(info, dt1, a1, 0)
        dh0, dn0 = conv_dx(info, dt1, h0, gains[0], res_w[0], dh1)
        d_patch = exact(dh0, pixels, ((0,), (0,)))
        grad_pixel = jnp.stack([reduce_whole(g) for g in (d_patch, d_head)])
        grad_res = jnp.stack([reduce_whole(g) for g in (d_res0, d_res1, d_res2, d_res3)])
        grad_scale = jnp.stack([reduce_whole(g) for g in (d_scale0, d_scale1)])
        grad_latent = jnp.stack([reduce_whole(g) for g in (d_lat0, d_lat1)])
        small = shuffle(small_blocks([dn0, dn1, dn2, dn3, loss_rows], devices), BOTH)
        small = jnp.sum(small, axis=0)

    squares = jnp.sum(grad_pixel * grad_pixel) + jnp.sum(grad_res * grad_res)
    squares = squares + jnp.sum(grad_scale * grad_scale) + jnp.sum(grad_latent * grad_latent)
    shared = everyone(jnp.concatenate([small, jnp.full((1, small.shape[1]), squares, F32)]))
    total_squares = jnp.sum(shared[:, -1, 0])
    sizes = [2 * C] * 4 + [2 * 128]
    every = shared[:, :-1].reshape(-1)[: sum(sizes)]
    dn0, dn1, dn2, dn3, losses = jnp.split(every, [2 * C, 4 * C, 6 * C, 8 * C])
    dn0, dn1, dn2, dn3 = [one.reshape(2, C) for one in (dn0, dn1, dn2, dn3)]
    grad_gains = jnp.stack([dn0[0], dn1[0], dn2[0], dn3[0], dn0[1], dn1[1], dn2[1], dn3[1]])
    smooth_sum, commit_sum = jnp.sum(losses[:128]), jnp.sum(losses[128:])
    total_squares = total_squares + jnp.sum(grad_gains * grad_gains)
    norm = jnp.sqrt(total_squares)
    factor = CLIP_AT / jnp.maximum(norm, CLIP_AT)
    groups_all = [
        (w_pixel, moment_pixel, second_pixel, grad_pixel),
        (w_res, moment_res, second_res, grad_res),
        (w_scale, moment_scale, second_scale, grad_scale),
        (w_latent, moment_latent, second_latent, grad_latent),
    ]
    outputs = [jnp.stack([smooth_sum, total_valid, commit_sum]), norm.reshape(1)]
    for weight, moment, second, grad in groups_all:
        grad = jnp.swapaxes(grad * factor, 1, 2)
        weight_new, moment_new, second_new = adam_step(weight, moment, second, grad, WEIGHT_RATE)
        outputs += [weight_new, moment_new, second_new, weight_new.astype(BF16)]
    outputs += list(adam_step(norm_gains, moment_gains, second_gains, grad_gains * factor, GAIN_RATE))
    outputs += [counts_new, sums_new, book_new, book_new.astype(BF16)]
    return tuple(outputs)


def solution(mesh):
    outer, inner = mesh.shape["dp"], mesh.shape["fsdp"]
    fine = Mesh(mesh.devices.reshape(outer // 2, 2, inner), BOTH)
    placed = (
        P(BOTH, None),
        P(BOTH, None),
        P(BOTH),
        P(None, BOTH),
        P(None, "fsdp", COLS),
        P(None, "fsdp", COLS),
        P(None, "fsdp", COLS),
        P(None, "fsdp", COLS),
        P(),
        P(None, "fsdp", COLS),
        P(None, "fsdp", COLS),
        P(None, "fsdp", COLS),
        P(None, "fsdp", COLS),
        P(),
        P(None, "fsdp", COLS),
        P(None, "fsdp", COLS),
        P(None, "fsdp", COLS),
        P(None, "fsdp", COLS),
        P(),
        P(BOTH),
        P(BOTH, None),
    )
    return jax.shard_map(
        on_device,
        mesh=fine,
        in_specs=placed,
        out_specs=(
            P(),
            P(),
            P(None, "fsdp", COLS),
            P(None, "fsdp", COLS),
            P(None, "fsdp", COLS),
            P(None, "fsdp", COLS),
            P(None, "fsdp", COLS),
            P(None, "fsdp", COLS),
            P(None, "fsdp", COLS),
            P(None, "fsdp", COLS),
            P(None, "fsdp", COLS),
            P(None, "fsdp", COLS),
            P(None, "fsdp", COLS),
            P(None, "fsdp", COLS),
            P(None, "fsdp", COLS),
            P(None, "fsdp", COLS),
            P(None, "fsdp", COLS),
            P(None, "fsdp", COLS),
            P(),
            P(),
            P(),
            P(BOTH),
            P(BOTH, None),
            P(BOTH, None),
            P(BOTH, None),
        ),
        check_vma=False,
    )
```

```python
import functools
import jax
import jax.numpy as jnp
from jax import lax
from jax.experimental import pallas as pl
from jax.experimental.pallas import tpu as pltpu
from jax.sharding import Mesh
from jax.sharding import PartitionSpec as P

C = 512
ZD = 256
GROUPS = 32
SIDE = 32
STEP = 5
COMMIT_WEIGHT = 0.25
CLIP_AT = 1e-05
EMA_DECAY = 0.8
WEIGHT_RATE = 0.03
GAIN_RATE = 0.4
ROWS = SIDE * SIDE
PAD = SIDE
HIGH = lax.Precision.HIGHEST
F32 = jnp.float32
BF16 = jnp.bfloat16
VMEM_LIMIT = 60 * 1024 * 1024


def sigmoid(v):
    return 0.5 * jnp.tanh(0.5 * v) + 0.5


def nt(left, right):
    return lax.dot_general(left, right, (((1,), (1,)), ((), ())), preferred_element_type=F32)


def nn(left, right):
    return lax.dot_general(left, right, (((1,), (0,)), ((), ())), preferred_element_type=F32)


def image_mean(sums, group):
    width = C // GROUPS
    row = lax.broadcasted_iota(jnp.int32, (C, C), 0) // width
    col = lax.broadcasted_iota(jnp.int32, (C, C), 1) // width
    same_group = (row == col).astype(F32)
    left = lax.broadcasted_iota(jnp.int32, (16, 16), 0)
    right = lax.broadcasted_iota(jnp.int32, (16, 16), 1)
    same_image = (((left >> 2) >> group) == ((right >> 2) >> group)) & (
        ((left & 3) >> group) == ((right & 3) >> group)
    )
    side = 8 << group
    count = (side * side * width).astype(F32)
    spread = lax.dot_general(
        sums, same_group, (((1,), (0,)), ((), ())), precision=HIGH, preferred_element_type=F32
    )
    total = lax.dot_general(
        same_image.astype(F32), spread, (((1,), (0,)), ((), ())), precision=HIGH, preferred_element_type=F32
    )
    return total / count


def tile_rows(block):
    return jnp.sum(block.reshape(4, 8, C), axis=1)


def spread_rows(ref, tiles):
    for ty in range(4):
        for tx in range(4):
            t = 4 * ty + tx
            ref[ty, 8 * tx : 8 * tx + 8, :] = jnp.broadcast_to(tiles[t : t + 1, :], (8, C))


def norm_stats(x_ref, group, mean_ref, rstd_ref):
    parts = []
    for ty in range(4):
        acc = x_ref[pl.ds(ty * 256, 32), :]
        for y in range(1, 8):
            acc = acc + x_ref[pl.ds(ty * 256 + y * 32, 32), :]
        parts.append(tile_rows(acc))
    spread_rows(mean_ref, image_mean(jnp.concatenate(parts, axis=0), group))
    parts = []
    for ty in range(4):
        mu = mean_ref[ty]
        acc = jnp.zeros((32, C), F32)
        for y in range(8):
            cen = x_ref[pl.ds(ty * 256 + y * 32, 32), :] - mu
            acc = acc + cen * cen
        parts.append(tile_rows(acc))
    var = image_mean(jnp.concatenate(parts, axis=0), group)
    spread_rows(rstd_ref, lax.rsqrt(var + 1e-05))


def store_shifts(ref, y, val, side):
    x = lax.broadcasted_iota(jnp.int32, (32, C), 0) & (side - 1)
    zero = jnp.zeros((32, C), F32)
    left = jnp.where(x != 0, pltpu.roll(val, 1, 0), zero)
    right = jnp.where(x != side - 1, pltpu.roll(val, 31, 0), zero)
    rows = pl.ds(pl.multiple_of(PAD + y * 32, 32), 32)
    ref[rows, 0:C] = left.astype(BF16)
    ref[rows, C : 2 * C] = val.astype(BF16)
    ref[rows, 2 * C : 3 * C] = right.astype(BF16)


def clear_pads(ref):
    ref[0:PAD, :] = jnp.zeros((PAD, 3 * C), BF16)
    ref[PAD + ROWS : 2 * PAD + ROWS, :] = jnp.zeros((PAD, 3 * C), BF16)


def row_mask(shape, dim, dy, side):
    y = (lax.broadcasted_iota(jnp.int32, shape, dim) // 32) & (side - 1)
    return y != 0 if dy < 0 else y != side - 1


SHARD = 64
RES = (("mat", 0, 1152),)
MIX = (("mat", 0, 512), ("mat", 512, 512), ("lat", 1024, 128))


def part_shapes(kind, lanes, z_size, dtype):
    rows = 2 * SHARD * z_size
    if kind == "mat":
        return [((rows, 4 * lanes), dtype)]
    if kind == "lat":
        return [((rows // 2, 4 * lanes), dtype)] * 2
    return [((4, rows, lanes), dtype)]


def part_blocks(kind, refs, lanes, dp, f):
    cols = pl.ds(pl.multiple_of(f * lanes, 128), lanes)
    if kind == "lat":
        half = SHARD // 2
        at = pl.ds(pl.multiple_of(dp * half, half), half)
        return [(pl.ds(i * half, half), refs[i].at[at, cols]) for i in range(2)]
    at = pl.ds(pl.multiple_of(dp * SHARD, SHARD), SHARD)
    where = refs[0].at[at, cols] if kind == "mat" else refs[0].at[f, at, :]
    return [(pl.ds(0, SHARD), where)]


def part_count(kind):
    return 2 if kind == "lat" else 1


def copy_count(parts, z_size):
    return 8 * z_size * sum(part_count(kind) for kind, _, _ in parts)


def block_copies(parts, info_ref, pieces, wholes, sems, inward):
    core, f = info_ref[1], info_ref[2]
    z_size = pieces[0][0].shape[0]
    copies = []
    for side in range(2):
        owner = core if side == 0 else 1 - core
        for far in range(2):
            for near in range(2):
                for z in range(z_size):
                    at_f = f ^ ((2 - owner) * near) ^ ((1 + owner) * far)
                    at_dp = 2 * z + owner
                    first = 0
                    for kind, lane, lanes in parts:
                        refs = wholes[first : first + part_count(kind)]
                        for rows, where in part_blocks(kind, refs, lanes, at_dp, at_f):
                            piece = pieces[side][2 * far + near].at[z, rows, pl.ds(lane, lanes)]
                            ends = (piece, where) if inward else (where, piece)
                            copies.append(pltpu.make_async_copy(*ends, sems.at[len(copies)]))
                        first += part_count(kind)
    return copies


def quarters(*refs):
    return [[ref.at[pl.ds(k * (ref.shape[0] // 4), ref.shape[0] // 4)] for k in range(4)] for ref in refs]


def weight_copies(info_ref, refs, dst_ref, sems):
    if len(refs) == 1:
        return [pltpu.make_async_copy(refs[0], dst_ref, sems.at[0])]
    return block_copies(RES, info_ref, (refs[:4], refs[4:]), (dst_ref,), sems, True)


def weight_sems(weight):
    return pltpu.SemaphoreType.DMA((1 if len(weight) == 1 else copy_count(RES, weight[0].shape[0]),))


def conv_fwd_kernel(n_weight, has_res, info_ref, x_ref, gain_ref, *rest):
    weight, rest = rest[:n_weight], rest[n_weight:]
    if has_res:
        res_ref, *rest = rest
    t_ref, a3_ref, wt_ref, mean_ref, rstd_ref, sems = rest
    copies = weight_copies(info_ref, weight, wt_ref, sems)
    for copy in copies:
        copy.start()
    group = info_ref[0]
    side = 8 << group
    norm_stats(x_ref, group, mean_ref, rstd_ref)
    clear_pads(a3_ref)
    gamma = gain_ref[0:1, :]
    beta = gain_ref[1:2, :]

    def body(y, carry):
        ty = y // 8
        v = (x_ref[pl.ds(pl.multiple_of(y * 32, 32), 32), :] - mean_ref[ty]) * rstd_ref[ty] * gamma + beta
        store_shifts(a3_ref, y, v * sigmoid(v), side)
        return carry

    lax.fori_loop(0, 32, body, 0, unroll=4)
    for copy in copies:
        copy.wait()
    out = nt(a3_ref[PAD : PAD + ROWS, :], wt_ref[:, 3 * C : 6 * C])
    if has_res:
        out = out + res_ref[...]
    t_ref[...] = out
    for dy in (-1, 1):
        part = nt(a3_ref[PAD + 32 * dy : PAD + 32 * dy + ROWS, :], wt_ref[:, (dy + 1) * 3 * C : (dy + 2) * 3 * C])
        t_ref[...] += jnp.where(row_mask((ROWS, 1), 0, dy, side), part, 0.0)


SMEM = pl.BlockSpec(memory_space=pltpu.SMEM)
VM = pl.BlockSpec(memory_space=pltpu.VMEM)
ANY = pl.BlockSpec(memory_space=pl.ANY)
PARAMS = pltpu.CompilerParams(vmem_limit_bytes=VMEM_LIMIT)
CONV_FLOPS = 2 * ROWS * 9 * C * C


def cost(flops, size):
    return pl.CostEstimate(flops=flops, bytes_accessed=size, transcendentals=0)


def conv_fwd(info, x, gains, weight, res=None):
    args = [info, x, gains, *weight] + ([] if res is None else [res])
    return pl.pallas_call(
        functools.partial(conv_fwd_kernel, len(weight), res is not None),
        out_shape=(
            jax.ShapeDtypeStruct((ROWS, C), F32),
            jax.ShapeDtypeStruct((ROWS + 2 * PAD, 3 * C), BF16),
        ),
        in_specs=[SMEM, VM, VM] + [ANY] * len(weight) + ([] if res is None else [VM]),
        out_specs=(VM, VM),
        scratch_shapes=[
            pltpu.VMEM((C, 9 * C), BF16),
            pltpu.VMEM((4, 32, C), F32),
            pltpu.VMEM((4, 32, C), F32),
            weight_sems(weight),
        ],
        compiler_params=PARAMS,
        cost_estimate=cost(2 * CONV_FLOPS, 12 << 20),
        name="conv_fwd",
    )(*args)


def conv_dw_kernel(split, info_ref, dt_ref, a3_ref, *rest):
    if split:
        keep_ref, send_ref, dw_ref, dtt_ref, sems = rest
    else:
        dw_ref, dtt_ref = rest
    side = 8 << info_ref[0]
    dtt_ref[1] = dt_ref[...].astype(F32).T.astype(BF16)
    flat = dtt_ref[1]
    for dy in (-1, 1):
        keep = row_mask((1, ROWS), 1, dy, side).astype(BF16)
        dtt_ref[dy + 1] = flat * keep
    for dy in (-1, 0, 1):
        dw = nn(dtt_ref[dy + 1], a3_ref[PAD + 32 * dy : PAD + 32 * dy + ROWS, :])
        dw_ref[:, (dy + 1) * 3 * C : (dy + 2) * 3 * C] = dw.astype(dw_ref.dtype)
    if split:
        copies = block_copies(RES, info_ref, quarters(keep_ref, send_ref), (dw_ref,), sems, False)
        for copy in copies:
            copy.start()
        for copy in copies:
            copy.wait()


def conv_dw(info, dt, a3, z_size):
    scratch = [pltpu.VMEM((3, C, ROWS), BF16)]
    if z_size:
        block = jax.ShapeDtypeStruct((4 * z_size, SHARD, 9 * C // 4), BF16)
        shapes, specs = (block, block), (ANY, ANY)
        scratch = [pltpu.VMEM((C, 9 * C), BF16)] + scratch + [pltpu.SemaphoreType.DMA((copy_count(RES, z_size),))]
    else:
        shapes, specs = jax.ShapeDtypeStruct((C, 9 * C), F32), VM
    return pl.pallas_call(
        functools.partial(conv_dw_kernel, z_size),
        out_shape=shapes,
        in_specs=[SMEM, VM, VM],
        out_specs=specs,
        scratch_shapes=scratch,
        compiler_params=PARAMS,
        cost_estimate=cost(2 * CONV_FLOPS, 12 << 20),
        name="conv_dw",
    )(info, dt, a3)


def conv_dx_kernel(n_weight, has_res, info_ref, dt_ref, x_ref, gain_ref, *rest):
    weight, rest = rest[:n_weight], rest[n_weight:]
    if has_res:
        res_ref, *rest = rest
    dx_ref, dgain_ref, wt_ref, d3_ref, mean_ref, rstd_ref, ds_ref, sems = rest
    copies = weight_copies(info_ref, weight, wt_ref, sems)
    for copy in copies:
        copy.start()
    group = info_ref[0]
    side = 8 << group
    clear_pads(d3_ref)

    def body(y, carry):
        val = dt_ref[pl.ds(pl.multiple_of(y * 32, 32), 32), :].astype(F32)
        store_shifts(d3_ref, y, val, side)
        return carry

    lax.fori_loop(0, 32, body, 0, unroll=4)
    norm_stats(x_ref, group, mean_ref, rstd_ref)
    for copy in copies:
        copy.wait()
    for dy in (0, -1, 1):
        part = None
        for dx in (-1, 0, 1):
            t = 3 * (dy + 1) + dx + 1
            one = nn(
                d3_ref[PAD - 32 * dy : PAD - 32 * dy + ROWS, (1 - dx) * C : (2 - dx) * C],
                wt_ref[:, t * C : (t + 1) * C],
            )
            part = one if part is None else part + one
        if dy == 0:
            ds_ref[...] = part
        else:
            ds_ref[...] += jnp.where(row_mask((ROWS, 1), 0, -dy, side), part, 0.0)
    gamma = gain_ref[0:1, :]
    beta = gain_ref[1:2, :]
    first, second = [], []
    for ty in range(4):
        mu, rs = mean_ref[ty], rstd_ref[ty]

        def step(y, carry, ty=ty, mu=mu, rs=rs):
            one, two = carry
            rows = pl.ds(pl.multiple_of(ty * 256 + y * 32, 32), 32)
            xh = (x_ref[rows, :] - mu) * rs
            v = xh * gamma + beta
            sg = sigmoid(v)
            ds = ds_ref[rows, :] * (sg * (1.0 + v * (1.0 - sg)))
            ds_ref[rows, :] = ds
            return (one + ds, two + ds * xh)

        zero = jnp.zeros((32, C), F32)
        one, two = lax.fori_loop(0, 8, step, (zero, zero), unroll=2)
        first.append(tile_rows(one))
        second.append(tile_rows(two))
    first = jnp.concatenate(first, axis=0)
    second = jnp.concatenate(second, axis=0)
    dgain_ref[0:1, :] = jnp.sum(second, axis=0, keepdims=True)
    dgain_ref[1:2, :] = jnp.sum(first, axis=0, keepdims=True)
    m_one = image_mean(first * gamma, group)
    m_two = image_mean(second * gamma, group)
    for ty in range(4):
        mu, rs = mean_ref[ty], rstd_ref[ty]
        one = jnp.concatenate([jnp.broadcast_to(m_one[4 * ty + tx : 4 * ty + tx + 1, :], (8, C)) for tx in range(4)], axis=0)
        two = jnp.concatenate([jnp.broadcast_to(m_two[4 * ty + tx : 4 * ty + tx + 1, :], (8, C)) for tx in range(4)], axis=0)

        def step(y, carry, ty=ty, mu=mu, rs=rs, one=one, two=two):
            rows = pl.ds(pl.multiple_of(ty * 256 + y * 32, 32), 32)
            xh = (x_ref[rows, :] - mu) * rs
            dx = rs * (ds_ref[rows, :] * gamma - one - xh * two)
            if has_res:
                dx = dx + res_ref[rows, :]
            dx_ref[rows, :] = dx.astype(dx_ref.dtype)
            return carry

        lax.fori_loop(0, 8, step, 0, unroll=2)


def conv_dx(info, dt, x, gains, weight, res=None, low=True):
    args = [info, dt, x, gains, *weight] + ([] if res is None else [res])
    return pl.pallas_call(
        functools.partial(conv_dx_kernel, len(weight), res is not None),
        out_shape=(
            jax.ShapeDtypeStruct((ROWS, C), BF16 if low else F32),
            jax.ShapeDtypeStruct((2, C), F32),
        ),
        in_specs=[SMEM, VM, VM, VM] + [ANY] * len(weight) + ([] if res is None else [VM]),
        out_specs=(VM, VM),
        scratch_shapes=[
            pltpu.VMEM((C, 9 * C), BF16),
            pltpu.VMEM((ROWS + 2 * PAD, 3 * C), BF16),
            pltpu.VMEM((4, 32, C), F32),
            pltpu.VMEM((4, 32, C), F32),
            pltpu.VMEM((ROWS, C), F32),
            weight_sems(weight),
        ],
        compiler_params=PARAMS,
        cost_estimate=cost(3 * CONV_FLOPS, 12 << 20),
        name="conv_dx",
    )(*args)


def silu_slope(value):
    gate = sigmoid(value)
    return gate * (1.0 + value * (1.0 - gate))


def transposed(value):
    return value.astype(F32).T.astype(BF16)


HALF = SIDE // 2
LAT = HALF * HALF


def to_depth(src_ref, lanes_ref, dst_ref):
    for k in range(C // 128):
        lanes_ref[k] = src_ref[:, k * 128 : (k + 1) * 128]
    for k in range(C // 128):
        for b in range(2):
            block = lanes_ref[k, pl.ds(b, ROWS // 2, stride=2), :].reshape(HALF, 2, HALF, 128)
            for a in range(2):
                at = (2 * a + b) * C + k * 128
                dst_ref[:, at : at + 128] = block[:, a].reshape(LAT, 128).astype(dst_ref.dtype)


def from_depth(src_ref, lanes_ref, dst_ref):
    for k in range(C // 128):
        for b in range(2):
            pair = [
                src_ref[:, (2 * a + b) * C + k * 128 : (2 * a + b) * C + (k + 1) * 128].reshape(HALF, 1, HALF, 128)
                for a in range(2)
            ]
            lanes_ref[k, pl.ds(b, ROWS // 2, stride=2), :] = jnp.concatenate(pair, axis=1).reshape(ROWS // 2, 128)
    for k in range(C // 128):
        dst_ref[:, k * 128 : (k + 1) * 128] = lanes_ref[k]


def mid_fwd_kernel(
    h_ref, ws0_ref, wl0_ref, code_ref, wl1_ref, ws1_ref,
    e_ref, d_ref, s_ref, q_ref, y_ref, s2_ref, g_ref, commit_ref, dcom_ref, resid_ref, u_ref, lanes_ref,
):
    to_depth(h_ref, lanes_ref, e_ref)
    d = nt(e_ref[...], ws0_ref[...])
    d_ref[...] = d
    s = (d * sigmoid(d)).astype(BF16)
    s_ref[...] = s
    z = nt(s, wl0_ref[...])
    q = jnp.zeros((LAT, ZD), F32)
    commit = jnp.zeros((LAT, ZD), F32)
    dcom = jnp.zeros((LAT, ZD), F32)
    for k in range(4):
        resid_ref[k * LAT : (k + 1) * LAT, :] = (z - q).astype(BF16)
        q = q + code_ref[k * LAT : (k + 1) * LAT, :].astype(F32)
        diff = z - q
        commit = commit + diff * diff
        dcom = dcom + diff
    commit_ref[...] = jnp.sum(commit, axis=0, keepdims=True)
    dcom_ref[...] = dcom
    quant = (z + (q - z)).astype(BF16)
    q_ref[...] = quant
    y = nn(quant, wl1_ref[...])
    y_ref[...] = y
    s2 = (y * sigmoid(y)).astype(BF16)
    s2_ref[...] = s2
    u_ref[...] = nn(s2, ws1_ref[...])
    from_depth(u_ref, lanes_ref, g_ref)


def mid_fwd(h, ws0, wl0, codes, wl1, ws1):
    shape = jax.ShapeDtypeStruct
    return pl.pallas_call(
        mid_fwd_kernel,
        out_shape=(
            shape((LAT, 4 * C), BF16),
            shape((LAT, C), F32),
            shape((LAT, C), BF16),
            shape((LAT, ZD), BF16),
            shape((LAT, C), F32),
            shape((LAT, C), BF16),
            shape((ROWS, C), F32),
            shape((1, ZD), F32),
            shape((LAT, ZD), F32),
            shape((4 * LAT, ZD), BF16),
        ),
        in_specs=[VM] * 6,
        out_specs=(VM,) * 10,
        scratch_shapes=[pltpu.VMEM((LAT, 4 * C), F32), pltpu.VMEM((C // 128, ROWS, 128), F32)],
        compiler_params=PARAMS,
        cost_estimate=cost(4 << 30, 12 << 20),
        name="mid_fwd",
    )(h, ws0, wl0, codes, wl1, ws1)


def mid_bwd_kernel(
    split, scale, info_ref, dg_ref, e_ref, d_ref, s_ref, q_ref, y_ref, s2_ref, dcom_ref, ws0_ref, wl0_ref, wl1_ref,
    ws1_ref, *rest,
):
    if split:
        keep_ref, send_ref, dh_ref, *wholes, du_ref, de_ref, lanes_ref, sems = rest
    else:
        *wholes, dh_ref, du_ref, de_ref, lanes_ref = rest
    dws0_ref, dws1_ref, dwl0_ref, dwl1_ref = wholes
    to_depth(dg_ref, lanes_ref, du_ref)
    out = dws0_ref.dtype
    ds2 = nt(du_ref[...], ws1_ref[...])
    dy = (ds2 * silu_slope(y_ref[...])).astype(BF16)
    dws1_ref[...] = nn(transposed(s2_ref[...]), du_ref[...]).astype(out)
    dwl1_ref[...] = nn(transposed(q_ref[...]), dy).astype(out)
    dz = (nt(dy, wl1_ref[...]) + scale * dcom_ref[...]).astype(BF16)
    dwl0_ref[...] = nn(transposed(dz), s_ref[...]).astype(out)
    ds = nn(dz, wl0_ref[...])
    dd = (ds * silu_slope(d_ref[...])).astype(BF16)
    dws0_ref[...] = nn(transposed(dd), e_ref[...]).astype(out)
    copies = []
    if split:
        copies = block_copies(MIX, info_ref, quarters(keep_ref, send_ref), wholes, sems, False)
    for copy in copies:
        copy.start()
    de_ref[...] = nn(dd, ws0_ref[...])
    from_depth(de_ref, lanes_ref, dh_ref)
    for copy in copies:
        copy.wait()


def mid_bwd(info, scale, dg, e, d, s, q, y, s2, dcom, ws0, wl0, wl1, ws1, z_size):
    shape = jax.ShapeDtypeStruct
    wholes = [(C, 4 * C), (C, 4 * C), (ZD, C), (ZD, C)]
    scratch = [
        pltpu.VMEM((LAT, 4 * C), BF16),
        pltpu.VMEM((LAT, 4 * C), F32),
        pltpu.VMEM((C // 128, ROWS, 128), F32),
    ]
    field = shape((ROWS, C), F32)
    if z_size:
        block = shape((4 * z_size, SHARD, 1152), BF16)
        shapes, specs = (block, block, field), (ANY, ANY, VM)
        scratch = [pltpu.VMEM(one, BF16) for one in wholes] + scratch
        scratch += [pltpu.SemaphoreType.DMA((copy_count(MIX, z_size),))]
    else:
        shapes, specs = tuple(shape(one, F32) for one in wholes) + (field,), (VM,) * 5
    out = pl.pallas_call(
        functools.partial(mid_bwd_kernel, z_size, scale),
        out_shape=shapes,
        in_specs=[SMEM] + [VM] * 12,
        out_specs=specs,
        scratch_shapes=scratch,
        compiler_params=PARAMS,
        cost_estimate=cost(4 << 30, 12 << 20),
        name="mid_bwd",
    )(info, dg, e, d, s, q, y, s2, dcom, ws0, wl0, wl1, ws1)
    return out[-1], out[:-1]


def head_kernel(total_ref, g_ref, wp_ref, pix_ref, mask_ref, dw_ref, dg_ref, loss_ref, o_ref, dr_ref):
    inv = total_ref[0]
    loss = jnp.zeros((1, pix_ref.shape[1]), F32)
    for i in range(4):
        rows = pl.ds(i * 256, 256)
        g = g_ref[rows, :]
        gate = sigmoid(g)
        o = (g * gate).astype(BF16)
        o_ref[rows, :] = o
        err = nn(o, wp_ref[...]) - pix_ref[rows, :].astype(F32)
        keep = mask_ref[rows, :].astype(F32)
        smooth = jnp.sqrt(err * err + 1.0)
        loss = loss + jnp.sum(keep * (smooth - 1.0), axis=0, keepdims=True)
        dr = (keep * err / smooth / inv).astype(BF16)
        dr_ref[rows, :] = dr
        do = nt(dr, wp_ref[...])
        dg_ref[rows, :] = do * (gate * (1.0 + g * (1.0 - gate)))
    loss_ref[...] = loss
    dw_ref[...] = nn(transposed(o_ref[...]), dr_ref[...]).astype(dw_ref.dtype)


def head(total, g, wp, pix, mask, grad_type=BF16):
    shape = jax.ShapeDtypeStruct
    width = pix.shape[1]
    return pl.pallas_call(
        head_kernel,
        out_shape=(shape((C, width), grad_type), shape((ROWS, C), F32), shape((1, width), F32)),
        in_specs=[SMEM, VM, VM, VM, VM],
        out_specs=(VM,) * 3,
        scratch_shapes=[pltpu.VMEM((ROWS, C), BF16), pltpu.VMEM((ROWS, width), BF16)],
        compiler_params=PARAMS,
        cost_estimate=cost(6 << 30, 12 << 20),
        name="head",
    )(total, g, wp, pix, mask)


BOTH = ("z", "core", "fsdp")
COLS = ("z", "core")


def swap(shard):
    return jnp.swapaxes(shard, -1, -2).astype(BF16)


def across(x, near):
    n = lax.axis_size("fsdp")
    masks = (2, 1) if near else (1, 2)
    return lax.ppermute(x, ("core", "fsdp"), [(c * n + f, c * n + (f ^ masks[c])) for c in range(2) for f in range(n)])


def partner(x):
    return lax.ppermute(x, "core", [(0, 1), (1, 0)])


def everyone(x):
    n = lax.axis_size("z") * lax.axis_size("core") * lax.axis_size("fsdp")
    return lax.all_to_all(jnp.broadcast_to(x[None], (n,) + x.shape), BOTH, 0, 0, tiled=True)


def along_z(x, step):
    n = lax.axis_size("z")
    return lax.ppermute(x, "z", [(i, i ^ step) for i in range(n)])


def shuffle(x, axis):
    return lax.all_to_all(x, axis, 0, 0, tiled=True)


def assemble_kernel(parts, info_ref, *rest):
    copies = block_copies(parts, info_ref, (rest[:4], rest[4:8]), rest[8:-1], rest[-1], True)
    for copy in copies:
        copy.start()
    for copy in copies:
        copy.wait()


def assemble(info, pieces, parts):
    z_size = pieces[0].shape[0]
    shapes = [s for kind, _, lanes in parts for s in part_shapes(kind, lanes, z_size, BF16)]
    return pl.pallas_call(
        functools.partial(assemble_kernel, parts),
        out_shape=tuple(jax.ShapeDtypeStruct(*s) for s in shapes),
        in_specs=[SMEM] + [ANY] * 8,
        out_specs=(VM,) * len(shapes),
        scratch_shapes=[pltpu.SemaphoreType.DMA((copy_count(parts, z_size),))],
        compiler_params=PARAMS,
        cost_estimate=cost(1 << 30, 10 << 20),
        name="assemble",
    )(info, *pieces)


def gather_all(shards, others, slow):
    z_size = lax.axis_size("z")
    count = len(shards)
    shards = list(shards)
    done = [{} for _ in shards]
    pieces, later, side, waiting, early = {}, {}, {}, {}, {}
    groups = [(1, 3), (3, count)] if count else []
    bulks = {}
    for first, last in groups:
        bulks[first] = lax.all_gather(jnp.concatenate(shards[first:last], axis=1), "z")
    for step in range(max([count + 2] + list(others)) + 1):
        new = {}
        if 0 <= step - 2 < count:
            new["both", step - 2] = across(done[step - 2]["near"], False)
        if 0 <= step - 1 < count:
            new["far", step - 1] = across(done[step - 1]["z"], False)
            new["near", step - 1] = across(done[step - 1]["z"], True)
        if step < min(count, 1):
            new["z", step] = shuffle(jnp.broadcast_to(shards[step][None], (z_size,) + shards[step].shape), "z")
        for i, (first, last) in enumerate(groups):
            if step == i + 1:
                new["bulk", first] = bulks[first]
        for j in list(early):
            new["z", j] = early.pop(j)
        if 0 <= step - 3 < count:
            own = [done[step - 3][name] for name in ("z", "near", "far", "both")]
            new["core", step - 3] = [partner(one) for one in own]
            pieces[step - 3] = (*own, *new["core", step - 3])
        if step in slow:
            due, function = slow[step]
            waiting[due] = function(pieces, side)
        if step in waiting:
            side = {**side, **waiting.pop(step)}
        if step in others:
            side = {**side, **others[step](pieces, side)}
        names = list(new)
        values, shards[step + 1 :], side = lax.optimization_barrier((list(new.values()), shards[step + 1 :], side))
        for (name, i), value in zip(names, values):
            done[i][name] = value
        for i, (first, last) in enumerate(groups):
            if step == i + 1:
                at = 0
                for j in range(first, last):
                    z_slice = done[first]["bulk"][:, :, at : at + shards[j].shape[1]]
                    at += shards[j].shape[1]
                    if j <= step:
                        done[j]["z"] = z_slice
                    else:
                        early[j] = z_slice
        if 0 <= step - 3 < count:
            later[step - 3] = (*[done[step - 3][name] for name in ("z", "near", "far", "both")], *done[step - 3]["core"])
    return later, side


def add_up(parts):
    total = parts[0].astype(F32)
    for part in parts[1:]:
        total = total + part.astype(F32)
    return total


class Slow:
    def __init__(self, value):
        self.value = value


def scatter_stages(keep, send, tie, bulk, out):
    half = keep.shape[0] // 2
    keep, got = yield keep, partner(send)
    parts = [keep, got]
    for near in (False, True):
        away = add_up([p[half : 2 * half] for p in parts]).astype(BF16)
        if near and tie:
            away, tie[0] = lax.optimization_barrier((away, tie[0]))
        *parts, got = yield *parts, across(away, near)
        parts.append(got)
        half = half // 2
    sums = add_up([p[: 2 * half] for p in parts]).astype(BF16)
    if bulk:
        got = yield Slow(lax.psum_scatter(sums, "z", scatter_dimension=0))
        out.append(got.astype(F32))
    else:
        got = yield shuffle(sums, "z")
        out.append(jnp.sum(got.astype(F32), axis=0))


def scatter_pair(blocks, out):
    got = yield shuffle(blocks, ("core", "fsdp"))
    sums = jnp.sum(got.astype(F32), axis=0)
    me = lax.axis_index("z")
    away = [along_z(lax.dynamic_index_in_dim(sums, me ^ k, keepdims=False).astype(BF16), k) for k in range(1, sums.shape[0])]
    away = yield away
    out.append(add_up([lax.dynamic_index_in_dim(sums, me, keepdims=False)] + away))


def scatter_direct(blocks, out):
    got = yield shuffle(blocks, BOTH)
    out.append(jnp.sum(got.astype(F32), axis=0))


class Overlap:
    def __init__(self):
        self.live = []

    def add(self, stages, *args, late=0):
        out = []
        stages = stages(*args, out)
        self.live.append((stages, next(stages), late))
        return out

    def finish(self):
        for stages, value, _ in self.live:
            try:
                while True:
                    value = stages.send(value.value if isinstance(value, Slow) else value)
            except StopIteration:
                pass
        self.live = []

    def push(self, values):
        stages, value, _ = self.live[-1]
        values, value = lax.optimization_barrier((values, value))
        self.live[-1] = (stages, stages.send(value), 0)
        return values

    def step(self, values, use=None):
        due = [value for _, value, late in self.live if not late]
        values, due = lax.optimization_barrier((values, due))
        if use is not None:
            use(values)
        live, at = [], 0
        for stages, value, late in self.live:
            if late:
                live.append((stages, value, late - 1))
                continue
            try:
                value = stages.send(due[at])
                live.append((stages, value.value, 1) if isinstance(value, Slow) else (stages, value, 0))
            except StopIteration:
                pass
            at += 1
        self.live = live
        return values


def fetch_whole(shard):
    cols = lax.all_gather(shard.astype(BF16), COLS, axis=1, tiled=True)
    return jnp.swapaxes(lax.all_gather(cols, "fsdp", axis=0, tiled=True), 0, 1)


def reduce_whole(grad):
    rows = lax.psum_scatter(jnp.swapaxes(grad, 0, 1), "fsdp", scatter_dimension=0, tiled=True)
    return jnp.swapaxes(lax.psum_scatter(rows, COLS, scatter_dimension=1, tiled=True), 0, 1)


def widen(block, width):
    return jnp.pad(block, ((0, 0),) * (block.ndim - 1) + ((0, width - block.shape[-1]),))


def pix_matrix(blocks, width):
    return blocks[:, :, :width].transpose(1, 0, 2).reshape(C, 4 * width)


def pix_blocks(matrix, shard):
    rows, cols = shard
    return matrix.reshape(-1, cols, matrix.shape[1] // rows, rows).transpose(0, 2, 1, 3).reshape(-1, cols, rows)


def adam_step(weight, moment, second, grad, rate):
    moment_new = 0.5 * moment + 0.5 * grad
    second_new = 0.5 * second + 0.5 * grad * grad
    fix = 1.0 - 0.5**STEP
    weight_new = weight - rate * (
        moment_new / fix / (jnp.sqrt(second_new / fix) + 1e-12) + 0.01 * weight
    )
    return (weight_new, moment_new, second_new)


def small_blocks(values, devices):
    flat = jnp.concatenate([value.reshape(-1) for value in values])
    lanes = -(-flat.shape[0] // (128 * devices)) * 128
    return jnp.pad(flat, (0, devices * lanes - flat.shape[0])).reshape(devices, 1, lanes)


def exact(left, right, dims):
    return lax.dot_general(left, right, (dims, ((), ())), preferred_element_type=F32)


def code_slots(codes, devices, capacity, rows):
    n = codes.shape[0]
    owner = codes // rows
    hot = (owner[:, None] == jnp.arange(devices, dtype=jnp.int32)[None, :]).astype(BF16)
    at = jnp.arange(n, dtype=jnp.int32)
    before = (at[None, :] < at[:, None]).astype(BF16)
    rank = exact(before, hot, ((1,), (0,)))
    place = jnp.sum(rank * hot.astype(F32), axis=1).astype(jnp.int32)
    slot = owner * capacity + place
    return (jnp.arange(devices * capacity, dtype=jnp.int32)[:, None] == slot[None, :]).astype(BF16)


def on_device(
    pixels,
    valid_mask,
    size_groups,
    code_index,
    w_pixel,
    w_res,
    w_scale,
    w_latent,
    norm_gains,
    moment_pixel,
    moment_res,
    moment_scale,
    moment_latent,
    moment_gains,
    second_pixel,
    second_res,
    second_scale,
    second_latent,
    second_gains,
    ema_counts,
    ema_sums,
):
    n_inner = lax.axis_size("fsdp")
    z_size = lax.axis_size("z")
    devices = 2 * z_size * n_inner
    latent_all = code_index.shape[1] * devices
    rows = ema_sums.shape[0]
    paired = n_inner == 4 and w_res.shape[1] == 1152 and w_res.shape[2] == SHARD
    blocks = z_size if paired else 0
    place = [lax.axis_index("core"), lax.axis_index("fsdp")]
    info = jnp.stack([size_groups[0]] + [one.astype(jnp.int32) for one in place])

    codes = code_index.reshape(-1)
    capacity = max(2, 2 * codes.shape[0] // devices)
    pick = code_slots(codes, devices, capacity, rows)
    local = codes % rows
    cols = jnp.stack([local // 16, local % 16, jnp.ones_like(local)], axis=1).astype(BF16)
    want = exact(pick, cols, ((1,), (0,)))
    wanted = jnp.where(want[:, 2] > 0.5, want[:, 0] * 16.0 + want[:, 1], -1.0).astype(jnp.int32)
    book = (ema_sums / ema_counts[:, None]).astype(BF16)
    valid = jnp.sum(valid_mask.astype(F32).reshape(-1, 128), axis=0, keepdims=True)

    def row_hot(asked):
        return (asked[:, None] == jnp.arange(rows, dtype=jnp.int32)[None, :]).astype(BF16)

    def prepare(pieces, side):
        wide = -(-capacity // 128) * 128
        request = widen(wanted.astype(F32).reshape(devices, 1, capacity), wide)
        count = jnp.broadcast_to(widen(valid, wide)[None], (devices, 1, wide))
        return {"request": jnp.concatenate([request, count], axis=1)}

    def ask(pieces, side):
        got = shuffle(side["request"], BOTH)
        return {"asked": got[:, 0, :capacity].reshape(-1).astype(jnp.int32), "count": jnp.sum(got[:, 1])}

    def answer(side):
        return {"answer": exact(row_hot(side["asked"]), book, ((1,), (0,))).astype(BF16)}

    def reply(pieces, side):
        return {"replies": shuffle(side["answer"].reshape(devices, capacity, ZD), BOTH)}

    gains = [jnp.stack([norm_gains[j], norm_gains[4 + j]]) for j in range(4)]
    width = w_pixel.shape[1]

    def run_conv0(pieces, side):
        if paired:
            (pix,) = assemble(info, pieces[0], (("pix", RES[0][2], 256),))
            h0 = nt(pixels, pix_matrix(pix, width))
            weight = pieces[0]
        else:
            h0 = nt(pixels, fetch_whole(w_pixel[0]))
            weight = (fetch_whole(w_res[0]),)
        t1, a1 = conv_fwd(info, h0, gains[0], weight)
        return {**answer(side), "h0": h0, "t1": t1, "a1": a1, **({} if paired else {"res0": weight})}

    def run_conv1(pieces, side):
        weight = pieces[1] if paired else (fetch_whole(w_res[1]),)
        h1, a2 = conv_fwd(info, side["t1"], gains[1], weight, side["h0"])
        return {"h1": h1, "a2": a2, **({} if paired else {"res1": weight})}

    def run_mid(pieces, side):
        if paired:
            mats = assemble(info, pieces[2], MIX)
        else:
            mats = [fetch_whole(w_scale[i]) for i in range(2)] + [fetch_whole(w_latent[i]) for i in range(2)]
        scale0, scale1, lat0, lat1 = mats
        picked = exact(pick, side["replies"].reshape(-1, ZD), ((0,), (0,))).astype(BF16)
        return {"mid": mid_fwd(side["h1"], scale0, lat0, picked, lat1, scale1), "mats": mats}

    def run_conv2(pieces, side):
        weight = pieces[3] if paired else (fetch_whole(w_res[2]),)
        t3, a3 = conv_fwd(info, side["mid"][6], gains[2], weight)
        return {"t3": t3, "a3": a3, **({} if paired else {"res2": weight})}

    def run_conv3(pieces, side):
        sent = exact(pick, side["mid"][9], ((1,), (0,))).astype(BF16)
        held = shuffle(sent.reshape(devices, capacity, ZD), BOTH)
        if paired:
            (pix,) = assemble(info, pieces[4], (("pix", RES[0][2], 256),))
            pix = pix_matrix(pix, width)
            weight = pieces[4]
        else:
            pix, weight = fetch_whole(w_pixel[1]), (fetch_whole(w_res[3]),)
        g1, a4 = conv_fwd(info, side["t3"], gains[3], weight, side["mid"][6])
        out = BF16 if paired else F32
        d_head, dg1, loss = head(side["count"].reshape(1), g1, pix, pixels, valid_mask, out)
        return {"held": held, "a4": a4, **({} if paired else {"res3": weight}), "d_head": d_head, "dg1": dg1, "loss": loss}

    others = {0: prepare, 2: ask, 3: run_conv0, 4: run_conv1, 5: run_mid, 6: run_conv2, 7: run_conv3}
    shards = []
    if paired:
        first = jnp.concatenate([swap(w_res[0]), widen(swap(w_pixel[0]), 256)], axis=1)
        first, res, pix, scale, latent = lax.optimization_barrier((first, w_res, w_pixel, w_scale, w_latent))
        scale, latent = swap(scale), swap(latent)
        mix = jnp.concatenate([scale[0], scale[1], latent.reshape(-1, latent.shape[2])], axis=1)
        last = jnp.concatenate([swap(res[3]), widen(swap(pix[1]), 256)], axis=1)
        shards = [first, swap(res[1]), mix, swap(res[2]), last]
    pieces, side = gather_all(shards, others, {4: (5, reply)})
    total_valid = side["count"]
    e, d, s, quant, y, s2, g0, commit, dcom, _ = side["mid"]
    h0, t1, a1, h1, a2, t3, a3, a4 = [side[name] for name in ("h0", "t1", "a1", "h1", "a2", "t3", "a3", "a4")]
    res_w = [pieces[i] for i in (0, 1, 3, 4)] if paired else [side[name] for name in ("res0", "res1", "res2", "res3")]
    scale0, scale1, lat0, lat1 = side["mats"]
    d_head, dg1, loss = side["d_head"], side["dg1"], side["loss"]

    hot_rows = row_hot(side["asked"])
    held = side["held"].reshape(-1, ZD)
    my_sums = exact(hot_rows, held, ((0,), (0,)))
    my_counts = jnp.sum(hot_rows.astype(F32), axis=0)
    counts_new = EMA_DECAY * ema_counts + (1.0 - EMA_DECAY) * my_counts
    sums_new = EMA_DECAY * ema_sums + (1.0 - EMA_DECAY) * my_sums
    book_new = sums_new / counts_new[:, None]

    scale = 2.0 * COMMIT_WEIGHT / (latent_all * ZD)
    loss_rows = jnp.stack([jnp.sum(one.reshape(-1, 128), axis=0) for one in (loss, commit)])
    if paired:
        overlap = Overlap()
        shard = w_pixel.shape[1:]
        sum_head = overlap.add(scatter_direct, pix_blocks(d_head, shard), late=2)
        dw, dg1 = overlap.step((conv_dw(info, dg1, a4, z_size), dg1))
        sum_res3 = overlap.add(scatter_stages, *dw, (), True)
        dt3, dn3 = overlap.step(conv_dx(info, dg1, t3, gains[3], res_w[3]))
        dw, dt3 = overlap.step((conv_dw(info, dt3, a3, z_size), dt3))
        sum_res2 = overlap.add(scatter_stages, *dw, (), True)
        dg0, dn2 = overlap.step(conv_dx(info, dt3, g0, gains[2], res_w[2], dg1, False))
        dh1, dw = overlap.step(
            mid_bwd(info, scale, dg0, e, d, s, quant, y, s2, dcom, scale0, lat0, lat1, scale1, z_size)
        )
        sum_mix = overlap.add(scatter_stages, *dw, (), True)
        dw, dh1 = overlap.step((conv_dw(info, dh1, a2, z_size), dh1))
        sum_res1 = overlap.add(scatter_stages, *dw, (), True)
        dh1 = overlap.push(dh1)
        dt1, dn1 = overlap.step(conv_dx(info, dh1, t1, gains[1], res_w[1]))
        dw, dt1 = overlap.step((conv_dw(info, dt1, a1, z_size), dt1))
        tie = []
        sum_res0 = overlap.add(scatter_stages, *dw, tie, True)
        dt1 = overlap.push(dt1)
        _, dn0 = overlap.step(conv_dx(info, dt1, h0, gains[0], res_w[0], dh1), lambda got: tie.append(got[0]))
        d_patch = exact(tie[0], pixels, ((0,), (0,))).astype(BF16)
        d_patch = pix_blocks(d_patch, shard).reshape(z_size, 2 * n_inner, *shard[::-1])
        sum_patch = overlap.add(scatter_pair, d_patch.transpose(1, 0, 2, 3))
        small = overlap.add(scatter_direct, small_blocks([dn0, dn1, dn2, dn3, loss_rows], devices))
        overlap.finish()
        small = small[0]
        grad_pixel = jnp.stack([sum_patch[0], sum_head[0]])
        grad_res = jnp.stack([sum_res0[0], sum_res1[0], sum_res2[0], sum_res3[0]])
        grad_scale = jnp.stack([sum_mix[0][:, :512], sum_mix[0][:, 512:1024]])
        grad_latent = sum_mix[0][:, 1024:].reshape(2, SHARD // 2, -1)
    else:
        d_res3 = conv_dw(info, dg1, a4, 0)
        dt3, dn3 = conv_dx(info, dg1, t3, gains[3], res_w[3])
        d_res2 = conv_dw(info, dt3, a3, 0)
        dg0, dn2 = conv_dx(info, dt3, g0, gains[2], res_w[2], dg1, False)
        dh1, (d_scale0, d_scale1, d_lat0, d_lat1) = mid_bwd(
            info, scale, dg0, e, d, s, quant, y, s2, dcom, scale0, lat0, lat1, scale1, 0
        )
        d_res1 = conv_dw(info, dh1, a2, 0)
        dt1, dn1 = conv_dx(info, dh1, t1, gains[1], res_w[1])
        d_res0 = conv_dw(info, dt1, a1, 0)
        dh0, dn0 = conv_dx(info, dt1, h0, gains[0], res_w[0], dh1)
        d_patch = exact(dh0, pixels, ((0,), (0,)))
        grad_pixel = jnp.stack([reduce_whole(g) for g in (d_patch, d_head)])
        grad_res = jnp.stack([reduce_whole(g) for g in (d_res0, d_res1, d_res2, d_res3)])
        grad_scale = jnp.stack([reduce_whole(g) for g in (d_scale0, d_scale1)])
        grad_latent = jnp.stack([reduce_whole(g) for g in (d_lat0, d_lat1)])
        small = shuffle(small_blocks([dn0, dn1, dn2, dn3, loss_rows], devices), BOTH)
        small = jnp.sum(small, axis=0)

    squares = jnp.sum(grad_pixel * grad_pixel) + jnp.sum(grad_res * grad_res)
    squares = squares + jnp.sum(grad_scale * grad_scale) + jnp.sum(grad_latent * grad_latent)
    shared = everyone(jnp.concatenate([small, jnp.full((1, small.shape[1]), squares, F32)]))
    total_squares = jnp.sum(shared[:, -1, 0])
    sizes = [2 * C] * 4 + [2 * 128]
    every = shared[:, :-1].reshape(-1)[: sum(sizes)]
    dn0, dn1, dn2, dn3, losses = jnp.split(every, [2 * C, 4 * C, 6 * C, 8 * C])
    dn0, dn1, dn2, dn3 = [one.reshape(2, C) for one in (dn0, dn1, dn2, dn3)]
    grad_gains = jnp.stack([dn0[0], dn1[0], dn2[0], dn3[0], dn0[1], dn1[1], dn2[1], dn3[1]])
    smooth_sum, commit_sum = jnp.sum(losses[:128]), jnp.sum(losses[128:])
    total_squares = total_squares + jnp.sum(grad_gains * grad_gains)
    norm = jnp.sqrt(total_squares)
    factor = CLIP_AT / jnp.maximum(norm, CLIP_AT)
    groups_all = [
        (w_pixel, moment_pixel, second_pixel, grad_pixel),
        (w_res, moment_res, second_res, grad_res),
        (w_scale, moment_scale, second_scale, grad_scale),
        (w_latent, moment_latent, second_latent, grad_latent),
    ]
    outputs = [jnp.stack([smooth_sum, total_valid, commit_sum]), norm.reshape(1)]
    for weight, moment, second, grad in groups_all:
        grad = jnp.swapaxes(grad * factor, 1, 2)
        weight_new, moment_new, second_new = adam_step(weight, moment, second, grad, WEIGHT_RATE)
        outputs += [weight_new, moment_new, second_new, weight_new.astype(BF16)]
    outputs += list(adam_step(norm_gains, moment_gains, second_gains, grad_gains * factor, GAIN_RATE))
    outputs += [counts_new, sums_new, book_new, book_new.astype(BF16)]
    return tuple(outputs)


def solution(mesh):
    outer, inner = mesh.shape["dp"], mesh.shape["fsdp"]
    fine = Mesh(mesh.devices.reshape(outer // 2, 2, inner), BOTH)
    placed = (
        P(BOTH, None),
        P(BOTH, None),
        P(BOTH),
        P(None, BOTH),
        P(None, "fsdp", COLS),
        P(None, "fsdp", COLS),
        P(None, "fsdp", COLS),
        P(None, "fsdp", COLS),
        P(),
        P(None, "fsdp", COLS),
        P(None, "fsdp", COLS),
        P(None, "fsdp", COLS),
        P(None, "fsdp", COLS),
        P(),
        P(None, "fsdp", COLS),
        P(None, "fsdp", COLS),
        P(None, "fsdp", COLS),
        P(None, "fsdp", COLS),
        P(),
        P(BOTH),
        P(BOTH, None),
    )
    return jax.shard_map(
        on_device,
        mesh=fine,
        in_specs=placed,
        out_specs=(
            P(),
            P(),
            P(None, "fsdp", COLS),
            P(None, "fsdp", COLS),
            P(None, "fsdp", COLS),
            P(None, "fsdp", COLS),
            P(None, "fsdp", COLS),
            P(None, "fsdp", COLS),
            P(None, "fsdp", COLS),
            P(None, "fsdp", COLS),
            P(None, "fsdp", COLS),
            P(None, "fsdp", COLS),
            P(None, "fsdp", COLS),
            P(None, "fsdp", COLS),
            P(None, "fsdp", COLS),
            P(None, "fsdp", COLS),
            P(None, "fsdp", COLS),
            P(None, "fsdp", COLS),
            P(),
            P(),
            P(),
            P(BOTH),
            P(BOTH, None),
            P(BOTH, None),
            P(BOTH, None),
        ),
        check_vma=False,
    )
```

```python
import functools
import jax
import jax.numpy as jnp
from jax import lax
from jax.experimental import pallas as pl
from jax.experimental.pallas import tpu as pltpu
from jax.sharding import Mesh
from jax.sharding import PartitionSpec as P

C = 512
ZD = 256
GROUPS = 32
SIDE = 32
STEP = 5
COMMIT_WEIGHT = 0.25
CLIP_AT = 1e-05
EMA_DECAY = 0.8
WEIGHT_RATE = 0.03
GAIN_RATE = 0.4
ROWS = SIDE * SIDE
PAD = SIDE
HIGH = lax.Precision.HIGHEST
F32 = jnp.float32
BF16 = jnp.bfloat16
VMEM_LIMIT = 60 * 1024 * 1024


def sigmoid(v):
    return 0.5 * jnp.tanh(0.5 * v) + 0.5


def nt(left, right):
    return lax.dot_general(left, right, (((1,), (1,)), ((), ())), preferred_element_type=F32)


def nn(left, right):
    return lax.dot_general(left, right, (((1,), (0,)), ((), ())), preferred_element_type=F32)


def image_mean(sums, group):
    width = C // GROUPS
    row = lax.broadcasted_iota(jnp.int32, (C, C), 0) // width
    col = lax.broadcasted_iota(jnp.int32, (C, C), 1) // width
    same_group = (row == col).astype(F32)
    left = lax.broadcasted_iota(jnp.int32, (16, 16), 0)
    right = lax.broadcasted_iota(jnp.int32, (16, 16), 1)
    same_image = (((left >> 2) >> group) == ((right >> 2) >> group)) & (
        ((left & 3) >> group) == ((right & 3) >> group)
    )
    side = 8 << group
    count = (side * side * width).astype(F32)
    spread = lax.dot_general(
        sums, same_group, (((1,), (0,)), ((), ())), precision=HIGH, preferred_element_type=F32
    )
    total = lax.dot_general(
        same_image.astype(F32), spread, (((1,), (0,)), ((), ())), precision=HIGH, preferred_element_type=F32
    )
    return total / count


def tile_rows(block):
    return jnp.sum(block.reshape(4, 8, C), axis=1)


def spread_rows(ref, tiles):
    for ty in range(4):
        for tx in range(4):
            t = 4 * ty + tx
            ref[ty, 8 * tx : 8 * tx + 8, :] = jnp.broadcast_to(tiles[t : t + 1, :], (8, C))


def norm_stats(x_ref, group, mean_ref, rstd_ref):
    parts = []
    for ty in range(4):
        acc = x_ref[pl.ds(ty * 256, 32), :]
        for y in range(1, 8):
            acc = acc + x_ref[pl.ds(ty * 256 + y * 32, 32), :]
        parts.append(tile_rows(acc))
    spread_rows(mean_ref, image_mean(jnp.concatenate(parts, axis=0), group))
    parts = []
    for ty in range(4):
        mu = mean_ref[ty]
        acc = jnp.zeros((32, C), F32)
        for y in range(8):
            cen = x_ref[pl.ds(ty * 256 + y * 32, 32), :] - mu
            acc = acc + cen * cen
        parts.append(tile_rows(acc))
    var = image_mean(jnp.concatenate(parts, axis=0), group)
    spread_rows(rstd_ref, lax.rsqrt(var + 1e-05))


def store_shifts(ref, y, val, side):
    x = lax.broadcasted_iota(jnp.int32, (32, C), 0) & (side - 1)
    zero = jnp.zeros((32, C), F32)
    left = jnp.where(x != 0, pltpu.roll(val, 1, 0), zero)
    right = jnp.where(x != side - 1, pltpu.roll(val, 31, 0), zero)
    rows = pl.ds(pl.multiple_of(PAD + y * 32, 32), 32)
    ref[rows, 0:C] = left.astype(BF16)
    ref[rows, C : 2 * C] = val.astype(BF16)
    ref[rows, 2 * C : 3 * C] = right.astype(BF16)


def clear_pads(ref):
    ref[0:PAD, :] = jnp.zeros((PAD, 3 * C), BF16)
    ref[PAD + ROWS : 2 * PAD + ROWS, :] = jnp.zeros((PAD, 3 * C), BF16)


def row_mask(shape, dim, dy, side):
    y = (lax.broadcasted_iota(jnp.int32, shape, dim) // 32) & (side - 1)
    return y != 0 if dy < 0 else y != side - 1


SHARD = 64
RES = (("mat", 0, 1152),)
MIX = (("mat", 0, 512), ("mat", 512, 512), ("lat", 1024, 128))


def part_shapes(kind, lanes, z_size, dtype):
    rows = 2 * SHARD * z_size
    if kind == "mat":
        return [((rows, 4 * lanes), dtype)]
    if kind == "lat":
        return [((rows // 2, 4 * lanes), dtype)] * 2
    return [((4, rows, lanes), dtype)]


def part_blocks(kind, refs, lanes, dp, f):
    cols = pl.ds(pl.multiple_of(f * lanes, 128), lanes)
    if kind == "lat":
        half = SHARD // 2
        at = pl.ds(pl.multiple_of(dp * half, half), half)
        return [(pl.ds(i * half, half), refs[i].at[at, cols]) for i in range(2)]
    at = pl.ds(pl.multiple_of(dp * SHARD, SHARD), SHARD)
    where = refs[0].at[at, cols] if kind == "mat" else refs[0].at[f, at, :]
    return [(pl.ds(0, SHARD), where)]


def part_count(kind):
    return 2 if kind == "lat" else 1


def copy_count(parts, z_size):
    return 8 * z_size * sum(part_count(kind) for kind, _, _ in parts)


def block_copies(parts, info_ref, pieces, wholes, sems, inward):
    core, f = info_ref[1], info_ref[2]
    z_size = pieces[0][0].shape[0]
    copies = []
    for side in range(2):
        owner = core if side == 0 else 1 - core
        for far in range(2):
            for near in range(2):
                for z in range(z_size):
                    at_f = f ^ ((2 - owner) * near) ^ ((1 + owner) * far)
                    at_dp = 2 * z + owner
                    first = 0
                    for kind, lane, lanes in parts:
                        refs = wholes[first : first + part_count(kind)]
                        for rows, where in part_blocks(kind, refs, lanes, at_dp, at_f):
                            piece = pieces[side][2 * far + near].at[z, rows, pl.ds(lane, lanes)]
                            ends = (piece, where) if inward else (where, piece)
                            copies.append(pltpu.make_async_copy(*ends, sems.at[len(copies)]))
                        first += part_count(kind)
    return copies


def grad_copies(info_ref, keep_ref, send_ref, dw_ref, sems):
    core, f = info_ref[1], info_ref[2]
    z_size = keep_ref.shape[0] // 4
    lanes = RES[0][2]
    groups = []
    for at_f in range(4):
        copies = []
        away = at_f ^ f
        high, low = away >> 1, away & 1
        for side, out_ref in enumerate((keep_ref, send_ref)):
            owner = core if side == 0 else 1 - core
            place = jnp.where(owner == 0, 2 * low + high, 2 * high + low) * z_size
            for z in range(z_size):
                rows = pl.ds(pl.multiple_of((2 * z + owner) * SHARD, SHARD), SHARD)
                sem = sems.at[(at_f * 2 + side) * z_size + z]
                copies.append(
                    pltpu.make_async_copy(dw_ref.at[rows, pl.ds(at_f * lanes, lanes)], out_ref.at[place + z], sem)
                )
        groups.append(copies)
    return groups


def quarters(*refs):
    return [[ref.at[pl.ds(k * (ref.shape[0] // 4), ref.shape[0] // 4)] for k in range(4)] for ref in refs]


def weight_copies(info_ref, refs, dst_ref, sems):
    if len(refs) == 1:
        return [pltpu.make_async_copy(refs[0], dst_ref, sems.at[0])]
    return block_copies(RES, info_ref, (refs[:4], refs[4:]), (dst_ref,), sems, True)


def weight_sems(weight):
    return pltpu.SemaphoreType.DMA((1 if len(weight) == 1 else copy_count(RES, weight[0].shape[0]),))


def conv_fwd_kernel(n_weight, has_res, info_ref, x_ref, gain_ref, *rest):
    weight, rest = rest[:n_weight], rest[n_weight:]
    if has_res:
        res_ref, *rest = rest
    t_ref, a3_ref, wt_ref, mean_ref, rstd_ref, sems = rest
    copies = weight_copies(info_ref, weight, wt_ref, sems)
    for copy in copies:
        copy.start()
    group = info_ref[0]
    side = 8 << group
    norm_stats(x_ref, group, mean_ref, rstd_ref)
    clear_pads(a3_ref)
    gamma = gain_ref[0:1, :]
    beta = gain_ref[1:2, :]

    def body(y, carry):
        ty = y // 8
        v = (x_ref[pl.ds(pl.multiple_of(y * 32, 32), 32), :] - mean_ref[ty]) * rstd_ref[ty] * gamma + beta
        store_shifts(a3_ref, y, v * sigmoid(v), side)
        return carry

    lax.fori_loop(0, 32, body, 0, unroll=4)
    for copy in copies:
        copy.wait()
    out = nt(a3_ref[PAD : PAD + ROWS, :], wt_ref[:, 3 * C : 6 * C])
    if has_res:
        out = out + res_ref[...]
    t_ref[...] = out
    for dy in (-1, 1):
        part = nt(a3_ref[PAD + 32 * dy : PAD + 32 * dy + ROWS, :], wt_ref[:, (dy + 1) * 3 * C : (dy + 2) * 3 * C])
        t_ref[...] += jnp.where(row_mask((ROWS, 1), 0, dy, side), part, 0.0)


SMEM = pl.BlockSpec(memory_space=pltpu.SMEM)
VM = pl.BlockSpec(memory_space=pltpu.VMEM)
ANY = pl.BlockSpec(memory_space=pl.ANY)
PARAMS = pltpu.CompilerParams(vmem_limit_bytes=VMEM_LIMIT)
CONV_FLOPS = 2 * ROWS * 9 * C * C


def cost(flops, size):
    return pl.CostEstimate(flops=flops, bytes_accessed=size, transcendentals=0)


def conv_fwd(info, x, gains, weight, res=None):
    args = [info, x, gains, *weight] + ([] if res is None else [res])
    return pl.pallas_call(
        functools.partial(conv_fwd_kernel, len(weight), res is not None),
        out_shape=(
            jax.ShapeDtypeStruct((ROWS, C), F32),
            jax.ShapeDtypeStruct((ROWS + 2 * PAD, 3 * C), BF16),
        ),
        in_specs=[SMEM, VM, VM] + [ANY] * len(weight) + ([] if res is None else [VM]),
        out_specs=(VM, VM),
        scratch_shapes=[
            pltpu.VMEM((C, 9 * C), BF16),
            pltpu.VMEM((4, 32, C), F32),
            pltpu.VMEM((4, 32, C), F32),
            weight_sems(weight),
        ],
        compiler_params=PARAMS,
        cost_estimate=cost(2 * CONV_FLOPS, 12 << 20),
        name="conv_fwd",
    )(*args)


def conv_dw_kernel(split, info_ref, dt_ref, a3_ref, *rest):
    if split:
        keep_ref, send_ref, dw_ref, dtt_ref, sems = rest
    else:
        dw_ref, dtt_ref = rest
    side = 8 << info_ref[0]
    dtt_ref[1] = dt_ref[...].astype(F32).T.astype(BF16)
    flat = dtt_ref[1]
    for dy in (-1, 1):
        keep = row_mask((1, ROWS), 1, dy, side).astype(BF16)
        dtt_ref[dy + 1] = flat * keep
    groups = grad_copies(info_ref, keep_ref, send_ref, dw_ref, sems) if split else [[]] * 4
    for dy in (-1, 0, 1):
        dw = nn(dtt_ref[dy + 1], a3_ref[PAD + 32 * dy : PAD + 32 * dy + ROWS, :])
        dw_ref[:, (dy + 1) * 3 * C : (dy + 2) * 3 * C] = dw.astype(dw_ref.dtype)
        for copy in groups[dy + 1] + (groups[3] if dy == 1 else []):
            copy.start()
    for copies in groups:
        for copy in copies:
            copy.wait()


def conv_dw(info, dt, a3, z_size):
    scratch = [pltpu.VMEM((3, C, ROWS), BF16)]
    if z_size:
        block = jax.ShapeDtypeStruct((4 * z_size, SHARD, 9 * C // 4), BF16)
        shapes, specs = (block, block), (ANY, ANY)
        scratch = [pltpu.VMEM((C, 9 * C), BF16)] + scratch + [pltpu.SemaphoreType.DMA((copy_count(RES, z_size),))]
    else:
        shapes, specs = jax.ShapeDtypeStruct((C, 9 * C), F32), VM
    return pl.pallas_call(
        functools.partial(conv_dw_kernel, z_size),
        out_shape=shapes,
        in_specs=[SMEM, VM, VM],
        out_specs=specs,
        scratch_shapes=scratch,
        compiler_params=PARAMS,
        cost_estimate=cost(2 * CONV_FLOPS, 12 << 20),
        name="conv_dw",
    )(info, dt, a3)


def conv_dx_kernel(n_weight, has_res, pix_z, info_ref, dt_ref, x_ref, gain_ref, *rest):
    weight, rest = rest[:n_weight], rest[n_weight:]
    if has_res:
        res_ref, *rest = rest
    if pix_z:
        pix_ref, dx_ref, dgain_ref, patch_ref, *rest = rest
    else:
        dx_ref, dgain_ref, *rest = rest
    wt_ref, d3_ref, mean_ref, rstd_ref, ds_ref, sems = rest
    copies = weight_copies(info_ref, weight, wt_ref, sems)
    for copy in copies:
        copy.start()
    group = info_ref[0]
    side = 8 << group
    clear_pads(d3_ref)

    def body(y, carry):
        val = dt_ref[pl.ds(pl.multiple_of(y * 32, 32), 32), :].astype(F32)
        store_shifts(d3_ref, y, val, side)
        return carry

    lax.fori_loop(0, 32, body, 0, unroll=4)
    norm_stats(x_ref, group, mean_ref, rstd_ref)
    for copy in copies:
        copy.wait()
    for dy in (0, -1, 1):
        part = None
        for dx in (-1, 0, 1):
            t = 3 * (dy + 1) + dx + 1
            one = nn(
                d3_ref[PAD - 32 * dy : PAD - 32 * dy + ROWS, (1 - dx) * C : (2 - dx) * C],
                wt_ref[:, t * C : (t + 1) * C],
            )
            part = one if part is None else part + one
        if dy == 0:
            ds_ref[...] = part
        else:
            ds_ref[...] += jnp.where(row_mask((ROWS, 1), 0, -dy, side), part, 0.0)
    gamma = gain_ref[0:1, :]
    beta = gain_ref[1:2, :]
    first, second = [], []
    for ty in range(4):
        mu, rs = mean_ref[ty], rstd_ref[ty]

        def step(y, carry, ty=ty, mu=mu, rs=rs):
            one, two = carry
            rows = pl.ds(pl.multiple_of(ty * 256 + y * 32, 32), 32)
            xh = (x_ref[rows, :] - mu) * rs
            v = xh * gamma + beta
            sg = sigmoid(v)
            ds = ds_ref[rows, :] * (sg * (1.0 + v * (1.0 - sg)))
            ds_ref[rows, :] = ds
            return (one + ds, two + ds * xh)

        zero = jnp.zeros((32, C), F32)
        one, two = lax.fori_loop(0, 8, step, (zero, zero), unroll=2)
        first.append(tile_rows(one))
        second.append(tile_rows(two))
    first = jnp.concatenate(first, axis=0)
    second = jnp.concatenate(second, axis=0)
    dgain_ref[0:1, :] = jnp.sum(second, axis=0, keepdims=True)
    dgain_ref[1:2, :] = jnp.sum(first, axis=0, keepdims=True)
    m_one = image_mean(first * gamma, group)
    m_two = image_mean(second * gamma, group)
    for ty in range(4):
        mu, rs = mean_ref[ty], rstd_ref[ty]
        one = jnp.concatenate([jnp.broadcast_to(m_one[4 * ty + tx : 4 * ty + tx + 1, :], (8, C)) for tx in range(4)], axis=0)
        two = jnp.concatenate([jnp.broadcast_to(m_two[4 * ty + tx : 4 * ty + tx + 1, :], (8, C)) for tx in range(4)], axis=0)

        def step(y, carry, ty=ty, mu=mu, rs=rs, one=one, two=two):
            rows = pl.ds(pl.multiple_of(ty * 256 + y * 32, 32), 32)
            xh = (x_ref[rows, :] - mu) * rs
            dx = rs * (ds_ref[rows, :] * gamma - one - xh * two)
            if has_res:
                dx = dx + res_ref[rows, :]
            dx_ref[rows, :] = dx.astype(dx_ref.dtype)
            return carry

        lax.fori_loop(0, 8, step, 0, unroll=2)
    if pix_z:
        patch = nn(transposed(dx_ref[...]), pix_ref[...]).astype(BF16)
        width = patch_ref.shape[3]
        for z in range(pix_z):
            for core in range(2):
                rows = patch[(2 * z + core) * SHARD : (2 * z + core + 1) * SHARD, :]
                for f in range(4):
                    patch_ref[4 * core + f, z] = rows[:, f * width : (f + 1) * width]


def conv_dx(info, dt, x, gains, weight, res=None, low=True, pixels=None, z_size=0):
    args = [info, dt, x, gains, *weight] + [one for one in (res, pixels) if one is not None]
    patch = []
    if pixels is not None:
        patch = [jax.ShapeDtypeStruct((8, z_size, SHARD, pixels.shape[1] // 4), BF16)]
    return pl.pallas_call(
        functools.partial(conv_dx_kernel, len(weight), res is not None, 0 if pixels is None else z_size),
        out_shape=(
            jax.ShapeDtypeStruct((ROWS, C), BF16 if low else F32),
            jax.ShapeDtypeStruct((2, C), F32),
            *patch,
        ),
        in_specs=[SMEM, VM, VM, VM] + [ANY] * len(weight) + [VM] * (len(args) - 4 - len(weight)),
        out_specs=(VM,) * (2 + len(patch)),
        scratch_shapes=[
            pltpu.VMEM((C, 9 * C), BF16),
            pltpu.VMEM((ROWS + 2 * PAD, 3 * C), BF16),
            pltpu.VMEM((4, 32, C), F32),
            pltpu.VMEM((4, 32, C), F32),
            pltpu.VMEM((ROWS, C), F32),
            weight_sems(weight),
        ],
        compiler_params=PARAMS,
        cost_estimate=cost(3 * CONV_FLOPS, 12 << 20),
        name="conv_dx",
    )(*args)


def silu_slope(value):
    gate = sigmoid(value)
    return gate * (1.0 + value * (1.0 - gate))


def transposed(value):
    return value.astype(F32).T.astype(BF16)


HALF = SIDE // 2
LAT = HALF * HALF


def to_depth(src_ref, lanes_ref, dst_ref):
    for k in range(C // 128):
        lanes_ref[k] = src_ref[:, k * 128 : (k + 1) * 128]
    for k in range(C // 128):
        for b in range(2):
            block = lanes_ref[k, pl.ds(b, ROWS // 2, stride=2), :].reshape(HALF, 2, HALF, 128)
            for a in range(2):
                at = (2 * a + b) * C + k * 128
                dst_ref[:, at : at + 128] = block[:, a].reshape(LAT, 128).astype(dst_ref.dtype)


def from_depth(src_ref, lanes_ref, dst_ref):
    for k in range(C // 128):
        for b in range(2):
            pair = [
                src_ref[:, (2 * a + b) * C + k * 128 : (2 * a + b) * C + (k + 1) * 128].reshape(HALF, 1, HALF, 128)
                for a in range(2)
            ]
            lanes_ref[k, pl.ds(b, ROWS // 2, stride=2), :] = jnp.concatenate(pair, axis=1).reshape(ROWS // 2, 128)
    for k in range(C // 128):
        dst_ref[:, k * 128 : (k + 1) * 128] = lanes_ref[k]


MIX_SHAPES = [(C, 4 * C), (C, 4 * C), (ZD, C), (ZD, C)]


def mix_copies(info_ref, refs, dst_refs, sems):
    if len(refs) == 4:
        return [pltpu.make_async_copy(ref, dst, sems.at[i]) for i, (ref, dst) in enumerate(zip(refs, dst_refs))]
    return block_copies(MIX, info_ref, (refs[:4], refs[4:]), dst_refs, sems, True)


def mix_scratch(weights):
    count = 4 if len(weights) == 4 else copy_count(MIX, weights[0].shape[0])
    return [pltpu.VMEM(one, BF16) for one in MIX_SHAPES] + [pltpu.SemaphoreType.DMA((count,))]


def mid_fwd_kernel(n_weight, info_ref, h_ref, code_ref, *rest):
    weights, rest = rest[:n_weight], rest[n_weight:]
    e_ref, d_ref, s_ref, q_ref, y_ref, s2_ref, g_ref, commit_ref, dcom_ref, resid_ref, *rest = rest
    u_ref, lanes_ref, ws0_ref, ws1_ref, wl0_ref, wl1_ref, load_sems = rest
    loads = mix_copies(info_ref, weights, (ws0_ref, ws1_ref, wl0_ref, wl1_ref), load_sems)
    for load in loads:
        load.start()
    to_depth(h_ref, lanes_ref, e_ref)
    for load in loads:
        load.wait()
    d = nt(e_ref[...], ws0_ref[...])
    d_ref[...] = d
    s = (d * sigmoid(d)).astype(BF16)
    s_ref[...] = s
    z = nt(s, wl0_ref[...])
    q = jnp.zeros((LAT, ZD), F32)
    commit = jnp.zeros((LAT, ZD), F32)
    dcom = jnp.zeros((LAT, ZD), F32)
    for k in range(4):
        resid_ref[k * LAT : (k + 1) * LAT, :] = (z - q).astype(BF16)
        q = q + code_ref[k * LAT : (k + 1) * LAT, :].astype(F32)
        diff = z - q
        commit = commit + diff * diff
        dcom = dcom + diff
    commit_ref[...] = jnp.sum(commit, axis=0, keepdims=True)
    dcom_ref[...] = dcom
    quant = (z + (q - z)).astype(BF16)
    q_ref[...] = quant
    y = nn(quant, wl1_ref[...])
    y_ref[...] = y
    s2 = (y * sigmoid(y)).astype(BF16)
    s2_ref[...] = s2
    u_ref[...] = nn(s2, ws1_ref[...])
    from_depth(u_ref, lanes_ref, g_ref)


def mid_fwd(info, h, codes, weights):
    shape = jax.ShapeDtypeStruct
    return pl.pallas_call(
        functools.partial(mid_fwd_kernel, len(weights)),
        out_shape=(
            shape((LAT, 4 * C), BF16),
            shape((LAT, C), F32),
            shape((LAT, C), BF16),
            shape((LAT, ZD), BF16),
            shape((LAT, C), F32),
            shape((LAT, C), BF16),
            shape((ROWS, C), F32),
            shape((1, ZD), F32),
            shape((LAT, ZD), F32),
            shape((4 * LAT, ZD), BF16),
        ),
        in_specs=[SMEM, VM, VM] + [ANY] * len(weights),
        out_specs=(VM,) * 10,
        scratch_shapes=[pltpu.VMEM((LAT, 4 * C), F32), pltpu.VMEM((C // 128, ROWS, 128), F32), *mix_scratch(weights)],
        compiler_params=PARAMS,
        cost_estimate=cost(4 << 30, 12 << 20),
        name="mid_fwd",
    )(info, h, codes, *weights)


def mid_bwd_kernel(
    split, scale, n_weight, info_ref, dg_ref, e_ref, d_ref, s_ref, q_ref, y_ref, s2_ref, dcom_ref, *rest,
):
    weights, rest = rest[:n_weight], rest[n_weight:]
    *rest, ws0_ref, ws1_ref, wl0_ref, wl1_ref, load_sems = rest
    loads = mix_copies(info_ref, weights, (ws0_ref, ws1_ref, wl0_ref, wl1_ref), load_sems)
    for load in loads:
        load.start()
    if split:
        keep_ref, send_ref, dh_ref, *wholes, du_ref, de_ref, lanes_ref, sems = rest
    else:
        *wholes, dh_ref, du_ref, de_ref, lanes_ref = rest
    dws0_ref, dws1_ref, dwl0_ref, dwl1_ref = wholes
    to_depth(dg_ref, lanes_ref, du_ref)
    for load in loads:
        load.wait()
    out = dws0_ref.dtype
    ds2 = nt(du_ref[...], ws1_ref[...])
    dy = (ds2 * silu_slope(y_ref[...])).astype(BF16)
    dws1_ref[...] = nn(transposed(s2_ref[...]), du_ref[...]).astype(out)
    dwl1_ref[...] = nn(transposed(q_ref[...]), dy).astype(out)
    dz = (nt(dy, wl1_ref[...]) + scale * dcom_ref[...]).astype(BF16)
    dwl0_ref[...] = nn(transposed(dz), s_ref[...]).astype(out)
    ds = nn(dz, wl0_ref[...])
    dd = (ds * silu_slope(d_ref[...])).astype(BF16)
    dws0_ref[...] = nn(transposed(dd), e_ref[...]).astype(out)
    copies = []
    if split:
        copies = block_copies(MIX, info_ref, quarters(keep_ref, send_ref), wholes, sems, False)
    for copy in copies:
        copy.start()
    de_ref[...] = nn(dd, ws0_ref[...])
    from_depth(de_ref, lanes_ref, dh_ref)
    for copy in copies:
        copy.wait()


def mid_bwd(info, scale, dg, e, d, s, q, y, s2, dcom, weights, z_size):
    shape = jax.ShapeDtypeStruct
    wholes = MIX_SHAPES
    scratch = [
        pltpu.VMEM((LAT, 4 * C), BF16),
        pltpu.VMEM((LAT, 4 * C), F32),
        pltpu.VMEM((C // 128, ROWS, 128), F32),
    ]
    field = shape((ROWS, C), F32)
    if z_size:
        block = shape((4 * z_size, SHARD, 1152), BF16)
        shapes, specs = (block, block, field), (ANY, ANY, VM)
        scratch = [pltpu.VMEM(one, BF16) for one in wholes] + scratch
        scratch += [pltpu.SemaphoreType.DMA((copy_count(MIX, z_size),))]
    else:
        shapes, specs = tuple(shape(one, F32) for one in wholes) + (field,), (VM,) * 5
    out = pl.pallas_call(
        functools.partial(mid_bwd_kernel, z_size, scale, len(weights)),
        out_shape=shapes,
        in_specs=[SMEM] + [VM] * 8 + [ANY] * len(weights),
        out_specs=specs,
        scratch_shapes=scratch + mix_scratch(weights),
        compiler_params=PARAMS,
        cost_estimate=cost(4 << 30, 12 << 20),
        name="mid_bwd",
    )(info, dg, e, d, s, q, y, s2, dcom, *weights)
    return out[-1], out[:-1]


def head_kernel(total_ref, g_ref, wp_ref, pix_ref, mask_ref, dw_ref, dg_ref, loss_ref, o_ref, dr_ref):
    inv = total_ref[0]
    loss = jnp.zeros((1, pix_ref.shape[1]), F32)
    for i in range(4):
        rows = pl.ds(i * 256, 256)
        g = g_ref[rows, :]
        gate = sigmoid(g)
        o = (g * gate).astype(BF16)
        o_ref[rows, :] = o
        err = nn(o, wp_ref[...]) - pix_ref[rows, :].astype(F32)
        keep = mask_ref[rows, :].astype(F32)
        smooth = jnp.sqrt(err * err + 1.0)
        loss = loss + jnp.sum(keep * (smooth - 1.0), axis=0, keepdims=True)
        dr = (keep * err / smooth / inv).astype(BF16)
        dr_ref[rows, :] = dr
        do = nt(dr, wp_ref[...])
        dg_ref[rows, :] = do * (gate * (1.0 + g * (1.0 - gate)))
    loss_ref[...] = loss
    dw_ref[...] = nn(transposed(o_ref[...]), dr_ref[...]).astype(dw_ref.dtype)


def head(total, g, wp, pix, mask, grad_type=BF16):
    shape = jax.ShapeDtypeStruct
    width = pix.shape[1]
    return pl.pallas_call(
        head_kernel,
        out_shape=(shape((C, width), grad_type), shape((ROWS, C), F32), shape((1, width), F32)),
        in_specs=[SMEM, VM, VM, VM, VM],
        out_specs=(VM,) * 3,
        scratch_shapes=[pltpu.VMEM((ROWS, C), BF16), pltpu.VMEM((ROWS, width), BF16)],
        compiler_params=PARAMS,
        cost_estimate=cost(6 << 30, 12 << 20),
        name="head",
    )(total, g, wp, pix, mask)


BOTH = ("z", "core", "fsdp")
COLS = ("z", "core")


def swap(shard):
    return jnp.swapaxes(shard, -1, -2).astype(BF16)


def across(x, near):
    n = lax.axis_size("fsdp")
    masks = (2, 1) if near else (1, 2)
    return lax.ppermute(x, ("core", "fsdp"), [(c * n + f, c * n + (f ^ masks[c])) for c in range(2) for f in range(n)])


def partner(x):
    return lax.ppermute(x, "core", [(0, 1), (1, 0)])


def everyone(x):
    n = lax.axis_size("z") * lax.axis_size("core") * lax.axis_size("fsdp")
    return lax.all_to_all(jnp.broadcast_to(x[None], (n,) + x.shape), BOTH, 0, 0, tiled=True)


def along_z(x, step):
    n = lax.axis_size("z")
    return lax.ppermute(x, "z", [(i, i ^ step) for i in range(n)])


def shuffle(x, axis):
    return lax.all_to_all(x, axis, 0, 0, tiled=True)


def assemble_kernel(parts, info_ref, *rest):
    copies = block_copies(parts, info_ref, (rest[:4], rest[4:8]), rest[8:-1], rest[-1], True)
    for copy in copies:
        copy.start()
    for copy in copies:
        copy.wait()


def assemble(info, pieces, parts):
    z_size = pieces[0].shape[0]
    shapes = [s for kind, _, lanes in parts for s in part_shapes(kind, lanes, z_size, BF16)]
    return pl.pallas_call(
        functools.partial(assemble_kernel, parts),
        out_shape=tuple(jax.ShapeDtypeStruct(*s) for s in shapes),
        in_specs=[SMEM] + [ANY] * 8,
        out_specs=(VM,) * len(shapes),
        scratch_shapes=[pltpu.SemaphoreType.DMA((copy_count(parts, z_size),))],
        compiler_params=PARAMS,
        cost_estimate=cost(1 << 30, 10 << 20),
        name="assemble",
    )(info, *pieces)


def gather_all(shards, others, slow):
    z_size = lax.axis_size("z")
    count = len(shards)
    shards = list(shards)
    done = [{} for _ in shards]
    pieces, later, side, waiting, early = {}, {}, {}, {}, {}
    groups = [(1, 3), (3, count)] if count else []
    ready = [1, 3]
    bulks = {}
    if count:
        bulks[1] = lax.all_gather(jnp.concatenate(shards[1:3], axis=1), "z")
        side["joined"] = jnp.concatenate(shards[3:], axis=1)
    for step in range(max([count + 2] + list(others)) + 1):
        new = {}
        if 0 <= step - 2 < count:
            new["both", step - 2] = across(done[step - 2]["near"], False)
        if 0 <= step - 1 < count:
            new["far", step - 1] = across(done[step - 1]["z"], False)
            new["near", step - 1] = across(done[step - 1]["z"], True)
        if step < min(count, 1):
            new["z", step] = shuffle(jnp.broadcast_to(shards[step][None], (z_size,) + shards[step].shape), "z")
        if step == 1 and count:
            bulks[3] = lax.all_gather(side.pop("joined"), "z")
        for i, (first, last) in enumerate(groups):
            if step == ready[i]:
                new["bulk", first] = bulks[first]
        for j in list(early):
            new["z", j] = early.pop(j)
        if 0 <= step - 3 < count:
            own = [done[step - 3][name] for name in ("z", "near", "far", "both")]
            new["core", step - 3] = [partner(one) for one in own]
            pieces[step - 3] = (*own, *new["core", step - 3])
        if step in slow:
            due, function = slow[step]
            waiting[due] = function(pieces, side)
        if step in waiting:
            side = {**side, **waiting.pop(step)}
        if step in others:
            side = {**side, **others[step](pieces, side)}
        names = list(new)
        values, shards[step + 1 :], side = lax.optimization_barrier((list(new.values()), shards[step + 1 :], side))
        for (name, i), value in zip(names, values):
            done[i][name] = value
        for i, (first, last) in enumerate(groups):
            if step == ready[i]:
                at = 0
                for j in range(first, last):
                    z_slice = done[first]["bulk"][:, :, at : at + shards[j].shape[1]]
                    at += shards[j].shape[1]
                    if j <= step:
                        done[j]["z"] = z_slice
                    else:
                        early[j] = z_slice
        if 0 <= step - 3 < count:
            later[step - 3] = (*[done[step - 3][name] for name in ("z", "near", "far", "both")], *done[step - 3]["core"])
    return later, side


def add_up(parts):
    total = parts[0].astype(F32)
    for part in parts[1:]:
        total = total + part.astype(F32)
    return total


class Slow:
    def __init__(self, value):
        self.value = value


def scatter_stages(keep, send, tie, bulk, out):
    half = keep.shape[0] // 2
    keep, got = yield keep, partner(send)
    parts = [keep, got]
    for near in (False, True):
        away = add_up([p[half : 2 * half] for p in parts]).astype(BF16)
        if near and tie:
            away, tie[0] = lax.optimization_barrier((away, tie[0]))
        *parts, got = yield *parts, across(away, near)
        parts.append(got)
        half = half // 2
    sums = add_up([p[: 2 * half] for p in parts]).astype(BF16)
    if bulk:
        got = yield Slow(lax.psum_scatter(sums, "z", scatter_dimension=0))
        out.append(got.astype(F32))
    else:
        got = yield shuffle(sums, "z")
        out.append(jnp.sum(got.astype(F32), axis=0))


def scatter_pair(blocks, out):
    got = yield shuffle(blocks, ("core", "fsdp"))
    sums = jnp.sum(got.astype(F32), axis=0)
    me = lax.axis_index("z")
    away = [along_z(lax.dynamic_index_in_dim(sums, me ^ k, keepdims=False).astype(BF16), k) for k in range(1, sums.shape[0])]
    away = yield away
    out.append(add_up([lax.dynamic_index_in_dim(sums, me, keepdims=False)] + away))


def scatter_direct(blocks, out):
    got = yield shuffle(blocks, BOTH)
    out.append(jnp.sum(got.astype(F32), axis=0))


class Overlap:
    def __init__(self):
        self.live = []

    def add(self, stages, *args, late=0):
        out = []
        stages = stages(*args, out)
        self.live.append((stages, next(stages), late))
        return out

    def finish(self):
        for stages, value, _ in self.live:
            try:
                while True:
                    value = stages.send(value.value if isinstance(value, Slow) else value)
            except StopIteration:
                pass
        self.live = []

    def push(self, values):
        stages, value, _ = self.live[-1]
        values, value = lax.optimization_barrier((values, value))
        self.live[-1] = (stages, stages.send(value), 0)
        return values

    def step(self, values, use=None):
        due = [value for _, value, late in self.live if not late]
        values, due = lax.optimization_barrier((values, due))
        if use is not None:
            use(values)
        live, at = [], 0
        for stages, value, late in self.live:
            if late:
                live.append((stages, value, late - 1))
                continue
            try:
                value = stages.send(due[at])
                live.append((stages, value.value, 1) if isinstance(value, Slow) else (stages, value, 0))
            except StopIteration:
                pass
            at += 1
        self.live = live
        return values


def fetch_whole(shard):
    cols = lax.all_gather(shard.astype(BF16), COLS, axis=1, tiled=True)
    return jnp.swapaxes(lax.all_gather(cols, "fsdp", axis=0, tiled=True), 0, 1)


def reduce_whole(grad):
    rows = lax.psum_scatter(jnp.swapaxes(grad, 0, 1), "fsdp", scatter_dimension=0, tiled=True)
    return jnp.swapaxes(lax.psum_scatter(rows, COLS, scatter_dimension=1, tiled=True), 0, 1)


def widen(block, width):
    return jnp.pad(block, ((0, 0),) * (block.ndim - 1) + ((0, width - block.shape[-1]),))


def pix_matrix(blocks, width):
    return blocks[:, :, :width].transpose(1, 0, 2).reshape(C, 4 * width)


def pix_blocks(matrix, shard):
    rows, cols = shard
    return matrix.reshape(-1, cols, matrix.shape[1] // rows, rows).transpose(0, 2, 1, 3).reshape(-1, cols, rows)


def adam_step(weight, moment, second, grad, rate):
    moment_new = 0.5 * moment + 0.5 * grad
    second_new = 0.5 * second + 0.5 * grad * grad
    fix = 1.0 - 0.5**STEP
    weight_new = weight - rate * (
        moment_new / fix / (jnp.sqrt(second_new / fix) + 1e-12) + 0.01 * weight
    )
    return (weight_new, moment_new, second_new)


def small_blocks(values, devices):
    flat = jnp.concatenate([value.reshape(-1) for value in values])
    lanes = -(-flat.shape[0] // (128 * devices)) * 128
    return jnp.pad(flat, (0, devices * lanes - flat.shape[0])).reshape(devices, 1, lanes)


def exact(left, right, dims):
    return lax.dot_general(left, right, (dims, ((), ())), preferred_element_type=F32)


def code_slots(codes, devices, capacity, rows):
    n = codes.shape[0]
    owner = codes // rows
    hot = (owner[:, None] == jnp.arange(devices, dtype=jnp.int32)[None, :]).astype(BF16)
    at = jnp.arange(n, dtype=jnp.int32)
    before = (at[None, :] < at[:, None]).astype(BF16)
    rank = exact(before, hot, ((1,), (0,)))
    place = jnp.sum(rank * hot.astype(F32), axis=1).astype(jnp.int32)
    slot = owner * capacity + place
    return (jnp.arange(devices * capacity, dtype=jnp.int32)[:, None] == slot[None, :]).astype(BF16)


def on_device(
    pixels,
    valid_mask,
    size_groups,
    code_index,
    w_pixel,
    w_res,
    w_scale,
    w_latent,
    norm_gains,
    moment_pixel,
    moment_res,
    moment_scale,
    moment_latent,
    moment_gains,
    second_pixel,
    second_res,
    second_scale,
    second_latent,
    second_gains,
    ema_counts,
    ema_sums,
):
    n_inner = lax.axis_size("fsdp")
    z_size = lax.axis_size("z")
    devices = 2 * z_size * n_inner
    latent_all = code_index.shape[1] * devices
    rows = ema_sums.shape[0]
    paired = n_inner == 4 and w_res.shape[1] == 1152 and w_res.shape[2] == SHARD
    blocks = z_size if paired else 0
    place = [lax.axis_index("core"), lax.axis_index("fsdp")]
    info = jnp.stack([size_groups[0]] + [one.astype(jnp.int32) for one in place])

    codes = code_index.reshape(-1)
    capacity = max(2, 2 * codes.shape[0] // devices)
    pick = code_slots(codes, devices, capacity, rows)
    local = codes % rows
    cols = jnp.stack([local // 16, local % 16, jnp.ones_like(local)], axis=1).astype(BF16)
    want = exact(pick, cols, ((1,), (0,)))
    wanted = jnp.where(want[:, 2] > 0.5, want[:, 0] * 16.0 + want[:, 1], -1.0).astype(jnp.int32)
    book = (ema_sums / ema_counts[:, None]).astype(BF16)
    valid = jnp.sum(valid_mask.astype(F32).reshape(-1, 128), axis=0, keepdims=True)

    def row_hot(asked):
        return (asked[:, None] == jnp.arange(rows, dtype=jnp.int32)[None, :]).astype(BF16)

    def prepare(pieces, side):
        wide = -(-capacity // 128) * 128
        request = widen(wanted.astype(F32).reshape(devices, 1, capacity), wide)
        count = jnp.broadcast_to(widen(valid, wide)[None], (devices, 1, wide))
        return {"request": jnp.concatenate([request, count], axis=1)}

    def ask(pieces, side):
        got = shuffle(side["request"], BOTH)
        return {"asked": got[:, 0, :capacity].reshape(-1).astype(jnp.int32), "count": jnp.sum(got[:, 1])}

    def answer(side):
        return {"answer": exact(row_hot(side["asked"]), book, ((1,), (0,))).astype(BF16)}

    def reply(pieces, side):
        return {"replies": shuffle(side["answer"].reshape(devices, capacity, ZD), BOTH)}

    gains = [jnp.stack([norm_gains[j], norm_gains[4 + j]]) for j in range(4)]
    width = w_pixel.shape[1]

    def run_conv0(pieces, side):
        if paired:
            (pix,) = assemble(info, pieces[0], (("pix", RES[0][2], 256),))
            h0 = nt(pixels, pix_matrix(pix, width))
            weight = pieces[0]
        else:
            h0 = nt(pixels, fetch_whole(w_pixel[0]))
            weight = (fetch_whole(w_res[0]),)
        t1, a1 = conv_fwd(info, h0, gains[0], weight)
        return {**answer(side), "h0": h0, "t1": t1, "a1": a1, **({} if paired else {"res0": weight})}

    def run_conv1(pieces, side):
        weight = pieces[1] if paired else (fetch_whole(w_res[1]),)
        h1, a2 = conv_fwd(info, side["t1"], gains[1], weight, side["h0"])
        return {"h1": h1, "a2": a2, **({} if paired else {"res1": weight})}

    def run_mid(pieces, side):
        if paired:
            mats = pieces[2]
        else:
            mats = [fetch_whole(w_scale[i]) for i in range(2)] + [fetch_whole(w_latent[i]) for i in range(2)]
        picked = exact(pick, side["replies"].reshape(-1, ZD), ((0,), (0,))).astype(BF16)
        return {"mid": mid_fwd(info, side["h1"], picked, mats), **({} if paired else {"mats": mats})}

    def run_conv2(pieces, side):
        weight = pieces[3] if paired else (fetch_whole(w_res[2]),)
        t3, a3 = conv_fwd(info, side["mid"][6], gains[2], weight)
        return {"t3": t3, "a3": a3, **({} if paired else {"res2": weight})}

    def run_conv3(pieces, side):
        sent = exact(pick, side["mid"][9], ((1,), (0,))).astype(BF16)
        held = shuffle(sent.reshape(devices, capacity, ZD), BOTH)
        if paired:
            (pix,) = assemble(info, pieces[4], (("pix", RES[0][2], 256),))
            pix = pix_matrix(pix, width)
            weight = pieces[4]
        else:
            pix, weight = fetch_whole(w_pixel[1]), (fetch_whole(w_res[3]),)
        g1, a4 = conv_fwd(info, side["t3"], gains[3], weight, side["mid"][6])
        out = BF16 if paired else F32
        d_head, dg1, loss = head(side["count"].reshape(1), g1, pix, pixels, valid_mask, out)
        return {"held": held, "a4": a4, **({} if paired else {"res3": weight}), "d_head": d_head, "dg1": dg1, "loss": loss}

    others = {0: prepare, 2: ask, 3: run_conv0, 4: run_conv1, 5: run_mid, 6: run_conv2, 7: run_conv3}
    shards = []
    if paired:
        first = jnp.concatenate([swap(w_res[0]), widen(swap(w_pixel[0]), 256)], axis=1)
        first, res, pix, scale, latent = lax.optimization_barrier((first, w_res, w_pixel, w_scale, w_latent))
        scale, latent = swap(scale), swap(latent)
        mix = jnp.concatenate([scale[0], scale[1], latent.reshape(-1, latent.shape[2])], axis=1)
        last = jnp.concatenate([swap(res[3]), widen(swap(pix[1]), 256)], axis=1)
        shards = [first, swap(res[1]), mix, swap(res[2]), last]
    pieces, side = gather_all(shards, others, {4: (5, reply)})
    total_valid = side["count"]
    e, d, s, quant, y, s2, g0, commit, dcom, _ = side["mid"]
    h0, t1, a1, h1, a2, t3, a3, a4 = [side[name] for name in ("h0", "t1", "a1", "h1", "a2", "t3", "a3", "a4")]
    res_w = [pieces[i] for i in (0, 1, 3, 4)] if paired else [side[name] for name in ("res0", "res1", "res2", "res3")]
    mats = pieces[2] if paired else side["mats"]
    d_head, dg1, loss = side["d_head"], side["dg1"], side["loss"]

    hot_rows = row_hot(side["asked"])
    held = side["held"].reshape(-1, ZD)
    my_sums = exact(hot_rows, held, ((0,), (0,)))
    my_counts = jnp.sum(hot_rows.astype(F32), axis=0)
    counts_new = EMA_DECAY * ema_counts + (1.0 - EMA_DECAY) * my_counts
    sums_new = EMA_DECAY * ema_sums + (1.0 - EMA_DECAY) * my_sums
    book_new = sums_new / counts_new[:, None]

    scale = 2.0 * COMMIT_WEIGHT / (latent_all * ZD)
    loss_rows = jnp.stack([jnp.sum(one.reshape(-1, 128), axis=0) for one in (loss, commit)])
    if paired:
        overlap = Overlap()
        shard = w_pixel.shape[1:]
        sum_head = overlap.add(scatter_direct, pix_blocks(d_head, shard), late=2)
        dw, dg1 = overlap.step((conv_dw(info, dg1, a4, z_size), dg1))
        sum_res3 = overlap.add(scatter_stages, *dw, (), True)
        dt3, dn3 = overlap.step(conv_dx(info, dg1, t3, gains[3], res_w[3]))
        dw, dt3 = overlap.step((conv_dw(info, dt3, a3, z_size), dt3))
        sum_res2 = overlap.add(scatter_stages, *dw, (), True)
        dg0, dn2 = overlap.step(conv_dx(info, dt3, g0, gains[2], res_w[2], dg1, False))
        dh1, dw = overlap.step(
            mid_bwd(info, scale, dg0, e, d, s, quant, y, s2, dcom, mats, z_size)
        )
        sum_mix = overlap.add(scatter_stages, *dw, (), True)
        dw, dh1 = overlap.step((conv_dw(info, dh1, a2, z_size), dh1))
        sum_res1 = overlap.add(scatter_stages, *dw, (), True)
        dh1 = overlap.push(dh1)
        dt1, dn1 = overlap.step(conv_dx(info, dh1, t1, gains[1], res_w[1]))
        dw, dt1 = overlap.step((conv_dw(info, dt1, a1, z_size), dt1))
        tie = []
        sum_res0 = overlap.add(scatter_stages, *dw, tie, True)
        dt1 = overlap.push(dt1)
        _, dn0, d_patch = overlap.step(
            conv_dx(info, dt1, h0, gains[0], res_w[0], dh1, True, pixels, z_size), lambda got: tie.append(got[2])
        )
        sum_patch = overlap.add(scatter_pair, tie[0])
        small = overlap.add(scatter_direct, small_blocks([dn0, dn1, dn2, dn3, loss_rows], devices))
        overlap.finish()
        small = small[0]
        grad_pixel = jnp.stack([sum_patch[0], sum_head[0]])
        grad_res = jnp.stack([sum_res0[0], sum_res1[0], sum_res2[0], sum_res3[0]])
        grad_scale = jnp.stack([sum_mix[0][:, :512], sum_mix[0][:, 512:1024]])
        grad_latent = sum_mix[0][:, 1024:].reshape(2, SHARD // 2, -1)
    else:
        d_res3 = conv_dw(info, dg1, a4, 0)
        dt3, dn3 = conv_dx(info, dg1, t3, gains[3], res_w[3])
        d_res2 = conv_dw(info, dt3, a3, 0)
        dg0, dn2 = conv_dx(info, dt3, g0, gains[2], res_w[2], dg1, False)
        dh1, (d_scale0, d_scale1, d_lat0, d_lat1) = mid_bwd(
            info, scale, dg0, e, d, s, quant, y, s2, dcom, mats, 0
        )
        d_res1 = conv_dw(info, dh1, a2, 0)
        dt1, dn1 = conv_dx(info, dh1, t1, gains[1], res_w[1])
        d_res0 = conv_dw(info, dt1, a1, 0)
        dh0, dn0 = conv_dx(info, dt1, h0, gains[0], res_w[0], dh1)
        d_patch = exact(dh0, pixels, ((0,), (0,)))
        grad_pixel = jnp.stack([reduce_whole(g) for g in (d_patch, d_head)])
        grad_res = jnp.stack([reduce_whole(g) for g in (d_res0, d_res1, d_res2, d_res3)])
        grad_scale = jnp.stack([reduce_whole(g) for g in (d_scale0, d_scale1)])
        grad_latent = jnp.stack([reduce_whole(g) for g in (d_lat0, d_lat1)])
        small = shuffle(small_blocks([dn0, dn1, dn2, dn3, loss_rows], devices), BOTH)
        small = jnp.sum(small, axis=0)

    squares = jnp.sum(grad_pixel * grad_pixel) + jnp.sum(grad_res * grad_res)
    squares = squares + jnp.sum(grad_scale * grad_scale) + jnp.sum(grad_latent * grad_latent)
    shared = everyone(jnp.concatenate([small, jnp.full((1, small.shape[1]), squares, F32)]))
    total_squares = jnp.sum(shared[:, -1, 0])
    sizes = [2 * C] * 4 + [2 * 128]
    every = shared[:, :-1].reshape(-1)[: sum(sizes)]
    dn0, dn1, dn2, dn3, losses = jnp.split(every, [2 * C, 4 * C, 6 * C, 8 * C])
    dn0, dn1, dn2, dn3 = [one.reshape(2, C) for one in (dn0, dn1, dn2, dn3)]
    grad_gains = jnp.stack([dn0[0], dn1[0], dn2[0], dn3[0], dn0[1], dn1[1], dn2[1], dn3[1]])
    smooth_sum, commit_sum = jnp.sum(losses[:128]), jnp.sum(losses[128:])
    total_squares = total_squares + jnp.sum(grad_gains * grad_gains)
    norm = jnp.sqrt(total_squares)
    factor = CLIP_AT / jnp.maximum(norm, CLIP_AT)
    groups_all = [
        (w_pixel, moment_pixel, second_pixel, grad_pixel),
        (w_res, moment_res, second_res, grad_res),
        (w_scale, moment_scale, second_scale, grad_scale),
        (w_latent, moment_latent, second_latent, grad_latent),
    ]
    outputs = [jnp.stack([smooth_sum, total_valid, commit_sum]), norm.reshape(1)]
    for weight, moment, second, grad in groups_all:
        grad = jnp.swapaxes(grad * factor, 1, 2)
        weight_new, moment_new, second_new = adam_step(weight, moment, second, grad, WEIGHT_RATE)
        outputs += [weight_new, moment_new, second_new, weight_new.astype(BF16)]
    outputs += list(adam_step(norm_gains, moment_gains, second_gains, grad_gains * factor, GAIN_RATE))
    outputs += [counts_new, sums_new, book_new, book_new.astype(BF16)]
    return tuple(outputs)


def solution(mesh):
    outer, inner = mesh.shape["dp"], mesh.shape["fsdp"]
    fine = Mesh(mesh.devices.reshape(outer // 2, 2, inner), BOTH)
    placed = (
        P(BOTH, None),
        P(BOTH, None),
        P(BOTH),
        P(None, BOTH),
        P(None, "fsdp", COLS),
        P(None, "fsdp", COLS),
        P(None, "fsdp", COLS),
        P(None, "fsdp", COLS),
        P(),
        P(None, "fsdp", COLS),
        P(None, "fsdp", COLS),
        P(None, "fsdp", COLS),
        P(None, "fsdp", COLS),
        P(),
        P(None, "fsdp", COLS),
        P(None, "fsdp", COLS),
        P(None, "fsdp", COLS),
        P(None, "fsdp", COLS),
        P(),
        P(BOTH),
        P(BOTH, None),
    )
    return jax.shard_map(
        on_device,
        mesh=fine,
        in_specs=placed,
        out_specs=(
            P(),
            P(),
            P(None, "fsdp", COLS),
            P(None, "fsdp", COLS),
            P(None, "fsdp", COLS),
            P(None, "fsdp", COLS),
            P(None, "fsdp", COLS),
            P(None, "fsdp", COLS),
            P(None, "fsdp", COLS),
            P(None, "fsdp", COLS),
            P(None, "fsdp", COLS),
            P(None, "fsdp", COLS),
            P(None, "fsdp", COLS),
            P(None, "fsdp", COLS),
            P(None, "fsdp", COLS),
            P(None, "fsdp", COLS),
            P(None, "fsdp", COLS),
            P(None, "fsdp", COLS),
            P(),
            P(),
            P(),
            P(BOTH),
            P(BOTH, None),
            P(BOTH, None),
            P(BOTH, None),
        ),
        check_vma=False,
    )
```
